32 devices in a mesh: group: 4 (over y, x), member: 8 (over z, core).
Axes of the slice: x: 2, y: 2, z: 4, core: 2. Of those that a mesh axis runs over, the one named last changes fastest.
Arguments:
- features: bfloat16 [131072, 128], P(('group', 'member')), may hold values from -6 to 6
- history: bfloat16 [131072, 128], P(('group', 'member')), may hold values from -6 to 6
- tiles: bfloat16 [16384, 128, 128], P(('group', 'member'))
- tile_src: int32 [1024, 16], P(('group', 'member')), may hold values from 0 to 47
- degree: int32 [131072], P(('group', 'member')), may hold values from 8 to 128
- boundary_rows: int32 [32, 256], P(('group', 'member')), may hold values from 0 to 4095
- picks: int32 [256, 1], P(('group', 'member')), may hold values from 0 to 1
- stale_rows: int32 [128, 256], P(('group', 'member')), may hold values from 0 to 4095
- w_self: bfloat16 [128, 128], replicated, may hold values from -0.5 to 0.5
- w_neigh: bfloat16 [128, 128], replicated, may hold values from -0.5 to 0.5
- cotangent: bfloat16 [131072, 128], P(('group', 'member')), may hold values from -6 to 6
Outputs:
- layer_out: bfloat16 [131072, 128], P(('group', 'member'))
- grad_features: bfloat16 [131072, 128], P(('group', 'member'))
- grad_self: float32 [128, 128], replicated
- grad_neigh: float32 [128, 128], replicated
The draws below stay inside these ranges and needn't reach their ends.
Inputs may be any that keep to these rules, and one draw needn't show every extreme that they name: `boundary_rows`: local row indices of the sending device. `stale_rows`: local row indices of the sending device, one list for each destination group. `tile_src`: indices into the device's source blocks: own blocks, then taken boundary blocks member by member, then historical blocks group by group. `degree`: a normalizer given with the graph, not derived from the tiles.
All inputs are finite; a program needn't handle non-finite values.
Results may differ from the reference program's by a relative error of at most 0.0051.
Values may be sent and summed in bfloat16 or wider, within the bound.
A program may use at most 192 MiB of HBM per device.

```python
import jax
import jax.numpy as jnp
from jax import lax

WIDTH = 128
OUT_WIDTH = 128
TILE = 128
BLOCKS_DEV = 32
TILES_ROW = 16
PICKED = 1
BOUNDARY = 2
STALE = 2
NODES_DEV = 4096
NODES = 131072
BLOCKS = 1024
SOURCES = 48
N_GROUP = 4
N_MEMBER = 8
DEVICES = 32


def draw_tiles(key, part):
    first, second = jax.random.split(jax.random.fold_in(key, 17))
    shape = (BLOCKS * TILES_ROW, TILE, TILE)
    density = 0.0625
    values = jax.random.uniform(second, shape, jnp.float32, 0.5, 1.5)
    keep = jax.random.uniform(first, shape, jnp.float32) < density
    return jnp.where(keep, values, 0.0).astype(jnp.bfloat16)


def plant(drawn, rng, low, largest):
    index_at = [jax.random.randint(jax.random.fold_in(rng, axis), (), 0, length) for axis, length in enumerate(drawn.shape)]
    main_axis = drawn.shape.index(max(drawn.shape))
    next_to = index_at[:main_axis] + [(index_at[main_axis] + 1) % drawn.shape[main_axis]] + index_at[main_axis + 1:]
    return drawn.at[tuple(index_at)].set(low).at[tuple(next_to)].set(largest)


def block_scale(stream_key, dims, shards, low, top_value):
    gain, own = 1.0, jax.random.fold_in(stream_key, 6)
    for position, shards_of in shards:
        heights = jnp.exp(jax.random.uniform(jax.random.fold_in(own, position), (shards_of,), jnp.float32, low / len(shards), top_value / len(shards)))
        gain = gain * jnp.repeat(heights, dims[position] // shards_of).reshape([-1 if axis == position else 1 for axis in range(len(dims))])
    return gain


def noise(rng, dims, width, most, cuts=(), kind=jnp.bfloat16):
    values = jax.random.normal(rng, dims, jnp.float32) * width
    if len(cuts) > 0:
        values = block_scale(rng, dims, cuts, -0.22, 0.18) * values
    return jnp.clip(values, min=-most, max=most).astype(kind)


def setup_inputs(seed: int = 0) -> dict:
    splits = jax.random.split(jax.random.key(seed), 12)
    features = noise(splits[0], (NODES, WIDTH), 1.0, 6.0, ((0, 32),))
    history = noise(splits[1], (NODES, WIDTH), 1.0, 6.0, ((0, 32),))
    tiles = draw_tiles(jax.random.fold_in(splits[11], 71), 0)
    tile_src = plant(jax.random.randint(splits[3], (BLOCKS, TILES_ROW), 0, SOURCES), jax.random.fold_in(splits[3], 1), 0, SOURCES - 1).astype(jnp.int32)
    degree = plant(jax.random.randint(splits[4], (NODES,), 8, 129), jax.random.fold_in(splits[4], 1), 8, 128).astype(jnp.int32)
    boundary_rows = plant(jax.random.randint(splits[5], (DEVICES, BOUNDARY * TILE), 0, NODES_DEV), jax.random.fold_in(splits[5], 1), 0, NODES_DEV - 1).astype(jnp.int32)
    picks = plant(jax.random.randint(splits[6], (DEVICES * N_MEMBER, PICKED), 0, BOUNDARY), jax.random.fold_in(splits[6], 1), 0, BOUNDARY - 1).astype(jnp.int32)
    stale_rows = plant(jax.random.randint(splits[7], (DEVICES * N_GROUP, STALE * TILE), 0, NODES_DEV), jax.random.fold_in(splits[7], 1), 0, NODES_DEV - 1).astype(jnp.int32)
    w_self = noise(splits[8], (WIDTH, OUT_WIDTH), WIDTH ** -0.5, 0.5)
    w_neigh = noise(splits[9], (WIDTH, OUT_WIDTH), WIDTH ** -0.5, 0.5)
    cotangent = noise(splits[10], (NODES, OUT_WIDTH), 1.0, 6.0, ((0, 32),))
    return dict(features=features, history=history, tiles=tiles, tile_src=tile_src, degree=degree, boundary_rows=boundary_rows, picks=picks, stale_rows=stale_rows, w_self=w_self, w_neigh=w_neigh, cotangent=cotangent)


def reference(features, history, tiles, tile_src, degree, boundary_rows, picks, stale_rows, w_self, w_neigh, cotangent):
    groups = N_GROUP
    members = N_MEMBER
    devs = groups * members
    feats = features.reshape(devs, NODES_DEV, WIDTH)
    hists = history.reshape(devs, NODES_DEV, WIDTH)
    brows = boundary_rows.reshape(devs, BOUNDARY * TILE)
    bound = jax.vmap(lambda table, rows: table[rows])(feats, brows).reshape(devs, BOUNDARY, TILE, WIDTH)
    chosen = picks.reshape(devs, members, PICKED)
    group_of = jnp.arange(devs, dtype=jnp.int32) // members
    owner = group_of[:, None] * members + jnp.arange(members, dtype=jnp.int32)[None, :]
    halo = bound[owner[:, :, None], chosen]
    srows = stale_rows.reshape(devs, groups, STALE * TILE)
    sent = jax.vmap(lambda table, rows: table[rows])(hists, srows)
    sent = sent.reshape(groups, members, groups, STALE, TILE, WIDTH)
    stale = sent.transpose(2, 1, 0, 3, 4, 5).reshape(devs, groups * STALE, TILE, WIDTH)
    sources = jnp.concatenate([feats.reshape(devs, BLOCKS_DEV, TILE, WIDTH), halo.reshape(devs, members * PICKED, TILE, WIDTH), stale], axis=1)
    tiled = tiles.reshape(devs, BLOCKS_DEV, TILES_ROW, TILE, TILE)
    src_index = tile_src.reshape(devs, BLOCKS_DEV, TILES_ROW)
    degs = degree.reshape(devs, NODES_DEV, 1).astype(jnp.float32)
    cots = cotangent.reshape(devs, NODES_DEV, OUT_WIDTH)

    def one_device(args):
        srcs, tl, idx, dg, own, cot = args
        picked = srcs[idx]
        summed = jnp.einsum('btij,btjf->bif', tl.astype(jnp.float32), picked.astype(jnp.float32))
        agg = (summed.reshape(NODES_DEV, WIDTH) / dg).astype(jnp.bfloat16)
        pre = jnp.dot(own, w_self, preferred_element_type=jnp.float32) + jnp.dot(agg, w_neigh, preferred_element_type=jnp.float32)
        scale_row = lax.rsqrt(lax.optimization_barrier(jnp.mean(pre * pre, axis=-1, keepdims=True)) + 1e-05)
        out = (pre * scale_row).astype(jnp.bfloat16)
        grad_out = cot.astype(jnp.float32)
        dpre = (scale_row * grad_out - pre * scale_row ** 3 * lax.optimization_barrier(jnp.mean(grad_out * pre, axis=-1, keepdims=True))).astype(jnp.bfloat16)
        part_self = jnp.dot(own.T, dpre, preferred_element_type=jnp.float32)
        part_neigh = jnp.dot(agg.T, dpre, preferred_element_type=jnp.float32)
        dself = jnp.dot(dpre, w_self.T, preferred_element_type=jnp.float32)
        back = (jnp.dot(dpre, w_neigh.T, preferred_element_type=jnp.float32) / dg).astype(jnp.bfloat16)
        back = back.reshape(BLOCKS_DEV, TILE, WIDTH)
        per_tile = jnp.einsum('btij,bif->btjf', tl.astype(jnp.float32), back.astype(jnp.float32))
        src_grad = jnp.zeros((SOURCES, TILE, WIDTH), jnp.float32).at[idx.reshape(-1)].add(per_tile.reshape(-1, TILE, WIDTH))
        return (out, part_self, part_neigh, dself, src_grad[:BLOCKS_DEV + members * PICKED])
    outs, parts_self, parts_neigh, dselfs, src_grads = lax.map(one_device, (sources, tiled, src_index, degs, feats, cots))
    factor = NODES ** (-0.5)
    grad_self = lax.optimization_barrier(jnp.sum(parts_self, axis=0)) * factor
    grad_neigh = lax.optimization_barrier(jnp.sum(parts_neigh, axis=0)) * factor
    local_grad = src_grads[:, :BLOCKS_DEV].reshape(devs, NODES_DEV, WIDTH)
    halo_grad = src_grads[:, BLOCKS_DEV:].reshape(devs, members, PICKED, TILE, WIDTH)
    bound_grad = jnp.zeros((devs, BOUNDARY, TILE, WIDTH), jnp.float32).at[owner[:, :, None], chosen].add(halo_grad)
    row_grad = dselfs + local_grad
    row_grad = jax.vmap(lambda grads, rows, extra: grads.at[rows].add(extra.reshape(-1, WIDTH)))(row_grad, brows, bound_grad)
    layer_out = outs.reshape(NODES, OUT_WIDTH)
    grad_features = row_grad.reshape(NODES, WIDTH).astype(jnp.bfloat16)
    return (layer_out, grad_features, grad_self, grad_neigh)
```

```python
import functools
import math

import jax
import jax.numpy as jnp
from jax import lax
from jax.experimental import pallas as pl
from jax.experimental.pallas import tpu as pltpu
from jax.sharding import PartitionSpec as P

QUAD = 4
STEP = 8
F32 = jnp.float32
BF16 = jnp.bfloat16
MESH = pl.DeviceIdType.MESH


def up(value, unit):
    return -(-value // unit) * unit


def iota(shape, axis):
    return lax.broadcasted_iota(jnp.int32, shape, axis).astype(F32)


def column(value):
    return jnp.broadcast_to(value, (8, value.shape[1])).T[:, :1]


def arrange(key, valid, value, keys, least, slots, quads, pad):
    total = key.shape[1]
    wide = up(keys + 1, 128)
    square = (total, total)
    same = (column(key) == key) & (column(valid) > 0.0) & (iota(square, 0) < iota(square, 1))
    within = jnp.sum(jnp.where(same, 1.0, 0.0), axis=0, keepdims=True)
    ids = iota((wide, total), 0)
    hit = (ids == key) & (valid > 0.0)
    count = jnp.sum(jnp.where(hit, 1.0, 0.0), axis=1, keepdims=True)
    need = jnp.floor((count + (QUAD - 1)) / QUAD)
    need = jnp.where(iota((wide, 1), 0) < keys, jnp.maximum(need, least), 0.0)
    spread = jnp.broadcast_to(need, (wide, wide)).T
    before = iota((wide, wide), 1) < iota((wide, wide), 0)
    offset = jnp.sum(jnp.where(before, spread, 0.0), axis=1, keepdims=True)
    end = jnp.sum(spread[:1, :], axis=1, keepdims=True)
    base = jnp.sum(jnp.where(hit, QUAD * offset, 0.0), axis=0, keepdims=True)
    pos = jnp.where(valid > 0.0, base + within, -1.0)
    here = column(pos) == iota((total, slots), 1)
    code = jnp.sum(jnp.where(here, column(value) + 1.0, 0.0), axis=0, keepdims=True)
    code = jnp.where(code > 0.0, code - 1.0, pad)
    q = iota((wide, quads), 1)
    inside = (offset <= q) & (q < offset + need)
    info = 2.0 * iota((wide, quads), 0) + jnp.where(offset == q, 1.0, 0.0)
    quad = jnp.sum(jnp.where(inside, info, 0.0), axis=0, keepdims=True)
    quad = jnp.where(q[:1, :] < end, quad, 2.0 * keys + 1.0)
    return code.astype(jnp.int32), quad.astype(jnp.int32), offset, need, end


def back_sizes(total, wanted):
    slots = up(total + wanted * (QUAD - 1), 128)
    return slots, up(slots // QUAD, 128)


def rest_sizes(blocks, per):
    quads = up(blocks * (-(-per // QUAD)), 128)
    return quads * QUAD, quads


def own_quads(total, blocks):
    return up((total + blocks * (QUAD - 1)) // QUAD, STEP)


def code_base(total):
    return 1 << (total - 1).bit_length()


def split(value, base):
    return lax.shift_right_logical(value, base.bit_length() - 1), value & (base - 1)


def greet(me_g, me_m, groups, members):
    barrier = pltpu.get_barrier_semaphore()
    for o in range(1, members):
        pl.semaphore_signal(
            barrier, inc=1, device_id=(me_g, lax.rem(me_m + o, members)), device_id_type=MESH
        )
    for o in range(1, groups):
        pl.semaphore_signal(
            barrier, inc=1, device_id=(lax.rem(me_g + o, groups), me_m), device_id_type=MESH
        )
    return lambda: pl.semaphore_wait(barrier, members + groups - 2)


def push(src, dst, send, recv, o, device):
    copy = pltpu.make_async_remote_copy(
        src_ref=src,
        dst_ref=dst,
        send_sem=send.at[o],
        recv_sem=recv.at[o],
        device_id=device,
        device_id_type=MESH,
    )
    copy.start()
    return copy


def pick_rows(row, table, chunk):
    count = row.shape[1]
    blocks, tile, width = table.shape
    ids_column = jnp.broadcast_to(row, (8, count)).T[:, :1]
    total = jnp.zeros((count, width), F32)
    depth = chunk * tile
    for c in range(0, blocks, chunk):
        ids = lax.broadcasted_iota(jnp.int32, (count, depth), 1) + c * tile
        hot = jnp.where(ids == ids_column, 1.0, 0.0).astype(BF16)
        total = total + jnp.dot(
            hot, table[c : c + chunk].reshape(depth, width), preferred_element_type=F32
        )
    return total


def gather_kernel(
    groups,
    members,
    blocks,
    feats_in,
    hist_in,
    tiles_in,
    cot_in,
    rows,
    picks,
    stale_rows,
    src,
    src_vec,
    tiles,
    srcs,
    cot,
    ext,
    part,
    wanted,
    code,
    quad,
    rest_code,
    rest_quad,
    marks,
    asked,
    hist,
    leaving,
    l_sems,
    t_sems,
    p_send,
    p_recv,
    d_send,
    d_recv,
    r_send,
    r_recv,
    s_send,
    s_recv,
):
    me_g, me_m = lax.axis_index("group"), lax.axis_index("member")
    taken = picks.shape[0]
    tile, width = srcs.shape[1], srcs.shape[2]
    offered = rows.shape[1] // tile
    each = stale_rows.shape[1] // tile
    per = src.shape[0]
    total = blocks * per
    pair = 2 if members % 2 == 0 else 1

    load_feats = pltpu.make_async_copy(feats_in, srcs.at[pl.ds(0, blocks)], l_sems.at[0])
    load_hist = pltpu.make_async_copy(hist_in, hist, l_sems.at[1])
    load_cot = pltpu.make_async_copy(cot_in, cot, l_sems.at[2])

    def chunk(b):
        at = pl.ds(b * per, per)
        return pltpu.make_async_copy(tiles_in.at[at], tiles.at[at], t_sems.at[b])

    load_feats.start()
    load_hist.start()
    entered = greet(me_g, me_m, groups, members)
    for p in range(members):
        for k in range(taken):
            asked[p, k] = jnp.broadcast_to(picks[k : k + 1, p : p + 1], asked.shape[2:])
    wanted[me_m] = asked[me_m]
    srcs[blocks] = jnp.zeros((tile, width), BF16)
    ext[ext.shape[0] - 1] = jnp.zeros((tile, width), BF16)
    load_feats.wait()

    @pl.loop(0, blocks)
    def _(b):
        chunk(b).start()

    load_cot.start()
    mine = pl.ds(me_m * offered, offered)
    ext[mine] = pick_rows(rows[...], srcs.at[pl.ds(0, blocks)], 4).astype(BF16).reshape(
        offered, tile, width
    )
    entered()
    direct, copies = [], []
    for o in range(pair, members, pair):
        peer = lax.rem(me_m + o, members)
        direct.append((o, push(ext.at[mine], ext.at[mine], d_send, d_recv, o, (me_g, peer))))
    if pair == 2:
        mate = me_m + 1 - 2 * lax.rem(me_m, 2)
        copies.append(push(ext.at[mine], ext.at[mine], d_send, d_recv, 1, (me_g, mate)))
    load_hist.wait()
    for o in range(groups - 1, -1, -1):
        to = lax.rem(me_g + o, groups)
        found = pick_rows(stale_rows[pl.ds(to, 1), :], hist, 4)
        found = found.astype(BF16).reshape(each, tile, width)
        at = pl.ds(members * offered + me_g * each, each)
        if o == 0:
            ext[at] = found
        else:
            leaving[o] = found
            copies.append(push(leaving.at[o], ext.at[at], s_send, s_recv, o, (to, me_m)))
    for o in range(1, members):
        peer = lax.rem(me_m + o, members)
        copies.append(push(asked.at[peer], wanted.at[me_m], p_send, p_recv, o, (me_g, peer)))

    def forward(b):
        chunk(b).wait()
        lhs = jnp.concatenate([tiles[b * per + t] for t in range(per)], axis=1)
        rhs = jnp.concatenate([srcs[jnp.minimum(src[t, b], blocks)] for t in range(per)], axis=0)
        part[b] = jnp.dot(lhs, rhs, preferred_element_type=F32)

    early = blocks * 3 // 4
    pl.loop(0, early, unroll=4)(forward)
    for o, copy in direct:
        copy.wait_recv()
        if pair == 2:
            at = pl.ds(lax.rem(me_m + members - o, members) * offered, offered)
            copies.append(push(ext.at[at], ext.at[at], r_send, r_recv, o, (me_g, mate)))
    pl.loop(early, blocks, unroll=4)(forward)

    one = (per, total)
    owner = jnp.floor((iota(one, 1) + 0.5) / per)
    rank = iota(one, 1) - per * owner
    place = jnp.where(iota((blocks, total), 0) == owner[:1, :], 1.0, 0.0).astype(BF16)
    spread = jnp.dot(src_vec[...].astype(F32).astype(BF16), place, preferred_element_type=F32)
    row = jnp.sum(jnp.where(iota(one, 0) == rank, spread, 0.0), axis=0, keepdims=True)
    owner = owner[:1, :]
    base = code_base(total)
    count = iota((1, total), 1)
    inner = blocks + members * taken
    code[...], quad[...], offset, need, end = arrange(
        row,
        jnp.where(row < inner, 1.0, 0.0),
        base * owner + count,
        inner,
        0.0,
        code.shape[1],
        quad.shape[1],
        float(base * blocks),
    )
    where = row - blocks
    spot = where - members * taken + members * offered
    for p in range(members):
        for k in range(taken):
            pick = picks[k : k + 1, p : p + 1].astype(F32)
            spot = jnp.where(where == p * taken + k, p * offered + pick, spot)
    rest_code[...], rest_quad[...], _, _, rest_end = arrange(
        owner,
        jnp.where(row < blocks, 0.0, 1.0),
        base * spot + count,
        blocks,
        1.0,
        rest_code.shape[1],
        rest_quad.shape[1],
        float(base * (ext.shape[0] - 1)),
    )
    wide = need.shape[0]
    last = jnp.where(need > 0.0, offset + need - 1.0, float(own_quads(total, blocks)))
    last = jnp.broadcast_to(last, (wide, wide)).T[:8, :]
    first = jnp.sum(jnp.where(iota((wide, 1), 0) == blocks, offset, 0.0), axis=0, keepdims=True)
    which = iota((8, wide), 0)
    found = jnp.where(which == 1, jnp.floor(first / STEP), last)
    found = jnp.where(which == 2, jnp.floor((end + (STEP - 1)) / STEP), found)
    found = jnp.where(which == 3, jnp.floor((rest_end + (STEP - 1)) / STEP), found)
    marks[...] = found.astype(jnp.int32)

    load_cot.wait()
    for _, copy in direct:
        copy.wait_send()
    for copy in copies:
        copy.wait()


def vmem_out(shape, dtype):
    return pltpu.VMEM(shape, dtype)


def hold(*arrays):
    return [pltpu.with_memory_space_constraint(a, pltpu.VMEM) for a in arrays]


def gather(features, history, tiles, cotangent, boundary_rows, picks, stale_rows, src, sizes):
    groups, members = sizes
    per, blocks = src.shape
    taken = picks.shape[0]
    tile, width = tiles.shape[1], features.shape[1]
    offered = boundary_rows.shape[1] // tile
    each = stale_rows.shape[1] // tile
    total = blocks * per
    inner = blocks + members * taken
    slots, quads = back_sizes(total, inner)
    rest_slots, rest_quads = rest_sizes(blocks, per)
    held = members * offered + groups * each + 1
    vmem = pl.BlockSpec(memory_space=pltpu.VMEM)
    anywhere = pl.BlockSpec(memory_space=pl.ANY)
    dma = pltpu.SemaphoreType.DMA
    return pl.pallas_call(
        functools.partial(gather_kernel, groups, members, blocks),
        out_shape=(
            vmem_out(tiles.shape, BF16),
            vmem_out((blocks + 1, tile, width), BF16),
            vmem_out((blocks * tile, width), BF16),
            vmem_out((held, tile, width), BF16),
            vmem_out((blocks, tile, width), F32),
            vmem_out((members, taken, 8, 128), jnp.int32),
            jax.ShapeDtypeStruct((1, slots), jnp.int32),
            jax.ShapeDtypeStruct((1, quads), jnp.int32),
            jax.ShapeDtypeStruct((1, rest_slots), jnp.int32),
            jax.ShapeDtypeStruct((1, rest_quads), jnp.int32),
            jax.ShapeDtypeStruct((8, up(inner + 1, 128)), jnp.int32),
        ),
        in_specs=[anywhere] * 4
        + [vmem] * 3
        + [pl.BlockSpec(memory_space=pltpu.SMEM), vmem],
        out_specs=[vmem] * 11,
        scratch_shapes=[
            pltpu.VMEM((members, taken, 8, 128), jnp.int32),
            pltpu.VMEM((blocks, tile, width), BF16),
            pltpu.VMEM((groups, each, tile, width), BF16),
            dma((3,)),
            dma((blocks,)),
            dma((members,)),
            dma((members,)),
            dma((members,)),
            dma((members,)),
            dma((members,)),
            dma((members,)),
            dma((groups,)),
            dma((groups,)),
        ],
        compiler_params=pltpu.CompilerParams(
            collective_id=0, has_side_effects=True, vmem_limit_bytes=16 << 20
        ),
    )(
        features.reshape(blocks, tile, width),
        history.reshape(blocks, tile, width),
        tiles,
        cotangent,
        boundary_rows,
        picks,
        stale_rows,
        src,
        src,
    )


def middle_kernel(
    code,
    quad,
    rest_code,
    rest_quad,
    marks,
    tiles,
    srcs,
    cot,
    ext,
    part,
    deg,
    w_self,
    w_neigh,
    out,
    back,
    dpre_out,
    halo_grad,
    weights,
    total,
    out_buf,
    grad,
    gt,
    inverse,
    sems,
):
    blocks, tile, width = part.shape
    base = code_base(tiles.shape[0])
    n_halo = halo_grad.shape[0]

    back[blocks] = jnp.zeros((width, tile), BF16)
    grad[blocks : blocks + n_halo] = jnp.zeros((n_halo, width, tile), F32)
    gt[...] = jnp.zeros_like(gt)
    inverse[...] = 1.0 / deg[...].astype(F32)

    def rest(step, acc):
        terms = []
        for u in range(STEP):
            lhs, rhs = [], []
            for i in range(QUAD):
                e, t = split(rest_code[0, (step * STEP + u) * QUAD + i], base)
                lhs.append(tiles[t])
                rhs.append(ext[e])
            terms.append(
                jnp.dot(
                    jnp.concatenate(lhs, axis=1),
                    jnp.concatenate(rhs, axis=0),
                    preferred_element_type=F32,
                )
            )
        for u in range(STEP):
            info = rest_quad[0, step * STEP + u]
            b = info // 2
            start = part[jnp.minimum(b, blocks - 1)]
            acc = terms[u] + jnp.where(info % 2 == 1, start, acc)
            total[b] = acc
        return acc

    lax.fori_loop(0, marks[3, 0], rest, jnp.zeros((tile, width), F32))

    group = 8
    rows = group * tile
    w_cat = jnp.concatenate([w_self[...], w_neigh[...]], axis=0)

    def store(c):
        at = pl.ds(pl.multiple_of(c * rows, rows), rows)
        return pltpu.make_async_copy(out_buf.at[at], out.at[at], sems.at[c])

    def middle(c):
        at = pl.ds(pl.multiple_of(c * rows, rows), rows)
        agg = []
        for i in range(group):
            b = c * group + i
            d = jnp.broadcast_to(inverse[pl.ds(b, 1), :], (tile, tile)).T
            agg.append((total[b] * d).astype(BF16))
        own = srcs[pl.ds(c * group, group)].reshape(rows, width)
        fa = jnp.concatenate([own, jnp.concatenate(agg, axis=0)], axis=1)
        pre = jnp.dot(fa, w_cat, preferred_element_type=F32)
        scale = lax.rsqrt(jnp.mean(pre * pre, axis=-1, keepdims=True) + 1e-05)
        out_buf[at, :] = (pre * scale).astype(BF16)
        store(c).start()
        g = cot[at, :].astype(F32)
        m = jnp.mean(g * pre, axis=-1, keepdims=True)
        dpre = (scale * g - pre * (scale**3 * m)).astype(BF16)
        dpre_out[at, :] = dpre
        gt[...] += lax.dot_general(dpre, fa, (((0,), (0,)), ((), ())), preferred_element_type=F32)
        bt = lax.dot_general(
            w_neigh[...], dpre, (((1,), (1,)), ((), ())), preferred_element_type=F32
        )
        for i in range(group):
            d = inverse[pl.ds(c * group + i, 1), :]
            back[c * group + i] = (bt[:, i * tile : (i + 1) * tile] * d).astype(BF16)

    pl.loop(0, blocks // group)(middle)

    weights[:width, :] = gt[:, :width].T
    weights[width:, :] = gt[:, width:].T

    def backward(step, acc):
        terms = quad_terms(step, code, back, tiles, base)
        for u in range(STEP):
            info = quad[0, step * STEP + u]
            acc = terms[u] + jnp.where(info % 2 == 1, 0.0, acc)
            grad[info // 2] = acc
        return acc

    lax.fori_loop(marks[1, 0], marks[2, 0], backward, jnp.zeros((width, tile), F32))
    for h in range(n_halo):
        halo_grad[h] = grad[blocks + h].T.astype(BF16)

    @pl.loop(0, blocks // group)
    def _(c):
        store(c).wait()


def quad_terms(step, code, back, tiles, base):
    terms = []
    for u in range(STEP):
        lhs, rhs = [], []
        for i in range(QUAD):
            b, t = split(code[0, (step * STEP + u) * QUAD + i], base)
            lhs.append(back[b])
            rhs.append(tiles[t])
        terms.append(
            jnp.dot(
                jnp.concatenate(lhs, axis=1),
                jnp.concatenate(rhs, axis=0),
                preferred_element_type=F32,
            )
        )
    return terms


def middle(plans, tiles, srcs, cot, ext, part, degree, w_self, w_neigh, n_halo):
    blocks, tile, width = part.shape
    nodes = blocks * tile
    smem = pl.BlockSpec(memory_space=pltpu.SMEM)
    vmem = pl.BlockSpec(memory_space=pltpu.VMEM)
    return pl.pallas_call(
        middle_kernel,
        out_shape=(
            jax.ShapeDtypeStruct((nodes, width), BF16),
            vmem_out((blocks + 1, width, tile), BF16),
            vmem_out((nodes, width), BF16),
            vmem_out((n_halo, tile, width), BF16),
            vmem_out((2 * width, width), F32),
        ),
        in_specs=[smem] * 5 + [vmem] * 8,
        out_specs=[pl.BlockSpec(memory_space=pl.ANY)] + [vmem] * 4,
        scratch_shapes=[
            pltpu.VMEM((blocks + 1, tile, width), F32),
            pltpu.VMEM((nodes, width), BF16),
            pltpu.VMEM((blocks + n_halo + 1, width, tile), F32),
            pltpu.VMEM((width, 2 * width), F32),
            pltpu.VMEM((blocks, tile), F32),
            pltpu.SemaphoreType.DMA((blocks,)),
        ],
        compiler_params=pltpu.CompilerParams(vmem_limit_bytes=20 << 20),
    )(
        *plans,
        *hold(tiles, srcs, cot, ext, part),
        degree.reshape(blocks, tile),
        w_self,
        w_neigh,
    )


def combine_kernel(
    groups,
    members,
    factor,
    code,
    quad,
    marks,
    tiles,
    back,
    dpre,
    halo_grad,
    weights,
    wanted,
    rows,
    w_self,
    grad_features,
    grad_self,
    grad_neigh,
    accs,
    returned,
    landed,
    partial,
    across,
    share,
    whole,
    h_send,
    h_recv,
    a_send,
    a_recv,
    b_send,
    b_recv,
    c_send,
    c_recv,
):
    me_g, me_m = lax.axis_index("group"), lax.axis_index("member")
    taken = wanted.shape[1]
    blocks, (width, tile) = back.shape[0] - 1, back.shape[1:]
    offered = rows.shape[1] // tile
    piece = weights.shape[0] // members
    base = code_base(tiles.shape[0])
    steps = (accs.shape[0] - 1) // STEP

    def backward(step, acc):
        terms = quad_terms(step, code, back, tiles, base)
        for u in range(STEP):
            q = step * STEP + u
            acc = terms[u] + jnp.where(quad[0, q] % 2 == 1, 0.0, acc)
            accs[q] = acc
        return acc

    entered = greet(me_g, me_m, groups, members)
    accs[accs.shape[0] - 1] = jnp.zeros((width, tile), F32)
    cuts = [0, 3 * steps // 19, 11 * steps // 19, 17 * steps // 19, steps]
    acc = lax.fori_loop(cuts[0], cuts[1], backward, jnp.zeros((width, tile), F32))
    entered()
    copies, first, second, third = [], [], [], []
    for o in range(1, members):
        peer = lax.rem(me_m + o, members)
        at = pl.ds(pl.multiple_of(peer * piece, piece), piece)
        first.append(push(weights.at[at], landed.at[me_m], a_send, a_recv, o, (me_g, peer)))
    for o in range(1, members):
        peer = lax.rem(me_m + o, members)
        copies.append(
            push(
                halo_grad.at[pl.ds(peer * taken, taken)],
                returned.at[me_m],
                h_send,
                h_recv,
                o,
                (me_g, peer),
            )
        )
    landed[me_m] = weights[pl.ds(pl.multiple_of(me_m * piece, piece), piece), :]
    returned[me_m] = halo_grad[pl.ds(me_m * taken, taken)]
    acc = lax.fori_loop(cuts[1], cuts[2], backward, acc)
    for copy in first:
        copy.wait_recv()
    total = landed[0]
    for p in range(1, members):
        total = total + landed[p]
    partial[...] = total
    across[me_g] = total
    for o in range(1, groups):
        to = lax.rem(me_g + o, groups)
        second.append(push(partial, across.at[me_g], b_send, b_recv, o, (to, me_m)))
    acc = lax.fori_loop(cuts[2], cuts[3], backward, acc)
    for copy in second:
        copy.wait_recv()
    total = across[0]
    for g in range(1, groups):
        total = total + across[g]
    mine = pl.ds(pl.multiple_of(me_m * piece, piece), piece)
    share[...] = total
    whole[mine, :] = total
    for o in range(1, members):
        peer = lax.rem(me_m + o, members)
        third.append(push(share, whole.at[mine], c_send, c_recv, o, (me_g, peer)))
    acc = lax.fori_loop(cuts[3], cuts[4], backward, acc)

    for copy in copies:
        copy.wait_recv()
    halves = []
    for j in range(offered):
        total = jnp.zeros((tile, width), F32)
        for p in range(members):
            for k in range(taken):
                w = jnp.broadcast_to(wanted[p, k][:1, :], (tile, width))
                total = total + jnp.where(w == j, returned[p, k].astype(F32), 0.0)
        high = total.astype(BF16)
        low = (total - high.astype(F32)).astype(BF16)
        halves.append(jnp.concatenate([high, low], axis=1))
    extra = jnp.concatenate(halves, axis=0)
    group = 4
    depth = group * tile

    def add(c):
        at = pl.ds(pl.multiple_of(c * depth, depth), depth)
        ids = lax.broadcasted_iota(jnp.int32, (depth, rows.shape[1]), 0) + c * depth
        hot = jnp.where(ids == rows[...], 1.0, 0.0).astype(BF16)
        more = jnp.dot(hot, extra, preferred_element_type=F32)
        own = lax.dot_general(
            dpre[at, :], w_self[...], (((1,), (1,)), ((), ())), preferred_element_type=F32
        )
        near = [accs[marks[0, c * group + i]].T for i in range(group)]
        own = own + jnp.concatenate(near, axis=0)
        grad_features[at, :] = (own + (more[:, :width] + more[:, width:])).astype(BF16)

    pl.loop(0, blocks // group)(add)
    for copy in third:
        copy.wait_recv()
    grad_self[...] = whole[:width, :] * factor
    grad_neigh[...] = whole[width:, :] * factor
    for copy in first + second + third + copies:
        copy.wait_send()


def combine(plans, tiles, back, dpre, halo_grad, weights, wanted, boundary_rows, w_self, sizes):
    groups, members = sizes
    nodes, width = dpre.shape
    tile = halo_grad.shape[1]
    blocks = nodes // tile
    taken = wanted.shape[1]
    piece = weights.shape[0] // members
    factor = 1.0 / math.sqrt(nodes * members * groups)
    smem = pl.BlockSpec(memory_space=pltpu.SMEM)
    vmem = pl.BlockSpec(memory_space=pltpu.VMEM)
    dma = pltpu.SemaphoreType.DMA
    return pl.pallas_call(
        functools.partial(combine_kernel, groups, members, factor),
        out_shape=(
            vmem_out((nodes, width), BF16),
            vmem_out((width, width), F32),
            vmem_out((width, width), F32),
        ),
        in_specs=[smem] * 3 + [vmem] * 8,
        out_specs=[vmem] * 3,
        scratch_shapes=[
            pltpu.VMEM((own_quads(tiles.shape[0], blocks) + 1, width, tile), F32),
            pltpu.VMEM((members, taken, tile, width), BF16),
            pltpu.VMEM((members, piece, width), F32),
            pltpu.VMEM((piece, width), F32),
            pltpu.VMEM((groups, piece, width), F32),
            pltpu.VMEM((piece, width), F32),
            pltpu.VMEM(weights.shape, F32),
            dma((members,)),
            dma((members,)),
            dma((members,)),
            dma((members,)),
            dma((groups,)),
            dma((groups,)),
            dma((members,)),
            dma((members,)),
        ],
        compiler_params=pltpu.CompilerParams(
            collective_id=1, has_side_effects=True, vmem_limit_bytes=24 << 20
        ),
    )(
        *plans,
        *hold(tiles, back, dpre, halo_grad, weights, wanted),
        boundary_rows,
        w_self,
    )


def on_device(
    features,
    history,
    tiles,
    tile_src,
    degree,
    boundary_rows,
    picks,
    stale_rows,
    w_self,
    w_neigh,
    cotangent,
):
    sizes = lax.axis_size("group"), lax.axis_size("member")
    tiles, srcs, cot, ext, part, wanted, code, quad, rest_code, rest_quad, marks = gather(
        features,
        history,
        tiles,
        cotangent,
        boundary_rows,
        picks.T,
        stale_rows,
        tile_src.T,
        sizes,
    )
    n_halo = sizes[1] * picks.shape[1]
    layer_out, back, dpre, halo_grad, weights = middle(
        (code, quad, rest_code, rest_quad, marks),
        tiles,
        srcs,
        cot,
        ext,
        part,
        degree,
        w_self,
        w_neigh,
        n_halo,
    )
    grad_features, grad_self, grad_neigh = combine(
        (code, quad, marks),
        tiles,
        back,
        dpre,
        halo_grad,
        weights,
        wanted,
        boundary_rows,
        w_self,
        sizes,
    )
    return layer_out, grad_features, grad_self, grad_neigh


def solution(mesh):
    nodes = P(("group", "member"), None)
    placed = (
        nodes,
        nodes,
        P(("group", "member"), None, None),
        nodes,
        P(("group", "member")),
        nodes,
        nodes,
        nodes,
        P(),
        P(),
        nodes,
    )
    return jax.shard_map(
        on_device,
        mesh=mesh,
        in_specs=placed,
        out_specs=(nodes, nodes, P(), P()),
        check_vma=False,
    )
```

```python
import functools
import math

import jax
import jax.numpy as jnp
from jax import lax
from jax.experimental import pallas as pl
from jax.experimental.pallas import tpu as pltpu
from jax.sharding import PartitionSpec as P

QUAD = 4
STEP = 8
EARLY = 12
F32 = jnp.float32
BF16 = jnp.bfloat16
MESH = pl.DeviceIdType.MESH


def up(value, unit):
    return -(-value // unit) * unit


def iota(shape, axis):
    return lax.broadcasted_iota(jnp.int32, shape, axis).astype(F32)


def column(value):
    return jnp.broadcast_to(value, (8, value.shape[1])).T[:, :1]


def arrange(hit, values, keys, least, quads, pad):
    wide, total = hit.shape
    low = hit.astype(BF16)
    earlier = jnp.where(iota((128, 128), 0) < iota((128, 128), 1), 1.0, 0.0).astype(BF16)
    count = jnp.zeros((wide, 1), F32)
    within = []
    for c in range(0, total, 128):
        part = low[:, c : c + 128]
        within.append(jnp.dot(part, earlier, preferred_element_type=F32) + count)
        count = count + jnp.sum(hit[:, c : c + 128], axis=1, keepdims=True)
    within = jnp.concatenate(within, axis=1)
    need = jnp.floor((count + (QUAD - 1)) / QUAD)
    need = jnp.where(iota((wide, 1), 0) < keys, jnp.maximum(need, least), 0.0)
    spread = jnp.broadcast_to(need, (wide, wide)).T
    before = iota((wide, wide), 1) < iota((wide, wide), 0)
    offset = jnp.sum(jnp.where(before, spread, 0.0), axis=1, keepdims=True)
    end = jnp.sum(spread[:1, :], axis=1, keepdims=True)
    pos = jnp.sum(hit * (QUAD * offset + within + 1.0), axis=0, keepdims=True) - 1.0
    high = jnp.floor(pos / 128.0)
    place = jnp.where(column(pos - 128.0 * high) == iota((total, 128), 1), 1.0, 0.0).astype(BF16)
    line = jnp.where(iota((8, total), 0) == high, 1.0, 0.0)
    terms = [line] + [line * row for row, _ in values]
    found = jnp.dot(
        jnp.concatenate(terms, axis=0).astype(BF16), place, preferred_element_type=F32
    )
    code = jnp.zeros((8, 128), F32)
    for i, (_, scale) in enumerate(values):
        code = code + scale * found[8 * (i + 1) : 8 * (i + 2), :]
    code = jnp.where(found[:8, :] > 0.0, code, pad)
    q = iota((wide, quads), 1)
    inside = (offset <= q) & (q < offset + need)
    info = 2.0 * iota((wide, quads), 0) + jnp.where(offset == q, 1.0, 0.0)
    quad = jnp.sum(jnp.where(inside, info, 0.0), axis=0, keepdims=True)
    quad = jnp.where(q[:1, :] < end, quad, 2.0 * keys + 1.0)
    return code.astype(jnp.int32), quad.astype(jnp.int32), offset, need, end


def back_quads(total, wanted):
    return up((total + wanted * (QUAD - 1)) // QUAD, 128)


def rest_quads_of(blocks, per):
    return up(blocks * (-(-per // QUAD)), 128)


def early_blocks(blocks):
    return blocks * EARLY // 32


def own_quads(total, blocks):
    return up((total + blocks * (QUAD - 1)) // QUAD, STEP)


def code_base(total):
    return 1 << (total - 1).bit_length()


def split(value, base):
    return lax.shift_right_logical(value, base.bit_length() - 1), value & (base - 1)


def entry(code, step, i):
    line = 128 // (STEP * QUAD)
    first = lax.shift_right_logical(step, line.bit_length() - 1)
    return code[first, (step & (line - 1)) * (STEP * QUAD) + i]


def greet(groups, members):
    me_g, me_m = lax.axis_index("group"), lax.axis_index("member")
    barrier = pltpu.get_barrier_semaphore()
    peers = [(me_g, lax.rem(me_m + o, members)) for o in range(1, members)]
    peers += [(lax.rem(me_g + o, groups), me_m) for o in range(1, groups)]
    for peer in peers:
        pl.semaphore_signal(barrier, inc=1, device_id=peer, device_id_type=MESH)
    return lambda: pl.semaphore_wait(barrier, len(peers))


def push(src, dst, send, recv, o, device):
    copy = pltpu.make_async_remote_copy(
        src_ref=src,
        dst_ref=dst,
        send_sem=send.at[o],
        recv_sem=recv.at[o],
        device_id=device,
        device_id_type=MESH,
    )
    copy.start()
    return copy


def pick_rows(row, table, chunk):
    count = row.shape[1]
    blocks, tile, width = table.shape
    half = blocks // 2
    ids_column = jnp.broadcast_to(row, (8, count)).T[:, :1]
    second = ids_column >= half * tile
    ids_column = jnp.where(second, ids_column - half * tile, ids_column)
    total = jnp.zeros((count, 2 * width), F32)
    depth = chunk * tile
    for c in range(0, half, chunk):
        ids = lax.broadcasted_iota(jnp.int32, (count, depth), 1) + c * tile
        hot = jnp.where(ids == ids_column, 1.0, 0.0).astype(BF16)
        both = [table[a : a + chunk].reshape(depth, width) for a in (c, half + c)]
        total = total + jnp.dot(
            hot, jnp.concatenate(both, axis=1), preferred_element_type=F32
        )
    return jnp.where(second, total[:, width:], total[:, :width])


def gather_kernel(
    groups,
    members,
    blocks,
    feats_in,
    hist_in,
    tiles_in,
    cot_in,
    rows_in,
    picks_in,
    stale_rows_in,
    src_in,
    tiles,
    srcs,
    cot,
    part,
    wanted,
    code,
    quad,
    rest_code,
    rest_quad,
    marks,
    rows,
    picks,
    stale_rows,
    src,
    src_vec,
    asked,
    own,
    hist,
    leaving,
    l_sems,
    t_sems,
    p_send,
    p_recv,
    d_send,
    d_recv,
    r_send,
    r_recv,
    s_send,
    s_recv,
):
    me_g, me_m = lax.axis_index("group"), lax.axis_index("member")
    taken = picks.shape[0]
    tile, width = srcs.shape[1], srcs.shape[2]
    offered = rows.shape[1] // tile
    each = stale_rows.shape[1] // tile
    per = src.shape[0]
    total = blocks * per
    pair = 2 if members % 2 == 0 else 1

    load_feats = pltpu.make_async_copy(feats_in, own.at[pl.ds(0, blocks)], l_sems.at[0])
    keep_feats = pltpu.make_async_copy(feats_in, srcs.at[pl.ds(0, blocks)], l_sems.at[8])
    load_hist = pltpu.make_async_copy(hist_in, hist, l_sems.at[1])
    load_cot = pltpu.make_async_copy(cot_in, cot, l_sems.at[2])

    def chunk(b):
        at = pl.ds(b * per, per)
        return pltpu.make_async_copy(tiles_in.at[at], tiles.at[at], t_sems.at[b])

    small = [
        pltpu.make_async_copy(a, b, l_sems.at[3 + i])
        for i, (a, b) in enumerate(
            (
                (rows_in, rows),
                (picks_in, picks),
                (stale_rows_in, stale_rows),
                (src_in, src),
                (src_in, src_vec),
            )
        )
    ]
    load_feats.start()
    for copy in small:
        copy.start()
    load_hist.start()
    entered = greet(groups, members)
    for copy in small:
        copy.wait()
    for p in range(members):
        for k in range(taken):
            asked[p, k] = jnp.broadcast_to(picks[k : k + 1, p : p + 1], asked.shape[2:])
    wanted[me_m] = asked[me_m]
    own[blocks] = jnp.zeros((tile, width), BF16)
    srcs[blocks] = jnp.zeros((tile, width), BF16)
    load_feats.wait()

    @pl.loop(0, blocks)
    def _(b):
        chunk(b).start()

    load_cot.start()
    keep_feats.start()
    bounds = blocks + 1
    stales = bounds + members * offered
    mine = pl.ds(bounds + me_m * offered, offered)
    srcs[mine] = pick_rows(rows[...], own.at[pl.ds(0, blocks)], 4).astype(BF16).reshape(
        offered, tile, width
    )
    entered()
    direct, copies = [], []
    for o in range(pair, members, pair):
        peer = lax.rem(me_m + o, members)
        direct.append((o, push(srcs.at[mine], srcs.at[mine], d_send, d_recv, o, (me_g, peer))))
    if pair == 2:
        mate = me_m + 1 - 2 * lax.rem(me_m, 2)
        copies.append(push(srcs.at[mine], srcs.at[mine], d_send, d_recv, 1, (me_g, mate)))
    load_hist.wait()
    for o in range(groups - 1, -1, -1):
        to = lax.rem(me_g + o, groups)
        found = pick_rows(stale_rows[pl.ds(to, 1), :], hist, 4)
        found = found.astype(BF16).reshape(each, tile, width)
        at = pl.ds(stales + me_g * each, each)
        if o == 0:
            srcs[at] = found
        else:
            leaving[o] = found
            copies.append(push(leaving.at[o], srcs.at[at], s_send, s_recv, o, (to, me_m)))
    for o in range(1, members):
        peer = lax.rem(me_m + o, members)
        copies.append(push(asked.at[peer], wanted.at[me_m], p_send, p_recv, o, (me_g, peer)))

    def forward(b):
        chunk(b).wait()
        lhs = jnp.concatenate([tiles[b * per + t] for t in range(per)], axis=1)
        rhs = jnp.concatenate([own[jnp.minimum(src[t, b], blocks)] for t in range(per)], axis=0)
        part[b] = jnp.dot(lhs, rhs, preferred_element_type=F32)

    early = early_blocks(blocks)
    pl.loop(0, early, unroll=4)(forward)
    part[early:] = jnp.zeros((blocks - early, tile, width), F32)
    for o, copy in direct:
        copy.wait_recv()
        if pair == 2:
            at = pl.ds(bounds + lax.rem(me_m + members - o, members) * offered, offered)
            copies.append(push(srcs.at[at], srcs.at[at], r_send, r_recv, o, (me_g, mate)))

    one = (per, total)
    owner = jnp.floor((iota(one, 1) + 0.5) / per)
    rank = iota(one, 1) - per * owner
    place = jnp.where(iota((blocks, total), 0) == owner[:1, :], 1.0, 0.0).astype(BF16)
    spread = jnp.dot(src_vec[...].astype(F32).astype(BF16), place, preferred_element_type=F32)
    row = jnp.sum(jnp.where(iota(one, 0) == rank, spread, 0.0), axis=0, keepdims=True)
    owner = owner[:1, :]
    base = code_base(total)
    inner = blocks + members * taken
    wide = up(inner + 1, 128)
    hit = jnp.where((iota((wide, total), 0) == row) & (row < inner), 1.0, 0.0)
    rank = rank[:1, :]
    numbers = [(owner, float(per)), (rank, 1.0)]
    code[...], quad[...], offset, need, end = arrange(
        hit,
        [(owner, float(base))] + numbers,
        inner,
        0.0,
        quad.shape[1],
        float(base * blocks),
    )
    where = row - blocks
    spot = jnp.where(where < 0.0, row, row - inner + stales)
    for p in range(members):
        for k in range(taken):
            pick = picks[k : k + 1, p : p + 1].astype(F32)
            spot = jnp.where(where == p * taken + k, bounds + p * offered + pick, spot)
    remains = (row >= blocks) | (owner >= early)
    hit = jnp.where((iota((128, total), 0) == owner) & remains, 1.0, 0.0)
    rest_code[...], rest_quad[...], _, _, rest_end = arrange(
        hit,
        [(spot, float(base))] + numbers,
        blocks,
        1.0,
        rest_quad.shape[1],
        float(base * blocks),
    )
    last = jnp.where(need > 0.0, offset + need - 1.0, float(own_quads(total, blocks)))
    last = jnp.broadcast_to(last, (wide, wide)).T[:8, :]
    first = jnp.sum(jnp.where(iota((wide, 1), 0) == blocks, offset, 0.0), axis=0, keepdims=True)
    which = iota((8, wide), 0)
    found = jnp.where(which == 1, jnp.floor(first / STEP), last)
    found = jnp.where(which == 2, jnp.floor((end + (STEP - 1)) / STEP), found)
    found = jnp.where(which == 3, jnp.floor((rest_end + (STEP - 1)) / STEP), found)
    marks[...] = found.astype(jnp.int32)

    @pl.loop(early, blocks)
    def _(b):
        chunk(b).wait()

    load_cot.wait()
    keep_feats.wait()
    for _, copy in direct:
        copy.wait_send()
    for copy in copies:
        copy.wait()


def vmem_out(shape, dtype):
    return pltpu.VMEM(shape, dtype)


def hold(space, *arrays):
    return [pltpu.with_memory_space_constraint(a, space) for a in arrays]


def gather(features, history, tiles, cotangent, boundary_rows, picks, stale_rows, src, sizes):
    groups, members = sizes
    per, blocks = src.shape
    taken = picks.shape[0]
    tile, width = tiles.shape[1], features.shape[1]
    offered = boundary_rows.shape[1] // tile
    each = stale_rows.shape[1] // tile
    total = blocks * per
    inner = blocks + members * taken
    held = blocks + 1 + members * offered + groups * each
    vmem = pl.BlockSpec(memory_space=pltpu.VMEM)
    dma = pltpu.SemaphoreType.DMA
    return pl.pallas_call(
        functools.partial(gather_kernel, groups, members, blocks),
        out_shape=(
            vmem_out(tiles.shape, BF16),
            vmem_out((held, tile, width), BF16),
            vmem_out((blocks * tile, width), BF16),
            vmem_out((blocks, tile, width), F32),
            vmem_out((members, taken, 8, 128), jnp.int32),
            jax.ShapeDtypeStruct((8, 128), jnp.int32),
            jax.ShapeDtypeStruct((1, back_quads(total, inner)), jnp.int32),
            jax.ShapeDtypeStruct((8, 128), jnp.int32),
            jax.ShapeDtypeStruct((1, rest_quads_of(blocks, per)), jnp.int32),
            jax.ShapeDtypeStruct((8, up(inner + 1, 128)), jnp.int32),
        ),
        in_specs=[pl.BlockSpec(memory_space=pltpu.HBM)] * 8,
        out_specs=[vmem] * 10,
        scratch_shapes=[
            pltpu.VMEM(boundary_rows.shape, jnp.int32),
            pltpu.VMEM(picks.shape, jnp.int32),
            pltpu.VMEM(stale_rows.shape, jnp.int32),
            pltpu.SMEM(src.shape, jnp.int32),
            pltpu.VMEM(src.shape, jnp.int32),
            pltpu.VMEM((members, taken, 8, 128), jnp.int32),
            pltpu.VMEM((blocks + 1, tile, width), BF16),
            pltpu.VMEM((blocks, tile, width), BF16),
            pltpu.VMEM((groups, each, tile, width), BF16),
            dma((9,)),
            dma((blocks,)),
            dma((members,)),
            dma((members,)),
            dma((members,)),
            dma((members,)),
            dma((members,)),
            dma((members,)),
            dma((groups,)),
            dma((groups,)),
        ],
        compiler_params=pltpu.CompilerParams(
            collective_id=0, has_side_effects=True, vmem_limit_bytes=16 << 20
        ),
    )(
        *hold(
            pltpu.HBM,
            features.reshape(blocks, tile, width),
            history.reshape(blocks, tile, width),
            tiles,
            cotangent,
            boundary_rows,
            picks,
            stale_rows,
            src,
        )
    )


def middle_kernel(
    code,
    quad,
    rest_code,
    rest_quad,
    marks,
    tiles,
    srcs,
    cot,
    part,
    deg,
    w_self,
    w_neigh,
    out,
    back,
    dpre_out,
    halo_grad,
    weights,
    total,
    out_buf,
    grad,
    gt,
    inverse,
    sems,
):
    blocks, tile, width = part.shape
    base = code_base(tiles.shape[0])
    n_halo = halo_grad.shape[0]

    back[blocks] = jnp.zeros((width, tile), BF16)
    grad[blocks : blocks + n_halo] = jnp.zeros((n_halo, width, tile), F32)
    gt[...] = jnp.zeros_like(gt)
    inverse[...] = 1.0 / deg[...].astype(F32)

    def rest(step, acc):
        terms = []
        for u in range(STEP):
            lhs, rhs = [], []
            for i in range(QUAD):
                e, t = split(entry(rest_code, step, u * QUAD + i), base)
                lhs.append(tiles[t])
                rhs.append(srcs[e])
            terms.append(
                jnp.dot(
                    jnp.concatenate(lhs, axis=1),
                    jnp.concatenate(rhs, axis=0),
                    preferred_element_type=F32,
                )
            )
        for u in range(STEP):
            info = rest_quad[0, step * STEP + u]
            b = info // 2
            start = part[jnp.minimum(b, blocks - 1)]
            acc = terms[u] + jnp.where(info % 2 == 1, start, acc)
            total[b] = acc
        return acc

    lax.fori_loop(0, marks[3, 0], rest, jnp.zeros((tile, width), F32))

    group = 8
    rows = group * tile
    w_cat = jnp.concatenate([w_self[...], w_neigh[...]], axis=0)

    def store(c):
        at = pl.ds(pl.multiple_of(c * rows, rows), rows)
        return pltpu.make_async_copy(out_buf.at[at], out.at[at], sems.at[c])

    def middle(c):
        at = pl.ds(pl.multiple_of(c * rows, rows), rows)
        agg = []
        for i in range(group):
            b = c * group + i
            d = jnp.broadcast_to(inverse[pl.ds(b, 1), :], (tile, tile)).T
            agg.append((total[b] * d).astype(BF16))
        own = srcs[pl.ds(c * group, group)].reshape(rows, width)
        fa = jnp.concatenate([own, jnp.concatenate(agg, axis=0)], axis=1)
        pre = jnp.dot(fa, w_cat, preferred_element_type=F32)
        scale = lax.rsqrt(jnp.mean(pre * pre, axis=-1, keepdims=True) + 1e-05)
        out_buf[at, :] = (pre * scale).astype(BF16)
        store(c).start()
        g = cot[at, :].astype(F32)
        m = jnp.mean(g * pre, axis=-1, keepdims=True)
        dpre = (scale * g - pre * (scale**3 * m)).astype(BF16)
        dpre_out[at, :] = dpre
        gt[...] += lax.dot_general(dpre, fa, (((0,), (0,)), ((), ())), preferred_element_type=F32)
        bt = lax.dot_general(
            w_neigh[...], dpre, (((1,), (1,)), ((), ())), preferred_element_type=F32
        )
        for i in range(group):
            d = inverse[pl.ds(c * group + i, 1), :]
            back[c * group + i] = (bt[:, i * tile : (i + 1) * tile] * d).astype(BF16)

    pl.loop(0, blocks // group)(middle)

    weights[:width, :] = gt[:, :width].T
    weights[width:, :] = gt[:, width:].T

    def backward(step, acc):
        terms = quad_terms(step, code, back, tiles, base)
        for u in range(STEP):
            info = quad[0, step * STEP + u]
            acc = terms[u] + jnp.where(info % 2 == 1, 0.0, acc)
            grad[info // 2] = acc
        return acc

    lax.fori_loop(marks[1, 0], marks[2, 0], backward, jnp.zeros((width, tile), F32))
    for h in range(n_halo):
        halo_grad[h] = grad[blocks + h].T.astype(BF16)

    @pl.loop(0, blocks // group)
    def _(c):
        store(c).wait()


def quad_terms(step, code, back, tiles, base):
    terms = []
    for u in range(STEP):
        lhs, rhs = [], []
        for i in range(QUAD):
            b, t = split(entry(code, step, u * QUAD + i), base)
            lhs.append(back[b])
            rhs.append(tiles[t])
        terms.append(
            jnp.dot(
                jnp.concatenate(lhs, axis=1),
                jnp.concatenate(rhs, axis=0),
                preferred_element_type=F32,
            )
        )
    return terms


def middle(plans, tiles, srcs, cot, part, degree, w_self, w_neigh, n_halo):
    blocks, tile, width = part.shape
    nodes = blocks * tile
    smem = pl.BlockSpec(memory_space=pltpu.SMEM)
    vmem = pl.BlockSpec(memory_space=pltpu.VMEM)
    return pl.pallas_call(
        middle_kernel,
        out_shape=(
            jax.ShapeDtypeStruct((nodes, width), BF16),
            vmem_out((blocks + 1, width, tile), BF16),
            vmem_out((nodes, width), BF16),
            vmem_out((n_halo, tile, width), BF16),
            vmem_out((2 * width, width), F32),
        ),
        in_specs=[smem] * 5 + [vmem] * 7,
        out_specs=[pl.BlockSpec(memory_space=pl.ANY)] + [vmem] * 4,
        scratch_shapes=[
            pltpu.VMEM((blocks + 1, tile, width), F32),
            pltpu.VMEM((nodes, width), BF16),
            pltpu.VMEM((blocks + n_halo + 1, width, tile), F32),
            pltpu.VMEM((width, 2 * width), F32),
            pltpu.VMEM((blocks, tile), F32),
            pltpu.SemaphoreType.DMA((blocks,)),
        ],
        compiler_params=pltpu.CompilerParams(vmem_limit_bytes=20 << 20),
    )(
        *plans,
        *hold(pltpu.VMEM, tiles, srcs, cot, part),
        degree.reshape(blocks, tile),
        w_self,
        w_neigh,
    )


def combine_kernel(
    groups,
    members,
    factor,
    code,
    quad,
    marks,
    tiles,
    back,
    dpre,
    halo_grad,
    weights,
    wanted,
    rows,
    w_self,
    grad_features,
    grad_self,
    grad_neigh,
    accs,
    returned,
    landed,
    partial,
    across,
    share,
    whole,
    h_send,
    h_recv,
    a_send,
    a_recv,
    b_send,
    b_recv,
    c_send,
    c_recv,
):
    me_g, me_m = lax.axis_index("group"), lax.axis_index("member")
    taken = wanted.shape[1]
    blocks, (width, tile) = back.shape[0] - 1, back.shape[1:]
    offered = rows.shape[1] // tile
    piece = landed.shape[1]
    base = code_base(tiles.shape[0])
    steps = (accs.shape[0] - 1) // STEP

    def backward(step, acc):
        terms = quad_terms(step, code, back, tiles, base)
        for u in range(STEP):
            q = step * STEP + u
            acc = terms[u] + jnp.where(quad[0, q] % 2 == 1, 0.0, acc)
            accs[q] = acc
        return acc

    entered = greet(groups, members)
    accs[accs.shape[0] - 1] = jnp.zeros((width, tile), F32)
    cuts = [0, 3 * steps // 19, 11 * steps // 19, 17 * steps // 19, steps]
    acc = lax.fori_loop(cuts[0], cuts[1], backward, jnp.zeros((width, tile), F32))
    entered()
    copies, first, second, third = [], [], [], []
    for o in range(1, members):
        peer = lax.rem(me_m + o, members)
        at = pl.ds(pl.multiple_of(peer * piece, piece), piece)
        first.append(push(weights.at[at], landed.at[me_m], a_send, a_recv, o, (me_g, peer)))
    for o in range(1, members):
        peer = lax.rem(me_m + o, members)
        copies.append(
            push(
                halo_grad.at[pl.ds(peer * taken, taken)],
                returned.at[me_m],
                h_send,
                h_recv,
                o,
                (me_g, peer),
            )
        )
    mine = pl.ds(pl.multiple_of(me_m * piece, piece), piece)
    landed[me_m] = weights[mine, :]
    returned[me_m] = halo_grad[pl.ds(me_m * taken, taken)]
    acc = lax.fori_loop(cuts[1], cuts[2], backward, acc)
    for copy in first:
        copy.wait_recv()
    total = landed[0]
    for p in range(1, members):
        total = total + landed[p]
    partial[...] = total
    across[me_g] = total
    for o in range(1, groups):
        to = lax.rem(me_g + o, groups)
        second.append(push(partial, across.at[me_g], b_send, b_recv, o, (to, me_m)))
    acc = lax.fori_loop(cuts[2], cuts[3], backward, acc)
    for copy in second:
        copy.wait_recv()
    total = across[0]
    for g in range(1, groups):
        total = total + across[g]
    share[...] = total
    whole[mine, :] = total
    for o in range(1, members):
        peer = lax.rem(me_m + o, members)
        third.append(push(share, whole.at[mine], c_send, c_recv, o, (me_g, peer)))
    acc = lax.fori_loop(cuts[3], cuts[4], backward, acc)

    for copy in copies:
        copy.wait_recv()
    halves = []
    for j in range(offered):
        total = jnp.zeros((tile, width), F32)
        for p in range(members):
            for k in range(taken):
                w = jnp.broadcast_to(wanted[p, k][:1, :], (tile, width))
                total = total + jnp.where(w == j, returned[p, k].astype(F32), 0.0)
        high = total.astype(BF16)
        low = (total - high.astype(F32)).astype(BF16)
        halves.append(jnp.concatenate([high, low], axis=1))
    extra = jnp.concatenate(halves, axis=0)
    group = 4
    depth = group * tile

    def add(c):
        at = pl.ds(pl.multiple_of(c * depth, depth), depth)
        ids = lax.broadcasted_iota(jnp.int32, (depth, rows.shape[1]), 0) + c * depth
        hot = jnp.where(ids == rows[...], 1.0, 0.0).astype(BF16)
        more = jnp.dot(hot, extra, preferred_element_type=F32)
        own = lax.dot_general(
            dpre[at, :], w_self[...], (((1,), (1,)), ((), ())), preferred_element_type=F32
        )
        near = [accs[marks[0, c * group + i]].T for i in range(group)]
        own = own + jnp.concatenate(near, axis=0)
        grad_features[at, :] = (own + (more[:, :width] + more[:, width:])).astype(BF16)

    pl.loop(0, blocks // group)(add)
    for copy in third:
        copy.wait_recv()
    grad_self[...] = whole[:width, :] * factor
    grad_neigh[...] = whole[width:, :] * factor
    for copy in first + second + third + copies:
        copy.wait_send()


def combine(plans, tiles, back, dpre, halo_grad, weights, wanted, boundary_rows, w_self, sizes):
    groups, members = sizes
    nodes, width = dpre.shape
    tile = halo_grad.shape[1]
    blocks = nodes // tile
    taken = wanted.shape[1]
    piece = weights.shape[0] // members
    factor = 1.0 / math.sqrt(nodes * members * groups)
    smem = pl.BlockSpec(memory_space=pltpu.SMEM)
    vmem = pl.BlockSpec(memory_space=pltpu.VMEM)
    dma = pltpu.SemaphoreType.DMA
    return pl.pallas_call(
        functools.partial(combine_kernel, groups, members, factor),
        out_shape=(
            vmem_out((nodes, width), BF16),
            vmem_out((width, width), F32),
            vmem_out((width, width), F32),
        ),
        in_specs=[smem] * 3 + [vmem] * 8,
        out_specs=[vmem] * 3,
        scratch_shapes=[
            pltpu.VMEM((own_quads(tiles.shape[0], blocks) + 1, width, tile), F32),
            pltpu.VMEM((members, taken, tile, width), BF16),
            pltpu.VMEM((members, piece, width), F32),
            pltpu.VMEM((piece, width), F32),
            pltpu.VMEM((groups, piece, width), F32),
            pltpu.VMEM((piece, width), F32),
            pltpu.VMEM(weights.shape, F32),
            dma((members,)),
            dma((members,)),
            dma((members,)),
            dma((members,)),
            dma((groups,)),
            dma((groups,)),
            dma((members,)),
            dma((members,)),
        ],
        compiler_params=pltpu.CompilerParams(
            collective_id=1, has_side_effects=True, vmem_limit_bytes=24 << 20
        ),
    )(
        *plans,
        *hold(pltpu.VMEM, tiles, back, dpre, halo_grad, weights, wanted),
        boundary_rows,
        w_self,
    )


def write_kernel(a, b, c, out_a, out_b, out_c, sems):
    pairs = (a, out_a), (b, out_b), (c, out_c)
    copies = [pltpu.make_async_copy(x, y, sems.at[i]) for i, (x, y) in enumerate(pairs)]
    for copy in copies:
        copy.start()
    for copy in copies:
        copy.wait()


def write(*arrays):
    return pl.pallas_call(
        write_kernel,
        out_shape=[jax.ShapeDtypeStruct(a.shape, a.dtype) for a in arrays],
        in_specs=[pl.BlockSpec(memory_space=pltpu.VMEM)] * 3,
        out_specs=[pl.BlockSpec(memory_space=pltpu.HBM)] * 3,
        scratch_shapes=[pltpu.SemaphoreType.DMA((3,))],
        compiler_params=pltpu.CompilerParams(vmem_limit_bytes=4 << 20),
    )(*hold(pltpu.VMEM, *arrays))


def on_device(
    features,
    history,
    tiles,
    tile_src,
    degree,
    boundary_rows,
    picks,
    stale_rows,
    w_self,
    w_neigh,
    cotangent,
):
    sizes = lax.axis_size("group"), lax.axis_size("member")
    tiles, srcs, cot, part, wanted, code, quad, rest_code, rest_quad, marks = gather(
        features,
        history,
        tiles,
        cotangent,
        boundary_rows,
        picks.T,
        stale_rows,
        tile_src.T,
        sizes,
    )
    n_halo = sizes[1] * picks.shape[1]
    layer_out, back, dpre, halo_grad, weights = middle(
        (code, quad, rest_code, rest_quad, marks),
        tiles,
        srcs,
        cot,
        part,
        degree,
        w_self,
        w_neigh,
        n_halo,
    )
    grad_features, grad_self, grad_neigh = combine(
        (code, quad, marks),
        tiles,
        back,
        dpre,
        halo_grad,
        weights,
        wanted,
        boundary_rows,
        w_self,
        sizes,
    )
    return layer_out, *write(grad_features, grad_self, grad_neigh)


def solution(mesh):
    nodes = P(("group", "member"), None)
    placed = (
        nodes,
        nodes,
        P(("group", "member"), None, None),
        nodes,
        P(("group", "member")),
        nodes,
        nodes,
        nodes,
        P(),
        P(),
        nodes,
    )
    return jax.shard_map(
        on_device,
        mesh=mesh,
        in_specs=placed,
        out_specs=(nodes, nodes, P(), P()),
        check_vma=False,
    )
```

```python
import functools
import math

import jax
import jax.numpy as jnp
from jax import lax
from jax.experimental import pallas as pl
from jax.experimental.pallas import tpu as pltpu
from jax.sharding import PartitionSpec as P

QUAD = 4
STEP = 8
EARLY = 12
CUTS = 0, 2, 6, 9
F32 = jnp.float32
BF16 = jnp.bfloat16
MESH = pl.DeviceIdType.MESH


def up(value, unit):
    return -(-value // unit) * unit


def iota(shape, axis):
    return lax.broadcasted_iota(jnp.int32, shape, axis).astype(F32)


def column(value):
    return jnp.broadcast_to(value, (8, value.shape[1])).T[:, :1]


def arrange(hit, values, keys, least, quads, pad):
    wide, total = hit.shape
    low = hit.astype(BF16)
    earlier = jnp.where(iota((128, 128), 0) < iota((128, 128), 1), 1.0, 0.0).astype(BF16)
    count = jnp.zeros((wide, 1), F32)
    within = []
    for c in range(0, total, 128):
        part = low[:, c : c + 128]
        within.append(jnp.dot(part, earlier, preferred_element_type=F32) + count)
        count = count + jnp.sum(hit[:, c : c + 128], axis=1, keepdims=True)
    within = jnp.concatenate(within, axis=1)
    need = jnp.floor((count + (QUAD - 1)) / QUAD)
    need = jnp.where(iota((wide, 1), 0) < keys, jnp.maximum(need, least), 0.0)
    spread = jnp.broadcast_to(need, (wide, wide)).T
    before = iota((wide, wide), 1) < iota((wide, wide), 0)
    offset = jnp.sum(jnp.where(before, spread, 0.0), axis=1, keepdims=True)
    end = jnp.sum(spread[:1, :], axis=1, keepdims=True)
    pos = jnp.sum(hit * (QUAD * offset + within + 1.0), axis=0, keepdims=True) - 1.0
    high = jnp.floor(pos / 128.0)
    place = jnp.where(column(pos - 128.0 * high) == iota((total, 128), 1), 1.0, 0.0).astype(BF16)
    line = jnp.where(iota((8, total), 0) == high, 1.0, 0.0)
    terms = [line] + [line * row for row, _ in values]
    found = jnp.dot(
        jnp.concatenate(terms, axis=0).astype(BF16), place, preferred_element_type=F32
    )
    code = jnp.zeros((8, 128), F32)
    for i, (_, scale) in enumerate(values):
        code = code + scale * found[8 * (i + 1) : 8 * (i + 2), :]
    code = jnp.where(found[:8, :] > 0.0, code, pad)
    q = iota((wide, quads), 1)
    inside = (offset <= q) & (q < offset + need)
    info = 2.0 * iota((wide, quads), 0) + jnp.where(offset == q, 1.0, 0.0)
    quad = jnp.sum(jnp.where(inside, info, 0.0), axis=0, keepdims=True)
    quad = jnp.where(q[:1, :] < end, quad, 2.0 * keys + 1.0)
    return code.astype(jnp.int32), quad.astype(jnp.int32), offset, need, end


def back_quads(total, wanted):
    return up((total + wanted * (QUAD - 1)) // QUAD, 128)


def rest_quads_of(blocks, per):
    return up(blocks * (-(-per // QUAD)), 128)


def early_blocks(blocks):
    return blocks * EARLY // 32


def own_quads(total, blocks):
    return up((total + blocks * (QUAD - 1)) // QUAD, STEP)


def code_base(total):
    return 1 << (total - 1).bit_length()


def split(value, base):
    return lax.shift_right_logical(value, base.bit_length() - 1), value & (base - 1)


def entry(code, step, i):
    line = 128 // (STEP * QUAD)
    first = lax.shift_right_logical(step, line.bit_length() - 1)
    return code[first, (step & (line - 1)) * (STEP * QUAD) + i]


def greet(groups, members):
    me_g, me_m = lax.axis_index("group"), lax.axis_index("member")
    barrier = pltpu.get_barrier_semaphore()
    peers = [(me_g, partner(me_m, o, members)) for o in range(1, members)]
    peers += [(lax.rem(me_g + o, groups), me_m) for o in range(1, groups)]
    for peer in peers:
        pl.semaphore_signal(barrier, inc=1, device_id=peer, device_id_type=MESH)
    return lambda: pl.semaphore_wait(barrier, len(peers))


def partner(me, o, members):
    if members & (members - 1):
        return lax.rem(me + o, members)
    bit = 1
    while bit <= o:
        if o & bit:
            me = me + bit - 2 * bit * lax.rem(lax.div(me, bit), 2)
        bit *= 2
    return me


def sender(me, o, members):
    if members & (members - 1):
        return lax.rem(me + members - o, members)
    return partner(me, o, members)


def push(src, dst, send, recv, o, device):
    copy = pltpu.make_async_remote_copy(
        src_ref=src,
        dst_ref=dst,
        send_sem=send.at[o],
        recv_sem=recv.at[o],
        device_id=device,
        device_id_type=MESH,
    )
    copy.start()
    return copy


def pick_rows(row, table, chunk):
    count = row.shape[1]
    blocks, tile, width = table.shape
    half = blocks // 2
    ids_column = jnp.broadcast_to(row, (8, count)).T[:, :1]
    second = ids_column >= half * tile
    ids_column = jnp.where(second, ids_column - half * tile, ids_column)
    total = jnp.zeros((count, 2 * width), F32)
    depth = chunk * tile
    for c in range(0, half, chunk):
        ids = lax.broadcasted_iota(jnp.int32, (count, depth), 1) + c * tile
        hot = jnp.where(ids == ids_column, 1.0, 0.0).astype(BF16)
        both = [table[a : a + chunk].reshape(depth, width) for a in (c, half + c)]
        total = total + jnp.dot(
            hot, jnp.concatenate(both, axis=1), preferred_element_type=F32
        )
    return jnp.where(second, total[:, width:], total[:, :width])


def gather_kernel(
    groups,
    members,
    blocks,
    feats_in,
    hist_in,
    tiles_in,
    cot_in,
    rows_in,
    picks_in,
    stale_rows_in,
    src_in,
    tiles,
    srcs,
    cot,
    part,
    wanted,
    code_out,
    quad_out,
    rest_code_out,
    rest_quad_out,
    marks_out,
    spots_out,
    code,
    quad,
    rest_code,
    rest_quad,
    marks,
    spots_vec,
    rows,
    picks,
    stale_rows,
    src,
    src_vec,
    asked,
    own,
    hist,
    leaving,
    l_sems,
    t_sems,
    p_send,
    p_recv,
    d_send,
    d_recv,
    r_send,
    r_recv,
    s_send,
    s_recv,
):
    me_g, me_m = lax.axis_index("group"), lax.axis_index("member")
    taken = picks.shape[0]
    tile, width = srcs.shape[1], srcs.shape[2]
    offered = rows.shape[1] // tile
    each = stale_rows.shape[1] // tile
    per = src.shape[0]
    total = blocks * per
    pair = 1 if members & (members - 1) else 2

    load_feats = pltpu.make_async_copy(feats_in, own.at[pl.ds(0, blocks)], l_sems.at[0])
    keep_feats = pltpu.make_async_copy(feats_in, srcs.at[pl.ds(0, blocks)], l_sems.at[8])
    load_hist = pltpu.make_async_copy(hist_in, hist, l_sems.at[1])
    load_cot = pltpu.make_async_copy(cot_in, cot, l_sems.at[2])

    def chunk(b):
        at = pl.ds(b * per, per)
        return pltpu.make_async_copy(tiles_in.at[at], tiles.at[at], t_sems.at[b])

    small = [
        pltpu.make_async_copy(a, b, l_sems.at[3 + i])
        for i, (a, b) in enumerate(
            (
                (rows_in, rows),
                (picks_in, picks),
                (stale_rows_in, stale_rows),
                (src_in, src),
                (src_in, src_vec),
            )
        )
    ]
    load_feats.start()
    for copy in small:
        copy.start()
    load_hist.start()
    entered = greet(groups, members)
    for copy in small:
        copy.wait()
    for p in range(members):
        for k in range(taken):
            asked[p, k] = jnp.broadcast_to(picks[k : k + 1, p : p + 1], asked.shape[2:])
    wanted[me_m] = asked[me_m]
    own[blocks] = jnp.zeros((tile, width), BF16)
    srcs[blocks] = jnp.zeros((tile, width), BF16)
    load_feats.wait()

    @pl.loop(0, blocks)
    def _(b):
        chunk(b).start()

    load_cot.start()
    keep_feats.start()
    bounds = blocks + 1
    stales = bounds + members * offered
    mine = pl.ds(bounds + me_m * offered, offered)
    srcs[mine] = pick_rows(rows[...], own.at[pl.ds(0, blocks)], 4).astype(BF16).reshape(
        offered, tile, width
    )
    entered()
    direct, copies = [], []
    for o in range(1, members):
        if o % pair == 0:
            peer = partner(me_m, o, members)
            direct.append((o, push(srcs.at[mine], srcs.at[mine], d_send, d_recv, o, (me_g, peer))))
    if pair == 2:
        mate = partner(me_m, 1, members)
        copies.append(push(srcs.at[mine], srcs.at[mine], d_send, d_recv, 1, (me_g, mate)))
    load_hist.wait()
    for o in range(groups - 1, -1, -1):
        to = lax.rem(me_g + o, groups)
        found = pick_rows(stale_rows[pl.ds(to, 1), :], hist, 4)
        found = found.astype(BF16).reshape(each, tile, width)
        at = pl.ds(stales + me_g * each, each)
        if o == 0:
            srcs[at] = found
        else:
            leaving[o] = found
            copies.append(push(leaving.at[o], srcs.at[at], s_send, s_recv, o, (to, me_m)))
    for o in range(1, members):
        peer = partner(me_m, o, members)
        copies.append(push(asked.at[peer], wanted.at[me_m], p_send, p_recv, o, (me_g, peer)))

    def forward(b):
        chunk(b).wait()
        lhs = jnp.concatenate([tiles[b * per + t] for t in range(per)], axis=1)
        rhs = jnp.concatenate([own[jnp.minimum(src[t, b], blocks)] for t in range(per)], axis=0)
        part[b] = jnp.dot(lhs, rhs, preferred_element_type=F32)

    early = early_blocks(blocks)
    pl.loop(0, early, unroll=4)(forward)
    for o, copy in direct:
        copy.wait_recv()
        if pair == 2:
            at = pl.ds(bounds + sender(me_m, o, members) * offered, offered)
            copies.append(push(srcs.at[at], srcs.at[at], r_send, r_recv, o, (me_g, mate)))

    one = (per, total)
    owner = jnp.floor((iota(one, 1) + 0.5) / per)
    rank = iota(one, 1) - per * owner
    place = jnp.where(iota((blocks, total), 0) == owner[:1, :], 1.0, 0.0).astype(BF16)
    spread = jnp.dot(src_vec[...].astype(F32).astype(BF16), place, preferred_element_type=F32)
    row = jnp.sum(jnp.where(iota(one, 0) == rank, spread, 0.0), axis=0, keepdims=True)
    owner = owner[:1, :]
    base = code_base(total)
    inner = blocks + members * taken
    wide = up(inner + 1, 128)
    hit = jnp.where((iota((wide, total), 0) == row) & (row < inner), 1.0, 0.0)
    rank = rank[:1, :]
    numbers = [(owner, float(per)), (rank, 1.0)]
    code[...], quad[...], offset, need, end = arrange(
        hit,
        [(owner, float(base))] + numbers,
        inner,
        0.0,
        quad.shape[1],
        float(base * blocks),
    )

    def place_of(s):
        halo = s - blocks
        spot = jnp.where(halo < 0.0, s, s - inner + stales)
        for p in range(members):
            for k in range(taken):
                pick = picks[k : k + 1, p : p + 1].astype(F32)
                spot = jnp.where(halo == p * taken + k, bounds + p * offered + pick, spot)
        return spot

    spots_vec[...] = place_of(src_vec[...].astype(F32)).astype(jnp.int32)
    spot = place_of(row)
    remains = (row >= blocks) & (owner < early)
    hit = jnp.where((iota((128, total), 0) == owner) & remains, 1.0, 0.0)
    rest_code[...], rest_quad[...], _, _, rest_end = arrange(
        hit,
        [(spot, float(base))] + numbers,
        early,
        1.0,
        rest_quad.shape[1],
        float(base * blocks),
    )
    last = jnp.where(need > 0.0, offset + need - 1.0, float(own_quads(total, blocks)))
    last = jnp.broadcast_to(last, (wide, wide)).T[:8, :]
    first = jnp.sum(jnp.where(iota((wide, 1), 0) == blocks, offset, 0.0), axis=0, keepdims=True)
    which = iota((8, wide), 0)
    found = jnp.where(which == 1, jnp.floor(first / STEP), last)
    found = jnp.where(which == 2, jnp.floor((end + (STEP - 1)) / STEP), found)
    found = jnp.where(which == 3, jnp.floor((rest_end + (STEP - 1)) / STEP), found)
    marks[...] = found.astype(jnp.int32)

    outs = [
        pltpu.make_async_copy(a, b, l_sems.at[9 + i])
        for i, (a, b) in enumerate(
            (
                (code, code_out),
                (quad, quad_out),
                (rest_code, rest_code_out),
                (rest_quad, rest_quad_out),
                (marks, marks_out),
                (spots_vec, spots_out),
            )
        )
    ]
    for copy in outs:
        copy.start()

    @pl.loop(early, blocks)
    def _(b):
        chunk(b).wait()

    for copy in outs:
        copy.wait()
    load_cot.wait()
    keep_feats.wait()
    for _, copy in direct:
        copy.wait_send()
    for copy in copies:
        copy.wait()


def vmem_out(shape, dtype):
    return pltpu.VMEM(shape, dtype)


def hold(space, *arrays):
    return [pltpu.with_memory_space_constraint(a, space) for a in arrays]


def gather(features, history, tiles, cotangent, boundary_rows, picks, stale_rows, src, sizes):
    groups, members = sizes
    per, blocks = src.shape
    taken = picks.shape[0]
    tile, width = tiles.shape[1], features.shape[1]
    offered = boundary_rows.shape[1] // tile
    each = stale_rows.shape[1] // tile
    total = blocks * per
    inner = blocks + members * taken
    lists = (
        (8, 128),
        (1, back_quads(total, inner)),
        (8, 128),
        (1, rest_quads_of(blocks, per)),
        (8, up(inner + 1, 128)),
        src.shape,
    )
    held = blocks + 1 + members * offered + groups * each
    vmem = pl.BlockSpec(memory_space=pltpu.VMEM)
    dma = pltpu.SemaphoreType.DMA
    return pl.pallas_call(
        functools.partial(gather_kernel, groups, members, blocks),
        out_shape=(
            vmem_out(tiles.shape, BF16),
            vmem_out((held, tile, width), BF16),
            vmem_out((blocks * tile, width), BF16),
            vmem_out((early_blocks(blocks), tile, width), F32),
            vmem_out((members, taken, 8, 128), jnp.int32),
            *[pltpu.SMEM(shape, jnp.int32) for shape in lists],
        ),
        in_specs=[pl.BlockSpec(memory_space=pltpu.HBM)] * 8,
        out_specs=[vmem] * 5 + [pl.BlockSpec(memory_space=pltpu.SMEM)] * 6,
        scratch_shapes=[
            *[pltpu.VMEM(shape, jnp.int32) for shape in lists],
            pltpu.VMEM(boundary_rows.shape, jnp.int32),
            pltpu.VMEM(picks.shape, jnp.int32),
            pltpu.VMEM(stale_rows.shape, jnp.int32),
            pltpu.SMEM(src.shape, jnp.int32),
            pltpu.VMEM(src.shape, jnp.int32),
            pltpu.VMEM((members, taken, 8, 128), jnp.int32),
            pltpu.VMEM((blocks + 1, tile, width), BF16),
            pltpu.VMEM((blocks, tile, width), BF16),
            pltpu.VMEM((groups, each, tile, width), BF16),
            dma((15,)),
            dma((blocks,)),
            dma((members,)),
            dma((members,)),
            dma((members,)),
            dma((members,)),
            dma((members,)),
            dma((members,)),
            dma((groups,)),
            dma((groups,)),
        ],
        compiler_params=pltpu.CompilerParams(
            collective_id=0, has_side_effects=True, vmem_limit_bytes=16 << 20
        ),
    )(
        *hold(
            pltpu.HBM,
            features.reshape(blocks, tile, width),
            history.reshape(blocks, tile, width),
            tiles,
            cotangent,
            boundary_rows,
            picks,
            stale_rows,
            src,
        )
    )


def middle_kernel(
    code,
    quad,
    rest_code,
    rest_quad,
    marks,
    spots,
    tiles,
    srcs,
    cot,
    part,
    deg,
    w_self,
    w_neigh,
    out,
    back,
    dpre_out,
    halo_grad,
    weights,
    total,
    out_buf,
    grad,
    gt,
    inverse,
    sems,
):
    early, tile, width = part.shape
    blocks = deg.shape[0]
    per = spots.shape[0]
    base = code_base(tiles.shape[0])
    n_halo = halo_grad.shape[0]

    back[blocks] = jnp.zeros((width, tile), BF16)
    grad[blocks : blocks + n_halo] = jnp.zeros((n_halo, width, tile), F32)
    gt[...] = jnp.zeros_like(gt)
    inverse[...] = 1.0 / deg[...].astype(F32)

    def rest(step, acc):
        terms = []
        for u in range(STEP):
            lhs, rhs = [], []
            for i in range(QUAD):
                e, t = split(entry(rest_code, step, u * QUAD + i), base)
                lhs.append(tiles[t])
                rhs.append(srcs[e])
            terms.append(
                jnp.dot(
                    jnp.concatenate(lhs, axis=1),
                    jnp.concatenate(rhs, axis=0),
                    preferred_element_type=F32,
                )
            )
        for u in range(STEP):
            info = rest_quad[0, step * STEP + u]
            b = info // 2
            start = part[jnp.minimum(b, early - 1)]
            acc = terms[u] + jnp.where(info % 2 == 1, start, acc)
            total[b] = acc
        return acc

    lax.fori_loop(0, marks[3, 0], rest, jnp.zeros((tile, width), F32))

    def forward(b):
        lhs = jnp.concatenate([tiles[b * per + t] for t in range(per)], axis=1)
        rhs = jnp.concatenate([srcs[spots[t, b]] for t in range(per)], axis=0)
        total[b] = jnp.dot(lhs, rhs, preferred_element_type=F32)

    pl.loop(early, blocks, unroll=4)(forward)

    group = 8
    rows = group * tile
    w_cat = jnp.concatenate([w_self[...], w_neigh[...]], axis=0)

    def store(c):
        at = pl.ds(pl.multiple_of(c * rows, rows), rows)
        return pltpu.make_async_copy(out_buf.at[at], out.at[at], sems.at[c])

    def middle(c):
        at = pl.ds(pl.multiple_of(c * rows, rows), rows)
        agg = []
        for i in range(group):
            b = c * group + i
            d = jnp.broadcast_to(inverse[pl.ds(b, 1), :], (tile, tile)).T
            agg.append((total[b] * d).astype(BF16))
        own = srcs[pl.ds(c * group, group)].reshape(rows, width)
        fa = jnp.concatenate([own, jnp.concatenate(agg, axis=0)], axis=1)
        pre = jnp.dot(fa, w_cat, preferred_element_type=F32)
        scale = lax.rsqrt(jnp.mean(pre * pre, axis=-1, keepdims=True) + 1e-05)
        out_buf[at, :] = (pre * scale).astype(BF16)
        store(c).start()
        g = cot[at, :].astype(F32)
        m = jnp.mean(g * pre, axis=-1, keepdims=True)
        dpre = (scale * g - pre * (scale**3 * m)).astype(BF16)
        dpre_out[at, :] = dpre
        gt[...] += lax.dot_general(dpre, fa, (((0,), (0,)), ((), ())), preferred_element_type=F32)
        bt = lax.dot_general(
            w_neigh[...], dpre, (((1,), (1,)), ((), ())), preferred_element_type=F32
        )
        for i in range(group):
            d = inverse[pl.ds(c * group + i, 1), :]
            back[c * group + i] = (bt[:, i * tile : (i + 1) * tile] * d).astype(BF16)

    pl.loop(0, blocks // group)(middle)

    weights[:width, :] = gt[:, :width].T.astype(weights.dtype)
    weights[width:, :] = gt[:, width:].T.astype(weights.dtype)

    def backward(step, acc):
        terms = quad_terms(step, code, back, tiles, base)
        for u in range(STEP):
            info = quad[0, step * STEP + u]
            acc = terms[u] + jnp.where(info % 2 == 1, 0.0, acc)
            grad[info // 2] = acc
        return acc

    lax.fori_loop(marks[1, 0], marks[2, 0], backward, jnp.zeros((width, tile), F32))
    for h in range(n_halo):
        halo_grad[h] = grad[blocks + h].T.astype(BF16)

    @pl.loop(0, blocks // group)
    def _(c):
        store(c).wait()


def quad_terms(step, code, back, tiles, base):
    terms = []
    for u in range(STEP):
        lhs, rhs = [], []
        for i in range(QUAD):
            b, t = split(entry(code, step, u * QUAD + i), base)
            lhs.append(back[b])
            rhs.append(tiles[t])
        terms.append(
            jnp.dot(
                jnp.concatenate(lhs, axis=1),
                jnp.concatenate(rhs, axis=0),
                preferred_element_type=F32,
            )
        )
    return terms


def middle(plans, tiles, srcs, cot, part, degree, w_self, w_neigh, n_halo, wire):
    tile, width = part.shape[1:]
    nodes = degree.shape[0]
    blocks = nodes // tile
    smem = pl.BlockSpec(memory_space=pltpu.SMEM)
    vmem = pl.BlockSpec(memory_space=pltpu.VMEM)
    return pl.pallas_call(
        middle_kernel,
        out_shape=(
            jax.ShapeDtypeStruct((nodes, width), BF16),
            vmem_out((blocks + 1, width, tile), BF16),
            vmem_out((nodes, width), BF16),
            vmem_out((n_halo, tile, width), BF16),
            vmem_out((2 * width, width), wire),
        ),
        in_specs=[smem] * 6 + [vmem] * 7,
        out_specs=[pl.BlockSpec(memory_space=pl.ANY)] + [vmem] * 4,
        scratch_shapes=[
            pltpu.VMEM((blocks + 1, tile, width), F32),
            pltpu.VMEM((nodes, width), BF16),
            pltpu.VMEM((blocks + n_halo + 1, width, tile), F32),
            pltpu.VMEM((width, 2 * width), F32),
            pltpu.VMEM((blocks, tile), F32),
            pltpu.SemaphoreType.DMA((blocks,)),
        ],
        compiler_params=pltpu.CompilerParams(vmem_limit_bytes=26 << 20),
    )(
        *hold(pltpu.SMEM, *plans),
        *hold(pltpu.VMEM, tiles, srcs, cot, part),
        degree.reshape(blocks, tile),
        w_self,
        w_neigh,
    )


def combine_kernel(
    groups,
    members,
    factor,
    code,
    quad,
    marks,
    tiles,
    back,
    dpre,
    halo_grad,
    weights,
    wanted,
    rows,
    w_self,
    grad_features,
    grad_self,
    grad_neigh,
    accs,
    returned,
    landed,
    partial,
    across,
    share,
    whole,
    h_send,
    h_recv,
    a_send,
    a_recv,
    b_send,
    b_recv,
    c_send,
    c_recv,
):
    me_g, me_m = lax.axis_index("group"), lax.axis_index("member")
    taken = wanted.shape[1]
    blocks, (width, tile) = back.shape[0] - 1, back.shape[1:]
    offered = rows.shape[1] // tile
    piece = landed.shape[1]
    base = code_base(tiles.shape[0])
    steps = (accs.shape[0] - 1) // STEP

    def backward(step, acc):
        terms = quad_terms(step, code, back, tiles, base)
        for u in range(STEP):
            q = step * STEP + u
            acc = terms[u] + jnp.where(quad[0, q] % 2 == 1, 0.0, acc)
            accs[q] = acc
        return acc

    entered = greet(groups, members)
    accs[accs.shape[0] - 1] = jnp.zeros((width, tile), F32)
    cuts = [steps * c // 10 for c in CUTS] + [steps]
    acc = lax.fori_loop(cuts[0], cuts[1], backward, jnp.zeros((width, tile), F32))
    entered()
    copies, first, second, third = [], [], [], []
    for o in range(1, members):
        peer = partner(me_m, o, members)
        at = pl.ds(pl.multiple_of(peer * piece, piece), piece)
        first.append(push(weights.at[at], landed.at[me_m], a_send, a_recv, o, (me_g, peer)))
    for o in range(1, members):
        peer = partner(me_m, o, members)
        copies.append(
            push(
                halo_grad.at[pl.ds(peer * taken, taken)],
                returned.at[me_m],
                h_send,
                h_recv,
                o,
                (me_g, peer),
            )
        )
    mine = pl.ds(pl.multiple_of(me_m * piece, piece), piece)
    landed[me_m] = weights[mine, :]
    returned[me_m] = halo_grad[pl.ds(me_m * taken, taken)]
    acc = lax.fori_loop(cuts[1], cuts[2], backward, acc)
    for copy in first:
        copy.wait_recv()
    total = landed[0].astype(F32)
    for p in range(1, members):
        total = total + landed[p].astype(F32)
    partial[...] = total.astype(partial.dtype)
    across[me_g] = total.astype(partial.dtype)
    for o in range(1, groups):
        to = lax.rem(me_g + o, groups)
        second.append(push(partial, across.at[me_g], b_send, b_recv, o, (to, me_m)))
    acc = lax.fori_loop(cuts[2], cuts[3], backward, acc)
    for copy in second:
        copy.wait_recv()
    total = across[0].astype(F32)
    for g in range(1, groups):
        total = total + across[g].astype(F32)
    share[...] = total.astype(share.dtype)
    whole[mine, :] = total.astype(share.dtype)
    for o in range(1, members):
        peer = partner(me_m, o, members)
        third.append(push(share, whole.at[mine], c_send, c_recv, o, (me_g, peer)))
    acc = lax.fori_loop(cuts[3], cuts[4], backward, acc)

    for copy in copies:
        copy.wait_recv()
    halves = []
    for j in range(offered):
        total = jnp.zeros((tile, width), F32)
        for p in range(members):
            for k in range(taken):
                w = jnp.broadcast_to(wanted[p, k][:1, :], (tile, width))
                total = total + jnp.where(w == j, returned[p, k].astype(F32), 0.0)
        high = total.astype(BF16)
        low = (total - high.astype(F32)).astype(BF16)
        halves.append(jnp.concatenate([high, low], axis=1))
    extra = jnp.concatenate(halves, axis=0)
    group = 4
    depth = group * tile

    def add(c):
        at = pl.ds(pl.multiple_of(c * depth, depth), depth)
        ids = lax.broadcasted_iota(jnp.int32, (depth, rows.shape[1]), 0) + c * depth
        hot = jnp.where(ids == rows[...], 1.0, 0.0).astype(BF16)
        more = jnp.dot(hot, extra, preferred_element_type=F32)
        own = lax.dot_general(
            dpre[at, :], w_self[...], (((1,), (1,)), ((), ())), preferred_element_type=F32
        )
        near = [accs[marks[0, c * group + i]].T for i in range(group)]
        own = own + jnp.concatenate(near, axis=0)
        grad_features[at, :] = (own + (more[:, :width] + more[:, width:])).astype(BF16)

    pl.loop(0, blocks // group)(add)
    for copy in third:
        copy.wait_recv()
    grad_self[...] = whole[:width, :].astype(F32) * factor
    grad_neigh[...] = whole[width:, :].astype(F32) * factor
    for copy in first + second + third + copies:
        copy.wait_send()


def combine(plans, tiles, back, dpre, halo_grad, weights, wanted, boundary_rows, w_self, sizes):
    groups, members = sizes
    nodes, width = dpre.shape
    tile = halo_grad.shape[1]
    blocks = nodes // tile
    taken = wanted.shape[1]
    piece = weights.shape[0] // members
    factor = 1.0 / math.sqrt(nodes * members * groups)
    smem = pl.BlockSpec(memory_space=pltpu.SMEM)
    vmem = pl.BlockSpec(memory_space=pltpu.VMEM)
    dma = pltpu.SemaphoreType.DMA
    return pl.pallas_call(
        functools.partial(combine_kernel, groups, members, factor),
        out_shape=(
            vmem_out((nodes, width), BF16),
            vmem_out((width, width), F32),
            vmem_out((width, width), F32),
        ),
        in_specs=[smem] * 3 + [vmem] * 8,
        out_specs=[vmem] * 3,
        scratch_shapes=[
            pltpu.VMEM((own_quads(tiles.shape[0], blocks) + 1, width, tile), F32),
            pltpu.VMEM((members, taken, tile, width), BF16),
            pltpu.VMEM((members, piece, width), weights.dtype),
            pltpu.VMEM((piece, width), weights.dtype),
            pltpu.VMEM((groups, piece, width), weights.dtype),
            pltpu.VMEM((piece, width), weights.dtype),
            pltpu.VMEM(weights.shape, weights.dtype),
            dma((members,)),
            dma((members,)),
            dma((members,)),
            dma((members,)),
            dma((groups,)),
            dma((groups,)),
            dma((members,)),
            dma((members,)),
        ],
        compiler_params=pltpu.CompilerParams(
            collective_id=1, has_side_effects=True, vmem_limit_bytes=24 << 20
        ),
    )(
        *hold(pltpu.SMEM, *plans),
        *hold(pltpu.VMEM, tiles, back, dpre, halo_grad, weights, wanted),
        boundary_rows,
        w_self,
    )


def write_kernel(a, b, c, out_a, out_b, out_c, sems):
    pairs = (a, out_a), (b, out_b), (c, out_c)
    copies = [pltpu.make_async_copy(x, y, sems.at[i]) for i, (x, y) in enumerate(pairs)]
    for copy in copies:
        copy.start()
    for copy in copies:
        copy.wait()


def write(*arrays):
    return pl.pallas_call(
        write_kernel,
        out_shape=[jax.ShapeDtypeStruct(a.shape, a.dtype) for a in arrays],
        in_specs=[pl.BlockSpec(memory_space=pltpu.VMEM)] * 3,
        out_specs=[pl.BlockSpec(memory_space=pltpu.HBM)] * 3,
        scratch_shapes=[pltpu.SemaphoreType.DMA((3,))],
        compiler_params=pltpu.CompilerParams(vmem_limit_bytes=4 << 20),
    )(*hold(pltpu.VMEM, *arrays))


def on_device(
    features,
    history,
    tiles,
    tile_src,
    degree,
    boundary_rows,
    picks,
    stale_rows,
    w_self,
    w_neigh,
    cotangent,
):
    sizes = lax.axis_size("group"), lax.axis_size("member")
    tiles, srcs, cot, part, wanted, code, quad, rest_code, rest_quad, marks, spots = gather(
        features,
        history,
        tiles,
        cotangent,
        boundary_rows,
        picks.T,
        stale_rows,
        tile_src.T,
        sizes,
    )
    n_halo = sizes[1] * picks.shape[1]
    wire = F32 if (2 * w_self.shape[0] // sizes[1]) % 16 else BF16
    layer_out, back, dpre, halo_grad, weights = middle(
        (code, quad, rest_code, rest_quad, marks, spots),
        tiles,
        srcs,
        cot,
        part,
        degree,
        w_self,
        w_neigh,
        n_halo,
        wire,
    )
    grad_features, grad_self, grad_neigh = combine(
        (code, quad, marks),
        tiles,
        back,
        dpre,
        halo_grad,
        weights,
        wanted,
        boundary_rows,
        w_self,
        sizes,
    )
    return layer_out, *write(grad_features, grad_self, grad_neigh)


def solution(mesh):
    nodes = P(("group", "member"), None)
    placed = (
        nodes,
        nodes,
        P(("group", "member"), None, None),
        nodes,
        P(("group", "member")),
        nodes,
        nodes,
        nodes,
        P(),
        P(),
        nodes,
    )
    return jax.shard_map(
        on_device,
        mesh=mesh,
        in_specs=placed,
        out_specs=(nodes, nodes, P(), P()),
        check_vma=False,
    )
```

```python
import functools
import math

import jax
import jax.numpy as jnp
from jax import lax
from jax.experimental import pallas as pl
from jax.experimental.pallas import tpu as pltpu
from jax.sharding import PartitionSpec as P

QUAD = 4
STEP = 8
EARLY = 12
CUTS = 0, 2, 6, 9
F32 = jnp.float32
BF16 = jnp.bfloat16
MESH = pl.DeviceIdType.MESH


def up(value, unit):
    return -(-value // unit) * unit


def iota(shape, axis):
    return lax.broadcasted_iota(jnp.int32, shape, axis).astype(F32)


def column(value):
    return jnp.broadcast_to(value, (8, value.shape[1])).T[:, :1]


def arrange(hit, values, keys, least, quads, pad):
    wide, total = hit.shape
    low = hit.astype(BF16)
    earlier = jnp.where(iota((128, 128), 0) < iota((128, 128), 1), 1.0, 0.0).astype(BF16)
    count = jnp.zeros((wide, 1), F32)
    within = []
    for c in range(0, total, 128):
        part = low[:, c : c + 128]
        within.append(jnp.dot(part, earlier, preferred_element_type=F32) + count)
        count = count + jnp.sum(hit[:, c : c + 128], axis=1, keepdims=True)
    within = jnp.concatenate(within, axis=1)
    need = jnp.floor((count + (QUAD - 1)) / QUAD)
    need = jnp.where(iota((wide, 1), 0) < keys, jnp.maximum(need, least), 0.0)
    spread = jnp.broadcast_to(need, (wide, wide)).T
    before = iota((wide, wide), 1) < iota((wide, wide), 0)
    offset = jnp.sum(jnp.where(before, spread, 0.0), axis=1, keepdims=True)
    end = jnp.sum(spread[:1, :], axis=1, keepdims=True)
    pos = jnp.sum(hit * (QUAD * offset + within + 1.0), axis=0, keepdims=True) - 1.0
    high = jnp.floor(pos / 128.0)
    place = jnp.where(column(pos - 128.0 * high) == iota((total, 128), 1), 1.0, 0.0).astype(BF16)
    line = jnp.where(iota((8, total), 0) == high, 1.0, 0.0)
    terms = [line] + [line * row for row, _ in values]
    found = jnp.dot(
        jnp.concatenate(terms, axis=0).astype(BF16), place, preferred_element_type=F32
    )
    code = jnp.zeros((8, 128), F32)
    for i, (_, scale) in enumerate(values):
        code = code + scale * found[8 * (i + 1) : 8 * (i + 2), :]
    code = jnp.where(found[:8, :] > 0.0, code, pad)
    q = iota((wide, quads), 1)
    inside = (offset <= q) & (q < offset + need)
    info = 2.0 * iota((wide, quads), 0) + jnp.where(offset == q, 1.0, 0.0)
    quad = jnp.sum(jnp.where(inside, info, 0.0), axis=0, keepdims=True)
    quad = jnp.where(q[:1, :] < end, quad, 2.0 * keys + 1.0)
    return code.astype(jnp.int32), quad.astype(jnp.int32), offset, need, end


def back_quads(total, wanted):
    return up((total + wanted * (QUAD - 1)) // QUAD, 128)


def rest_quads_of(blocks, per):
    return up(blocks * (-(-per // QUAD)), 128)


def early_blocks(blocks):
    return blocks * EARLY // 32


def own_quads(total, blocks):
    return up((total + blocks * (QUAD - 1)) // QUAD, STEP)


def code_base(total):
    return 1 << (total - 1).bit_length()


def split(value, base):
    return lax.shift_right_logical(value, base.bit_length() - 1), value & (base - 1)


def entry(code, step, i):
    line = 128 // (STEP * QUAD)
    first = lax.shift_right_logical(step, line.bit_length() - 1)
    return code[first, (step & (line - 1)) * (STEP * QUAD) + i]


def greet(groups, members):
    me_g, me_m = lax.axis_index("group"), lax.axis_index("member")
    barrier = pltpu.get_barrier_semaphore()
    peers = [(me_g, partner(me_m, o, members)) for o in range(1, members)]
    peers += [(lax.rem(me_g + o, groups), me_m) for o in range(1, groups)]
    for peer in peers:
        pl.semaphore_signal(barrier, inc=1, device_id=peer, device_id_type=MESH)
    return lambda: pl.semaphore_wait(barrier, len(peers))


def partner(me, o, members):
    if members & (members - 1):
        return lax.rem(me + o, members)
    bit = 1
    while bit <= o:
        if o & bit:
            me = me + bit - 2 * bit * lax.rem(lax.div(me, bit), 2)
        bit *= 2
    return me


def sender(me, o, members):
    if members & (members - 1):
        return lax.rem(me + members - o, members)
    return partner(me, o, members)


def push(src, dst, send, recv, o, device):
    copy = pltpu.make_async_remote_copy(
        src_ref=src,
        dst_ref=dst,
        send_sem=send.at[o],
        recv_sem=recv.at[o],
        device_id=device,
        device_id_type=MESH,
    )
    copy.start()
    return copy


def pick_rows(row, table, chunk):
    count = row.shape[1]
    blocks, tile, width = table.shape
    half = blocks // 2
    ids_column = jnp.broadcast_to(row, (8, count)).T[:, :1]
    second = ids_column >= half * tile
    ids_column = jnp.where(second, ids_column - half * tile, ids_column)
    total = jnp.zeros((count, 2 * width), F32)
    depth = chunk * tile
    for c in range(0, half, chunk):
        ids = lax.broadcasted_iota(jnp.int32, (count, depth), 1) + c * tile
        hot = jnp.where(ids == ids_column, 1.0, 0.0).astype(BF16)
        both = [table[a : a + chunk].reshape(depth, width) for a in (c, half + c)]
        total = total + jnp.dot(
            hot, jnp.concatenate(both, axis=1), preferred_element_type=F32
        )
    return jnp.where(second, total[:, width:], total[:, :width])


def gather_kernel(
    groups,
    members,
    blocks,
    feats_in,
    hist_in,
    tiles_in,
    cot_in,
    rows_in,
    picks_in,
    stale_rows_in,
    src_in,
    tiles,
    srcs,
    cot,
    part,
    wanted,
    code_out,
    quad_out,
    rest_code_out,
    rest_quad_out,
    marks_out,
    spots_out,
    code,
    quad,
    rest_code,
    rest_quad,
    marks,
    spots_vec,
    rows,
    picks,
    stale_rows,
    src,
    src_vec,
    asked,
    own,
    hist,
    leaving,
    l_sems,
    t_sems,
    p_send,
    p_recv,
    d_send,
    d_recv,
    r_send,
    r_recv,
    s_send,
    s_recv,
):
    me_g, me_m = lax.axis_index("group"), lax.axis_index("member")
    taken = picks.shape[0]
    tile, width = srcs.shape[1], srcs.shape[2]
    offered = rows.shape[1] // tile
    each = stale_rows.shape[1] // tile
    per = src.shape[0]
    total = blocks * per
    pair = 1 if members & (members - 1) else 2

    load_feats = pltpu.make_async_copy(feats_in, own.at[pl.ds(0, blocks)], l_sems.at[0])
    keep_feats = pltpu.make_async_copy(feats_in, srcs.at[pl.ds(0, blocks)], l_sems.at[8])
    load_hist = pltpu.make_async_copy(hist_in, hist, l_sems.at[1])
    load_cot = pltpu.make_async_copy(cot_in, cot, l_sems.at[2])

    def chunk(b):
        at = pl.ds(b * per, per)
        return pltpu.make_async_copy(tiles_in.at[at], tiles.at[at], t_sems.at[b])

    small = [
        pltpu.make_async_copy(a, b, l_sems.at[3 + i])
        for i, (a, b) in enumerate(
            (
                (rows_in, rows),
                (picks_in, picks),
                (stale_rows_in, stale_rows),
                (src_in, src),
                (src_in, src_vec),
            )
        )
    ]
    load_feats.start()
    for copy in small:
        copy.start()
    load_hist.start()
    entered = greet(groups, members)
    for copy in small:
        copy.wait()
    for p in range(members):
        for k in range(taken):
            asked[p, k] = jnp.broadcast_to(picks[k : k + 1, p : p + 1], asked.shape[2:])
    wanted[me_m] = asked[me_m]
    own[blocks] = jnp.zeros((tile, width), BF16)
    srcs[blocks] = jnp.zeros((tile, width), BF16)
    load_feats.wait()

    @pl.loop(0, blocks)
    def _(b):
        chunk(b).start()

    load_cot.start()
    keep_feats.start()
    bounds = blocks + 1
    stales = bounds + members * offered
    mine = pl.ds(bounds + me_m * offered, offered)
    srcs[mine] = pick_rows(rows[...], own.at[pl.ds(0, blocks)], 4).astype(BF16).reshape(
        offered, tile, width
    )
    entered()
    direct, copies = [], []
    for o in range(1, members):
        if o % pair == 0:
            peer = partner(me_m, o, members)
            direct.append((o, push(srcs.at[mine], srcs.at[mine], d_send, d_recv, o, (me_g, peer))))
    if pair == 2:
        mate = partner(me_m, 1, members)
        copies.append(push(srcs.at[mine], srcs.at[mine], d_send, d_recv, 1, (me_g, mate)))
    load_hist.wait()
    for o in range(groups - 1, -1, -1):
        to = lax.rem(me_g + o, groups)
        found = pick_rows(stale_rows[pl.ds(to, 1), :], hist, 4)
        found = found.astype(BF16).reshape(each, tile, width)
        at = pl.ds(stales + me_g * each, each)
        if o == 0:
            srcs[at] = found
        else:
            leaving[o] = found
            copies.append(push(leaving.at[o], srcs.at[at], s_send, s_recv, o, (to, me_m)))
    for o in range(1, members):
        peer = partner(me_m, o, members)
        copies.append(push(asked.at[peer], wanted.at[me_m], p_send, p_recv, o, (me_g, peer)))

    def forward(b):
        chunk(b).wait()
        lhs = jnp.concatenate([tiles[b * per + t] for t in range(per)], axis=1)
        rhs = jnp.concatenate([own[jnp.minimum(src[t, b], blocks)] for t in range(per)], axis=0)
        part[b] = jnp.dot(lhs, rhs, preferred_element_type=F32)

    early = early_blocks(blocks)
    pl.loop(0, early, unroll=4)(forward)
    for o, copy in direct:
        copy.wait_recv()
        if pair == 2:
            at = pl.ds(bounds + sender(me_m, o, members) * offered, offered)
            copies.append(push(srcs.at[at], srcs.at[at], r_send, r_recv, o, (me_g, mate)))

    one = (per, total)
    owner = jnp.floor((iota(one, 1) + 0.5) / per)
    rank = iota(one, 1) - per * owner
    place = jnp.where(iota((blocks, total), 0) == owner[:1, :], 1.0, 0.0).astype(BF16)
    spread = jnp.dot(src_vec[...].astype(F32).astype(BF16), place, preferred_element_type=F32)
    row = jnp.sum(jnp.where(iota(one, 0) == rank, spread, 0.0), axis=0, keepdims=True)
    owner = owner[:1, :]
    base = code_base(total)
    inner = blocks + members * taken
    wide = up(inner + 1, 128)
    hit = jnp.where((iota((wide, total), 0) == row) & (row < inner), 1.0, 0.0)
    rank = rank[:1, :]
    numbers = [(owner, float(per)), (rank, 1.0)]
    code[...], quad[...], offset, need, end = arrange(
        hit,
        [(owner, float(base))] + numbers,
        inner,
        0.0,
        quad.shape[1],
        float(base * blocks),
    )

    def place_of(s):
        halo = s - blocks
        spot = jnp.where(halo < 0.0, s, s - inner + stales)
        for p in range(members):
            for k in range(taken):
                pick = picks[k : k + 1, p : p + 1].astype(F32)
                spot = jnp.where(halo == p * taken + k, bounds + p * offered + pick, spot)
        return spot

    spots_vec[...] = place_of(src_vec[...].astype(F32)).astype(jnp.int32)
    spot = place_of(row)
    remains = (row >= blocks) & (owner < early)
    hit = jnp.where((iota((128, total), 0) == owner) & remains, 1.0, 0.0)
    rest_code[...], rest_quad[...], _, _, rest_end = arrange(
        hit,
        [(spot, float(base))] + numbers,
        early,
        1.0,
        rest_quad.shape[1],
        float(base * blocks),
    )
    last = jnp.where(need > 0.0, offset + need - 1.0, float(own_quads(total, blocks)))
    last = jnp.broadcast_to(last, (wide, wide)).T[:8, :]
    first = jnp.sum(jnp.where(iota((wide, 1), 0) == blocks, offset, 0.0), axis=0, keepdims=True)
    which = iota((8, wide), 0)
    found = jnp.where(which == 1, jnp.floor(first / STEP), last)
    found = jnp.where(which == 2, jnp.floor((end + (STEP - 1)) / STEP), found)
    found = jnp.where(which == 3, jnp.floor((rest_end + (STEP - 1)) / STEP), found)
    marks[...] = found.astype(jnp.int32)

    outs = [
        pltpu.make_async_copy(a, b, l_sems.at[9 + i])
        for i, (a, b) in enumerate(
            (
                (code, code_out),
                (quad, quad_out),
                (rest_code, rest_code_out),
                (rest_quad, rest_quad_out),
                (marks, marks_out),
                (spots_vec, spots_out),
            )
        )
    ]
    for copy in outs:
        copy.start()

    @pl.loop(early, blocks)
    def _(b):
        chunk(b).wait()

    for copy in outs:
        copy.wait()
    load_cot.wait()
    keep_feats.wait()
    for _, copy in direct:
        copy.wait_send()
    for copy in copies:
        copy.wait()


def vmem_out(shape, dtype):
    return pltpu.VMEM(shape, dtype)


def hold(space, *arrays):
    return [pltpu.with_memory_space_constraint(a, space) for a in arrays]


def gather(features, history, tiles, cotangent, boundary_rows, picks, stale_rows, src, sizes):
    groups, members = sizes
    per, blocks = src.shape
    taken = picks.shape[0]
    tile, width = tiles.shape[1], features.shape[1]
    offered = boundary_rows.shape[1] // tile
    each = stale_rows.shape[1] // tile
    total = blocks * per
    inner = blocks + members * taken
    lists = (
        (8, 128),
        (1, back_quads(total, inner)),
        (8, 128),
        (1, rest_quads_of(blocks, per)),
        (8, up(inner + 1, 128)),
        src.shape,
    )
    held = blocks + 1 + members * offered + groups * each
    vmem = pl.BlockSpec(memory_space=pltpu.VMEM)
    dma = pltpu.SemaphoreType.DMA
    return pl.pallas_call(
        functools.partial(gather_kernel, groups, members, blocks),
        out_shape=(
            vmem_out(tiles.shape, BF16),
            vmem_out((held, tile, width), BF16),
            vmem_out((blocks * tile, width), BF16),
            vmem_out((early_blocks(blocks), tile, width), F32),
            vmem_out((members, taken, 8, 128), jnp.int32),
            *[pltpu.SMEM(shape, jnp.int32) for shape in lists],
        ),
        in_specs=[pl.BlockSpec(memory_space=pltpu.HBM)] * 8,
        out_specs=[vmem] * 5 + [pl.BlockSpec(memory_space=pltpu.SMEM)] * 6,
        scratch_shapes=[
            *[pltpu.VMEM(shape, jnp.int32) for shape in lists],
            pltpu.VMEM(boundary_rows.shape, jnp.int32),
            pltpu.VMEM(picks.shape, jnp.int32),
            pltpu.VMEM(stale_rows.shape, jnp.int32),
            pltpu.SMEM(src.shape, jnp.int32),
            pltpu.VMEM(src.shape, jnp.int32),
            pltpu.VMEM((members, taken, 8, 128), jnp.int32),
            pltpu.VMEM((blocks + 1, tile, width), BF16),
            pltpu.VMEM((blocks, tile, width), BF16),
            pltpu.VMEM((groups, each, tile, width), BF16),
            dma((15,)),
            dma((blocks,)),
            dma((members,)),
            dma((members,)),
            dma((members,)),
            dma((members,)),
            dma((members,)),
            dma((members,)),
            dma((groups,)),
            dma((groups,)),
        ],
        compiler_params=pltpu.CompilerParams(
            collective_id=0, has_side_effects=True, vmem_limit_bytes=16 << 20
        ),
    )(
        *hold(
            pltpu.HBM,
            features.reshape(blocks, tile, width),
            history.reshape(blocks, tile, width),
            tiles,
            cotangent,
            boundary_rows,
            picks,
            stale_rows,
            src,
        )
    )


def middle_kernel(
    code,
    quad,
    rest_code,
    rest_quad,
    marks,
    spots,
    tiles,
    srcs,
    cot,
    part,
    deg,
    w_self,
    w_neigh,
    out,
    back,
    dpre_out,
    halo_grad,
    weights,
    total,
    out_buf,
    grad,
    gt,
    inverse,
    sems,
):
    early, tile, width = part.shape
    blocks = deg.shape[0]
    per = spots.shape[0]
    base = code_base(tiles.shape[0])
    n_halo = halo_grad.shape[0]

    back[blocks] = jnp.zeros((width, tile), BF16)
    grad[blocks : blocks + n_halo] = jnp.zeros((n_halo, width, tile), F32)
    gt[...] = jnp.zeros_like(gt)
    inverse[...] = 1.0 / deg[...].astype(F32)

    def rest(step, acc):
        terms = []
        for u in range(STEP):
            lhs, rhs = [], []
            for i in range(QUAD):
                e, t = split(entry(rest_code, step, u * QUAD + i), base)
                lhs.append(tiles[t])
                rhs.append(srcs[e])
            terms.append(
                jnp.dot(
                    jnp.concatenate(lhs, axis=1),
                    jnp.concatenate(rhs, axis=0),
                    preferred_element_type=F32,
                )
            )
        for u in range(STEP):
            info = rest_quad[0, step * STEP + u]
            b = info // 2
            start = part[jnp.minimum(b, early - 1)]
            acc = terms[u] + jnp.where(info % 2 == 1, start, acc)
            total[b] = acc
        return acc

    lax.fori_loop(0, marks[3, 0], rest, jnp.zeros((tile, width), F32))

    def forward(b):
        lhs = jnp.concatenate([tiles[b * per + t] for t in range(per)], axis=1)
        rhs = jnp.concatenate([srcs[spots[t, b]] for t in range(per)], axis=0)
        total[b] = jnp.dot(lhs, rhs, preferred_element_type=F32)

    pl.loop(early, blocks, unroll=4)(forward)

    group = 8
    rows = group * tile
    w_cat = jnp.concatenate([w_self[...], w_neigh[...]], axis=0)

    def store(c):
        at = pl.ds(pl.multiple_of(c * rows, rows), rows)
        return pltpu.make_async_copy(out_buf.at[at], out.at[at], sems.at[c])

    def middle(c):
        at = pl.ds(pl.multiple_of(c * rows, rows), rows)
        agg = []
        for i in range(group):
            b = c * group + i
            d = jnp.broadcast_to(inverse[pl.ds(b, 1), :], (tile, tile)).T
            agg.append((total[b] * d).astype(BF16))
        own = srcs[pl.ds(c * group, group)].reshape(rows, width)
        fa = jnp.concatenate([own, jnp.concatenate(agg, axis=0)], axis=1)
        pre = jnp.dot(fa, w_cat, preferred_element_type=F32)
        scale = lax.rsqrt(jnp.mean(pre * pre, axis=-1, keepdims=True) + 1e-05)
        out_buf[at, :] = (pre * scale).astype(BF16)
        store(c).start()
        g = cot[at, :].astype(F32)
        m = jnp.mean(g * pre, axis=-1, keepdims=True)
        dpre = (scale * g - pre * (scale**3 * m)).astype(BF16)
        dpre_out[at, :] = dpre
        gt[...] += lax.dot_general(dpre, fa, (((0,), (0,)), ((), ())), preferred_element_type=F32)
        bt = lax.dot_general(
            w_neigh[...], dpre, (((1,), (1,)), ((), ())), preferred_element_type=F32
        )
        for i in range(group):
            d = inverse[pl.ds(c * group + i, 1), :]
            back[c * group + i] = (bt[:, i * tile : (i + 1) * tile] * d).astype(BF16)

    pl.loop(0, blocks // group)(middle)

    weights[:width, :] = gt[:, :width].T.astype(weights.dtype)
    weights[width:, :] = gt[:, width:].T.astype(weights.dtype)

    def backward(step, acc):
        terms = quad_terms(step, code, back, tiles, base)
        for u in range(STEP):
            info = quad[0, step * STEP + u]
            acc = terms[u] + jnp.where(info % 2 == 1, 0.0, acc)
            grad[info // 2] = acc
        return acc

    lax.fori_loop(marks[1, 0], marks[2, 0], backward, jnp.zeros((width, tile), F32))
    for h in range(n_halo):
        halo_grad[h] = grad[blocks + h].T.astype(BF16)

    @pl.loop(0, blocks // group)
    def _(c):
        store(c).wait()


def quad_terms(step, code, back, tiles, base):
    terms = []
    for u in range(STEP):
        lhs, rhs = [], []
        for i in range(QUAD):
            b, t = split(entry(code, step, u * QUAD + i), base)
            lhs.append(back[b])
            rhs.append(tiles[t])
        terms.append(
            jnp.dot(
                jnp.concatenate(lhs, axis=1),
                jnp.concatenate(rhs, axis=0),
                preferred_element_type=F32,
            )
        )
    return terms


def middle(plans, tiles, srcs, cot, part, degree, w_self, w_neigh, n_halo, wire):
    tile, width = part.shape[1:]
    nodes = degree.shape[0]
    blocks = nodes // tile
    smem = pl.BlockSpec(memory_space=pltpu.SMEM)
    vmem = pl.BlockSpec(memory_space=pltpu.VMEM)
    return pl.pallas_call(
        middle_kernel,
        out_shape=(
            jax.ShapeDtypeStruct((nodes, width), BF16),
            vmem_out((blocks + 1, width, tile), BF16),
            vmem_out((nodes, width), BF16),
            vmem_out((n_halo, tile, width), BF16),
            vmem_out((2 * width, width), wire),
        ),
        in_specs=[smem] * 6 + [vmem] * 7,
        out_specs=[pl.BlockSpec(memory_space=pl.ANY)] + [vmem] * 4,
        scratch_shapes=[
            pltpu.VMEM((blocks + 1, tile, width), F32),
            pltpu.VMEM((nodes, width), BF16),
            pltpu.VMEM((blocks + n_halo + 1, width, tile), F32),
            pltpu.VMEM((width, 2 * width), F32),
            pltpu.VMEM((blocks, tile), F32),
            pltpu.SemaphoreType.DMA((blocks,)),
        ],
        compiler_params=pltpu.CompilerParams(vmem_limit_bytes=20 << 20),
    )(
        *hold(pltpu.SMEM, *plans),
        *hold(pltpu.VMEM, tiles, srcs, cot, part),
        degree.reshape(blocks, tile),
        w_self,
        w_neigh,
    )


def combine_kernel(
    groups,
    members,
    factor,
    code,
    quad,
    marks,
    tiles,
    back,
    dpre,
    halo_grad,
    weights,
    wanted,
    rows,
    w_self,
    grad_features,
    grad_self,
    grad_neigh,
    accs,
    returned,
    landed,
    partial,
    across,
    share,
    whole,
    h_send,
    h_recv,
    a_send,
    a_recv,
    b_send,
    b_recv,
    c_send,
    c_recv,
):
    me_g, me_m = lax.axis_index("group"), lax.axis_index("member")
    taken = wanted.shape[1]
    blocks, (width, tile) = back.shape[0] - 1, back.shape[1:]
    offered = rows.shape[1] // tile
    piece = landed.shape[1]
    base = code_base(tiles.shape[0])
    steps = (accs.shape[0] - 1) // STEP

    def backward(step, acc):
        terms = quad_terms(step, code, back, tiles, base)
        for u in range(STEP):
            q = step * STEP + u
            acc = terms[u] + jnp.where(quad[0, q] % 2 == 1, 0.0, acc)
            accs[q] = acc
        return acc

    entered = greet(groups, members)
    accs[accs.shape[0] - 1] = jnp.zeros((width, tile), F32)
    cuts = [steps * c // 10 for c in CUTS] + [steps]
    acc = lax.fori_loop(cuts[0], cuts[1], backward, jnp.zeros((width, tile), F32))
    entered()
    copies, first, second, third = [], [], [], []
    for o in range(1, members):
        peer = partner(me_m, o, members)
        at = pl.ds(pl.multiple_of(peer * piece, piece), piece)
        first.append(push(weights.at[at], landed.at[me_m], a_send, a_recv, o, (me_g, peer)))
    for o in range(1, members):
        peer = partner(me_m, o, members)
        copies.append(
            push(
                halo_grad.at[pl.ds(peer * taken, taken)],
                returned.at[me_m],
                h_send,
                h_recv,
                o,
                (me_g, peer),
            )
        )
    mine = pl.ds(pl.multiple_of(me_m * piece, piece), piece)
    landed[me_m] = weights[mine, :]
    returned[me_m] = halo_grad[pl.ds(me_m * taken, taken)]
    acc = lax.fori_loop(cuts[1], cuts[2], backward, acc)
    for copy in first:
        copy.wait_recv()
    total = landed[0].astype(F32)
    for p in range(1, members):
        total = total + landed[p].astype(F32)
    partial[...] = total.astype(partial.dtype)
    across[me_g] = total.astype(partial.dtype)
    for o in range(1, groups):
        to = lax.rem(me_g + o, groups)
        second.append(push(partial, across.at[me_g], b_send, b_recv, o, (to, me_m)))
    acc = lax.fori_loop(cuts[2], cuts[3], backward, acc)
    for copy in second:
        copy.wait_recv()
    total = across[0].astype(F32)
    for g in range(1, groups):
        total = total + across[g].astype(F32)
    share[...] = total.astype(share.dtype)
    whole[mine, :] = total.astype(share.dtype)
    for o in range(1, members):
        peer = partner(me_m, o, members)
        third.append(push(share, whole.at[mine], c_send, c_recv, o, (me_g, peer)))
    acc = lax.fori_loop(cuts[3], cuts[4], backward, acc)

    for copy in copies:
        copy.wait_recv()
    halves = []
    for j in range(offered):
        total = jnp.zeros((tile, width), F32)
        for p in range(members):
            for k in range(taken):
                w = jnp.broadcast_to(wanted[p, k][:1, :], (tile, width))
                total = total + jnp.where(w == j, returned[p, k].astype(F32), 0.0)
        high = total.astype(BF16)
        low = (total - high.astype(F32)).astype(BF16)
        halves.append(jnp.concatenate([high, low], axis=1))
    extra = jnp.concatenate(halves, axis=0)
    group = 4
    depth = group * tile

    def add(c):
        at = pl.ds(pl.multiple_of(c * depth, depth), depth)
        ids = lax.broadcasted_iota(jnp.int32, (depth, rows.shape[1]), 0) + c * depth
        hot = jnp.where(ids == rows[...], 1.0, 0.0).astype(BF16)
        more = jnp.dot(hot, extra, preferred_element_type=F32)
        own = lax.dot_general(
            dpre[at, :], w_self[...], (((1,), (1,)), ((), ())), preferred_element_type=F32
        )
        near = [accs[marks[0, c * group + i]].T for i in range(group)]
        own = own + jnp.concatenate(near, axis=0)
        grad_features[at, :] = (own + (more[:, :width] + more[:, width:])).astype(BF16)

    pl.loop(0, blocks // group)(add)
    for copy in third:
        copy.wait_recv()
    grad_self[...] = whole[:width, :].astype(F32) * factor
    grad_neigh[...] = whole[width:, :].astype(F32) * factor
    for copy in first + second + third + copies:
        copy.wait_send()


def combine(plans, tiles, back, dpre, halo_grad, weights, wanted, boundary_rows, w_self, sizes):
    groups, members = sizes
    nodes, width = dpre.shape
    tile = halo_grad.shape[1]
    blocks = nodes // tile
    taken = wanted.shape[1]
    piece = weights.shape[0] // members
    factor = 1.0 / math.sqrt(nodes * members * groups)
    smem = pl.BlockSpec(memory_space=pltpu.SMEM)
    vmem = pl.BlockSpec(memory_space=pltpu.VMEM)
    dma = pltpu.SemaphoreType.DMA
    return pl.pallas_call(
        functools.partial(combine_kernel, groups, members, factor),
        out_shape=(
            vmem_out((nodes, width), BF16),
            vmem_out((width, width), F32),
            vmem_out((width, width), F32),
        ),
        in_specs=[smem] * 3 + [vmem] * 8,
        out_specs=[vmem] * 3,
        scratch_shapes=[
            pltpu.VMEM((own_quads(tiles.shape[0], blocks) + 1, width, tile), F32),
            pltpu.VMEM((members, taken, tile, width), BF16),
            pltpu.VMEM((members, piece, width), weights.dtype),
            pltpu.VMEM((piece, width), weights.dtype),
            pltpu.VMEM((groups, piece, width), weights.dtype),
            pltpu.VMEM((piece, width), weights.dtype),
            pltpu.VMEM(weights.shape, weights.dtype),
            dma((members,)),
            dma((members,)),
            dma((members,)),
            dma((members,)),
            dma((groups,)),
            dma((groups,)),
            dma((members,)),
            dma((members,)),
        ],
        compiler_params=pltpu.CompilerParams(
            collective_id=1, has_side_effects=True, vmem_limit_bytes=24 << 20
        ),
    )(
        *hold(pltpu.SMEM, *plans),
        *hold(pltpu.VMEM, tiles, back, dpre, halo_grad, weights, wanted),
        boundary_rows,
        w_self,
    )


def write_kernel(a, b, c, out_a, out_b, out_c, sems):
    pairs = (a, out_a), (b, out_b), (c, out_c)
    copies = [pltpu.make_async_copy(x, y, sems.at[i]) for i, (x, y) in enumerate(pairs)]
    for copy in copies:
        copy.start()
    for copy in copies:
        copy.wait()


def write(*arrays):
    return pl.pallas_call(
        write_kernel,
        out_shape=[jax.ShapeDtypeStruct(a.shape, a.dtype) for a in arrays],
        in_specs=[pl.BlockSpec(memory_space=pltpu.VMEM)] * 3,
        out_specs=[pl.BlockSpec(memory_space=pltpu.HBM)] * 3,
        scratch_shapes=[pltpu.SemaphoreType.DMA((3,))],
        compiler_params=pltpu.CompilerParams(vmem_limit_bytes=4 << 20),
    )(*hold(pltpu.VMEM, *arrays))


def on_device(
    features,
    history,
    tiles,
    tile_src,
    degree,
    boundary_rows,
    picks,
    stale_rows,
    w_self,
    w_neigh,
    cotangent,
):
    sizes = lax.axis_size("group"), lax.axis_size("member")
    tiles, srcs, cot, part, wanted, code, quad, rest_code, rest_quad, marks, spots = gather(
        features,
        history,
        tiles,
        cotangent,
        boundary_rows,
        picks.T,
        stale_rows,
        tile_src.T,
        sizes,
    )
    n_halo = sizes[1] * picks.shape[1]
    wire = F32 if (2 * w_self.shape[0] // sizes[1]) % 16 else BF16
    layer_out, back, dpre, halo_grad, weights = middle(
        (code, quad, rest_code, rest_quad, marks, spots),
        tiles,
        srcs,
        cot,
        part,
        degree,
        w_self,
        w_neigh,
        n_halo,
        wire,
    )
    grad_features, grad_self, grad_neigh = combine(
        (code, quad, marks),
        tiles,
        back,
        dpre,
        halo_grad,
        weights,
        wanted,
        boundary_rows,
        w_self,
        sizes,
    )
    return layer_out, *write(grad_features, grad_self, grad_neigh)


def solution(mesh):
    nodes = P(("group", "member"), None)
    placed = (
        nodes,
        nodes,
        P(("group", "member"), None, None),
        nodes,
        P(("group", "member")),
        nodes,
        nodes,
        nodes,
        P(),
        P(),
        nodes,
    )
    return jax.shard_map(
        on_device,
        mesh=mesh,
        in_specs=placed,
        out_specs=(nodes, nodes, P(), P()),
        check_vma=False,
    )
```

```python
import functools
import math

import jax
import jax.numpy as jnp
from jax import lax
from jax.experimental import pallas as pl
from jax.experimental.pallas import tpu as pltpu
from jax.sharding import PartitionSpec as P

QUAD = 4
STEP = 8
EARLY = 8
CUTS = 0, 2, 6, 9
F32 = jnp.float32
BF16 = jnp.bfloat16
MESH = pl.DeviceIdType.MESH


def up(value, unit):
    return -(-value // unit) * unit


def iota(shape, axis):
    return lax.broadcasted_iota(jnp.int32, shape, axis).astype(F32)


def column(value):
    return jnp.broadcast_to(value, (8, value.shape[1])).T[:, :1]


def arrange(hit, values, keys, least, quads, pad, fence):
    wide, total = hit.shape
    low = hit.astype(BF16)
    earlier = jnp.where(iota((128, 128), 0) < iota((128, 128), 1), 1.0, 0.0).astype(BF16)
    count = jnp.zeros((wide, 1), F32)
    within = []
    for c in range(0, total, 128):
        part = low[:, c : c + 128]
        within.append(jnp.dot(part, earlier, preferred_element_type=F32) + count)
        count = count + jnp.sum(hit[:, c : c + 128], axis=1, keepdims=True)
    within = jnp.concatenate(within, axis=1)
    need = jnp.floor((count + (QUAD - 1)) / QUAD)
    need = jnp.where(iota((wide, 1), 0) < keys, jnp.maximum(need, least), 0.0)
    spread = jnp.broadcast_to(need, (wide, wide)).T
    before = iota((wide, wide), 1) < iota((wide, wide), 0)
    offset = jnp.sum(jnp.where(before, spread, 0.0), axis=1, keepdims=True)
    at_fence = iota((wide, 1), 0)
    first = jnp.sum(jnp.where(at_fence == fence, offset, 0.0), axis=0, keepdims=True)
    shift = STEP * jnp.floor((first + (STEP - 1)) / STEP) - first
    offset = offset + jnp.where(at_fence >= fence, shift, 0.0)
    end = jnp.sum(spread[:1, :], axis=1, keepdims=True) + shift
    pos = jnp.sum(hit * (QUAD * offset + within + 1.0), axis=0, keepdims=True) - 1.0
    high = jnp.floor(pos / 128.0)
    place = jnp.where(column(pos - 128.0 * high) == iota((total, 128), 1), 1.0, 0.0).astype(BF16)
    line = jnp.where(iota((8, total), 0) == high, 1.0, 0.0)
    terms = [line] + [line * row for row, _ in values]
    found = jnp.dot(
        jnp.concatenate(terms, axis=0).astype(BF16), place, preferred_element_type=F32
    )
    code = jnp.zeros((8, 128), F32)
    for i, (_, scale) in enumerate(values):
        code = code + scale * found[8 * (i + 1) : 8 * (i + 2), :]
    code = jnp.where(found[:8, :] > 0.0, code, pad)
    q = iota((wide, quads), 1)
    inside = (offset <= q) & (q < offset + need)
    info = 2.0 * iota((wide, quads), 0) + jnp.where(offset == q, 1.0, 0.0)
    quad = jnp.sum(jnp.where(inside, info + 1.0, 0.0), axis=0, keepdims=True)
    quad = jnp.where(quad > 0.0, quad - 1.0, 2.0 * keys + 1.0)
    return code.astype(jnp.int32), quad.astype(jnp.int32), offset, need, end


def back_quads(total, wanted):
    return up((total + wanted * (QUAD - 1)) // QUAD, 128)


def rest_quads_of(blocks, per):
    return up(blocks * (-(-per // QUAD)), 128)


def early_blocks(blocks):
    return blocks * EARLY // 32


def own_quads(total, blocks):
    return up((total + blocks * (QUAD - 1)) // QUAD, STEP)


def code_base(total):
    return 1 << (total - 1).bit_length()


def split(value, base):
    return lax.shift_right_logical(value, base.bit_length() - 1), value & (base - 1)


def entry(code, step, i):
    line = 128 // (STEP * QUAD)
    first = lax.shift_right_logical(step, line.bit_length() - 1)
    return code[first, (step & (line - 1)) * (STEP * QUAD) + i]


def greet(groups, members):
    me_g, me_m = lax.axis_index("group"), lax.axis_index("member")
    barrier = pltpu.get_barrier_semaphore()
    peers = [(me_g, partner(me_m, o, members)) for o in range(1, members)]
    peers += [(lax.rem(me_g + o, groups), me_m) for o in range(1, groups)]
    for peer in peers:
        pl.semaphore_signal(barrier, inc=1, device_id=peer, device_id_type=MESH)
    return lambda: pl.semaphore_wait(barrier, len(peers))


def partner(me, o, members):
    if members & (members - 1):
        return lax.rem(me + o, members)
    bit = 1
    while bit <= o:
        if o & bit:
            me = me + bit - 2 * bit * lax.rem(lax.div(me, bit), 2)
        bit *= 2
    return me


def sender(me, o, members):
    if members & (members - 1):
        return lax.rem(me + members - o, members)
    return partner(me, o, members)


def push(src, dst, send, recv, o, device):
    copy = pltpu.make_async_remote_copy(
        src_ref=src,
        dst_ref=dst,
        send_sem=send.at[o],
        recv_sem=recv.at[o],
        device_id=device,
        device_id_type=MESH,
    )
    copy.start()
    return copy


def pick_rows(row, table, chunk):
    count = row.shape[1]
    blocks, tile, width = table.shape
    half = blocks // 2
    ids_column = jnp.broadcast_to(row, (8, count)).T[:, :1]
    second = ids_column >= half * tile
    ids_column = jnp.where(second, ids_column - half * tile, ids_column)
    total = jnp.zeros((count, 2 * width), F32)
    depth = chunk * tile
    for c in range(0, half, chunk):
        ids = lax.broadcasted_iota(jnp.int32, (count, depth), 1) + c * tile
        hot = jnp.where(ids == ids_column, 1.0, 0.0).astype(BF16)
        both = [table[a : a + chunk].reshape(depth, width) for a in (c, half + c)]
        total = total + jnp.dot(
            hot, jnp.concatenate(both, axis=1), preferred_element_type=F32
        )
    return jnp.where(second, total[:, width:], total[:, :width])


def gather_kernel(
    groups,
    members,
    blocks,
    feats_in,
    hist_in,
    tiles_in,
    cot_in,
    rows_in,
    picks_in,
    stale_rows_in,
    src_in,
    tiles,
    srcs,
    cot,
    part,
    wanted,
    code_out,
    quad_out,
    rest_code_out,
    rest_quad_out,
    marks_out,
    spots_out,
    code,
    quad,
    rest_code,
    rest_quad,
    marks,
    spots_vec,
    rows,
    picks,
    stale_rows,
    src,
    src_vec,
    asked,
    own,
    hist,
    leaving,
    l_sems,
    t_sems,
    p_send,
    p_recv,
    d_send,
    d_recv,
    r_send,
    r_recv,
    s_send,
    s_recv,
):
    me_g, me_m = lax.axis_index("group"), lax.axis_index("member")
    taken = picks.shape[0]
    tile, width = srcs.shape[1], srcs.shape[2]
    offered = rows.shape[1] // tile
    each = stale_rows.shape[1] // tile
    per = src.shape[0]
    total = blocks * per
    pair = 1 if members & (members - 1) else 2

    load_feats = pltpu.make_async_copy(feats_in, own.at[pl.ds(0, blocks)], l_sems.at[0])
    keep_feats = pltpu.make_async_copy(feats_in, srcs.at[pl.ds(0, blocks)], l_sems.at[8])
    load_hist = pltpu.make_async_copy(hist_in, hist, l_sems.at[1])
    load_cot = pltpu.make_async_copy(cot_in, cot, l_sems.at[2])

    def chunk(b):
        at = pl.ds(b * per, per)
        return pltpu.make_async_copy(tiles_in.at[at], tiles.at[at], t_sems.at[b])

    small = [
        pltpu.make_async_copy(a, b, l_sems.at[3 + i])
        for i, (a, b) in enumerate(
            (
                (rows_in, rows),
                (picks_in, picks),
                (stale_rows_in, stale_rows),
                (src_in, src),
                (src_in, src_vec),
            )
        )
    ]
    load_feats.start()
    for copy in small:
        copy.start()
    load_hist.start()
    entered = greet(groups, members)
    for copy in small:
        copy.wait()
    for p in range(members):
        for k in range(taken):
            asked[p, k] = jnp.broadcast_to(picks[k : k + 1, p : p + 1], asked.shape[2:])
    wanted[me_m] = asked[me_m]
    own[blocks] = jnp.zeros((tile, width), BF16)
    srcs[blocks] = jnp.zeros((tile, width), BF16)
    load_feats.wait()

    @pl.loop(0, blocks)
    def _(b):
        chunk(b).start()

    load_cot.start()
    keep_feats.start()
    bounds = blocks + 1
    stales = bounds + members * offered
    mine = pl.ds(bounds + me_m * offered, offered)
    srcs[mine] = pick_rows(rows[...], own.at[pl.ds(0, blocks)], 4).astype(BF16).reshape(
        offered, tile, width
    )
    entered()
    direct, copies = [], []
    for o in range(1, members):
        if o % pair == 0:
            peer = partner(me_m, o, members)
            direct.append((o, push(srcs.at[mine], srcs.at[mine], d_send, d_recv, o, (me_g, peer))))
    if pair == 2:
        mate = partner(me_m, 1, members)
        copies.append(push(srcs.at[mine], srcs.at[mine], d_send, d_recv, 1, (me_g, mate)))
    load_hist.wait()
    for o in range(groups - 1, -1, -1):
        to = lax.rem(me_g + o, groups)
        found = pick_rows(stale_rows[pl.ds(to, 1), :], hist, 4)
        found = found.astype(BF16).reshape(each, tile, width)
        at = pl.ds(stales + me_g * each, each)
        if o == 0:
            srcs[at] = found
        else:
            leaving[o] = found
            copies.append(push(leaving.at[o], srcs.at[at], s_send, s_recv, o, (to, me_m)))
    for o in range(1, members):
        peer = partner(me_m, o, members)
        copies.append(push(asked.at[peer], wanted.at[me_m], p_send, p_recv, o, (me_g, peer)))

    def forward(b):
        chunk(b).wait()
        lhs = jnp.concatenate([tiles[b * per + t] for t in range(per)], axis=1)
        rhs = jnp.concatenate([own[jnp.minimum(src[t, b], blocks)] for t in range(per)], axis=0)
        part[b] = jnp.dot(lhs, rhs, preferred_element_type=F32)

    early = early_blocks(blocks)
    pl.loop(0, early, unroll=4)(forward)
    one = (per, total)
    owner = jnp.floor((iota(one, 1) + 0.5) / per)
    rank = iota(one, 1) - per * owner
    place = jnp.where(iota((blocks, total), 0) == owner[:1, :], 1.0, 0.0).astype(BF16)
    spread = jnp.dot(src_vec[...].astype(F32).astype(BF16), place, preferred_element_type=F32)
    row = jnp.sum(jnp.where(iota(one, 0) == rank, spread, 0.0), axis=0, keepdims=True)
    owner = owner[:1, :]
    base = code_base(total)
    inner = blocks + members * taken
    wide = up(inner + 1, 128)
    hit = jnp.where((iota((wide, total), 0) == row) & (row < inner), 1.0, 0.0)
    rank = rank[:1, :]
    numbers = [(owner, float(per)), (rank, 1.0)]
    code[...], quad[...], offset, need, end = arrange(
        hit,
        [(owner, float(base))] + numbers,
        inner,
        0.0,
        quad.shape[1],
        float(base * blocks),
        blocks,
    )

    def place_of(s):
        halo = s - blocks
        spot = jnp.where(halo < 0.0, s, s - inner + stales)
        for p in range(members):
            for k in range(taken):
                pick = picks[k : k + 1, p : p + 1].astype(F32)
                spot = jnp.where(halo == p * taken + k, bounds + p * offered + pick, spot)
        return spot

    spots_vec[...] = place_of(src_vec[...].astype(F32)).astype(jnp.int32)
    spot = place_of(row)
    remains = (row >= blocks) & (owner < early)
    hit = jnp.where((iota((128, total), 0) == owner) & remains, 1.0, 0.0)
    rest_code[...], rest_quad[...], _, _, rest_end = arrange(
        hit,
        [(spot, float(base))] + numbers,
        early,
        1.0,
        rest_quad.shape[1],
        float(base * blocks),
        blocks,
    )
    last = jnp.where(need > 0.0, offset + need - 1.0, float(own_quads(total, blocks)))
    last = jnp.broadcast_to(last, (wide, wide)).T[:8, :]
    first = jnp.sum(jnp.where(iota((wide, 1), 0) == blocks, offset, 0.0), axis=0, keepdims=True)
    which = iota((8, wide), 0)
    found = jnp.where(which == 1, jnp.floor(first / STEP), last)
    found = jnp.where(which == 2, jnp.floor((end + (STEP - 1)) / STEP), found)
    found = jnp.where(which == 3, jnp.floor((rest_end + (STEP - 1)) / STEP), found)
    marks[...] = found.astype(jnp.int32)

    outs = [
        pltpu.make_async_copy(a, b, l_sems.at[9 + i])
        for i, (a, b) in enumerate(
            (
                (code, code_out),
                (quad, quad_out),
                (rest_code, rest_code_out),
                (rest_quad, rest_quad_out),
                (marks, marks_out),
                (spots_vec, spots_out),
            )
        )
    ]
    for copy in outs:
        copy.start()

    for o, copy in direct:
        copy.wait_recv()
        if pair == 2:
            at = pl.ds(bounds + sender(me_m, o, members) * offered, offered)
            copies.append(push(srcs.at[at], srcs.at[at], r_send, r_recv, o, (me_g, mate)))

    @pl.loop(early, blocks)
    def _(b):
        chunk(b).wait()

    for copy in outs:
        copy.wait()
    load_cot.wait()
    keep_feats.wait()
    for _, copy in direct:
        copy.wait_send()
    for copy in copies:
        copy.wait()


def vmem_out(shape, dtype):
    return pltpu.VMEM(shape, dtype)


def hold(space, *arrays):
    return [pltpu.with_memory_space_constraint(a, space) for a in arrays]


def gather(features, history, tiles, cotangent, boundary_rows, picks, stale_rows, src, sizes):
    groups, members = sizes
    per, blocks = src.shape
    taken = picks.shape[0]
    tile, width = tiles.shape[1], features.shape[1]
    offered = boundary_rows.shape[1] // tile
    each = stale_rows.shape[1] // tile
    total = blocks * per
    inner = blocks + members * taken
    lists = (
        (8, 128),
        (1, back_quads(total, inner)),
        (8, 128),
        (1, rest_quads_of(blocks, per)),
        (8, up(inner + 1, 128)),
        src.shape,
    )
    held = blocks + 1 + members * offered + groups * each
    vmem = pl.BlockSpec(memory_space=pltpu.VMEM)
    dma = pltpu.SemaphoreType.DMA
    return pl.pallas_call(
        functools.partial(gather_kernel, groups, members, blocks),
        out_shape=(
            vmem_out(tiles.shape, BF16),
            vmem_out((held, tile, width), BF16),
            vmem_out((blocks * tile, width), BF16),
            vmem_out((early_blocks(blocks), tile, width), F32),
            vmem_out((members, taken, 8, 128), jnp.int32),
            *[pltpu.SMEM(shape, jnp.int32) for shape in lists],
        ),
        in_specs=[pl.BlockSpec(memory_space=pltpu.HBM)] * 8,
        out_specs=[vmem] * 5 + [pl.BlockSpec(memory_space=pltpu.SMEM)] * 6,
        scratch_shapes=[
            *[pltpu.VMEM(shape, jnp.int32) for shape in lists],
            pltpu.VMEM(boundary_rows.shape, jnp.int32),
            pltpu.VMEM(picks.shape, jnp.int32),
            pltpu.VMEM(stale_rows.shape, jnp.int32),
            pltpu.SMEM(src.shape, jnp.int32),
            pltpu.VMEM(src.shape, jnp.int32),
            pltpu.VMEM((members, taken, 8, 128), jnp.int32),
            pltpu.VMEM((blocks + 1, tile, width), BF16),
            pltpu.VMEM((blocks, tile, width), BF16),
            pltpu.VMEM((groups, each, tile, width), BF16),
            dma((15,)),
            dma((blocks,)),
            dma((members,)),
            dma((members,)),
            dma((members,)),
            dma((members,)),
            dma((members,)),
            dma((members,)),
            dma((groups,)),
            dma((groups,)),
        ],
        compiler_params=pltpu.CompilerParams(
            collective_id=0, has_side_effects=True, vmem_limit_bytes=16 << 20
        ),
    )(
        *hold(
            pltpu.HBM,
            features.reshape(blocks, tile, width),
            history.reshape(blocks, tile, width),
            tiles,
            cotangent,
            boundary_rows,
            picks,
            stale_rows,
            src,
        )
    )


def middle_kernel(
    code,
    quad,
    rest_code,
    rest_quad,
    marks,
    spots,
    tiles,
    srcs,
    cot,
    part,
    deg,
    w_self,
    w_neigh,
    out,
    back,
    dpre_out,
    halo_grad,
    weights,
    total,
    out_buf,
    grad,
    gt,
    inverse,
    sems,
):
    early, tile, width = part.shape
    blocks = deg.shape[0]
    per = spots.shape[0]
    base = code_base(tiles.shape[0])
    n_halo = halo_grad.shape[0]

    back[blocks] = jnp.zeros((width, tile), BF16)
    grad[blocks : blocks + n_halo] = jnp.zeros((n_halo, width, tile), F32)
    gt[...] = jnp.zeros_like(gt)
    inverse[...] = 1.0 / deg[...].astype(F32)

    def rest(step, acc):
        terms = []
        for u in range(STEP):
            lhs, rhs = [], []
            for i in range(QUAD):
                e, t = split(entry(rest_code, step, u * QUAD + i), base)
                lhs.append(tiles[t])
                rhs.append(srcs[e])
            terms.append(
                jnp.dot(
                    jnp.concatenate(lhs, axis=1),
                    jnp.concatenate(rhs, axis=0),
                    preferred_element_type=F32,
                )
            )
        for u in range(STEP):
            info = rest_quad[0, step * STEP + u]
            b = info // 2
            start = part[jnp.minimum(b, early - 1)]
            acc = terms[u] + jnp.where(info % 2 == 1, start, acc)
            total[b] = acc
        return acc

    lax.fori_loop(0, marks[3, 0], rest, jnp.zeros((tile, width), F32))

    def forward(b):
        lhs = jnp.concatenate([tiles[b * per + t] for t in range(per)], axis=1)
        rhs = jnp.concatenate([srcs[spots[t, b]] for t in range(per)], axis=0)
        total[b] = jnp.dot(lhs, rhs, preferred_element_type=F32)

    pl.loop(early, blocks, unroll=8)(forward)

    group = 16
    rows = group * tile
    w_cat = jnp.concatenate([w_self[...], w_neigh[...]], axis=0)

    def store(c):
        at = pl.ds(pl.multiple_of(c * rows, rows), rows)
        return pltpu.make_async_copy(out_buf.at[at], out.at[at], sems.at[c])

    def middle(c):
        at = pl.ds(pl.multiple_of(c * rows, rows), rows)
        agg = []
        for i in range(group):
            b = c * group + i
            d = jnp.broadcast_to(inverse[pl.ds(b, 1), :], (tile, tile)).T
            agg.append((total[b] * d).astype(BF16))
        own = srcs[pl.ds(c * group, group)].reshape(rows, width)
        fa = jnp.concatenate([own, jnp.concatenate(agg, axis=0)], axis=1)
        pre = jnp.dot(fa, w_cat, preferred_element_type=F32)
        scale = lax.rsqrt(jnp.mean(pre * pre, axis=-1, keepdims=True) + 1e-05)
        out_buf[at, :] = (pre * scale).astype(BF16)
        store(c).start()
        g = cot[at, :].astype(F32)
        m = jnp.mean(g * pre, axis=-1, keepdims=True)
        dpre = (scale * g - pre * (scale**3 * m)).astype(BF16)
        dpre_out[at, :] = dpre
        dpre_t = dpre.T
        gt[...] += jnp.dot(dpre_t, fa, preferred_element_type=F32)
        bt = jnp.dot(w_neigh[...], dpre_t, preferred_element_type=F32)
        for i in range(group):
            d = inverse[pl.ds(c * group + i, 1), :]
            back[c * group + i] = (bt[:, i * tile : (i + 1) * tile] * d).astype(BF16)

    pl.loop(0, blocks // group)(middle)

    weights[:width, :] = gt[:, :width].T.astype(weights.dtype)
    weights[width:, :] = gt[:, width:].T.astype(weights.dtype)

    def backward(step, acc):
        terms = quad_terms(step, code, back, tiles, base)
        for u in range(STEP):
            info = quad[0, step * STEP + u]
            acc = terms[u] + jnp.where(info % 2 == 1, 0.0, acc)
            grad[info // 2] = acc
        return acc

    lax.fori_loop(marks[1, 0], marks[2, 0], backward, jnp.zeros((width, tile), F32))
    for h in range(n_halo):
        halo_grad[h] = grad[blocks + h].T.astype(BF16)

    @pl.loop(0, blocks // group)
    def _(c):
        store(c).wait()


def quad_terms(step, code, back, tiles, base):
    terms = []
    for u in range(STEP):
        lhs, rhs = [], []
        for i in range(QUAD):
            b, t = split(entry(code, step, u * QUAD + i), base)
            lhs.append(back[b])
            rhs.append(tiles[t])
        terms.append(
            jnp.dot(
                jnp.concatenate(lhs, axis=1),
                jnp.concatenate(rhs, axis=0),
                preferred_element_type=F32,
            )
        )
    return terms


def middle(plans, tiles, srcs, cot, part, degree, w_self, w_neigh, n_halo, wire):
    tile, width = part.shape[1:]
    nodes = degree.shape[0]
    blocks = nodes // tile
    smem = pl.BlockSpec(memory_space=pltpu.SMEM)
    vmem = pl.BlockSpec(memory_space=pltpu.VMEM)
    return pl.pallas_call(
        middle_kernel,
        out_shape=(
            jax.ShapeDtypeStruct((nodes, width), BF16),
            vmem_out((blocks + 1, width, tile), BF16),
            vmem_out((nodes, width), BF16),
            vmem_out((n_halo, tile, width), BF16),
            vmem_out((2 * width, width), wire),
        ),
        in_specs=[smem] * 6 + [vmem] * 7,
        out_specs=[pl.BlockSpec(memory_space=pl.ANY)] + [vmem] * 4,
        scratch_shapes=[
            pltpu.VMEM((blocks + 1, tile, width), F32),
            pltpu.VMEM((nodes, width), BF16),
            pltpu.VMEM((blocks + n_halo + 1, width, tile), F32),
            pltpu.VMEM((width, 2 * width), F32),
            pltpu.VMEM((blocks, tile), F32),
            pltpu.SemaphoreType.DMA((blocks,)),
        ],
        compiler_params=pltpu.CompilerParams(vmem_limit_bytes=20 << 20),
    )(
        *hold(pltpu.SMEM, *plans),
        *hold(pltpu.VMEM, tiles, srcs, cot, part),
        degree.reshape(blocks, tile),
        w_self,
        w_neigh,
    )


def combine_kernel(
    groups,
    members,
    factor,
    code,
    quad,
    marks,
    tiles,
    back,
    dpre,
    halo_grad,
    weights,
    wanted,
    rows,
    w_self,
    grad_features,
    grad_self,
    grad_neigh,
    accs,
    returned,
    landed,
    partial,
    across,
    share,
    whole,
    h_send,
    h_recv,
    a_send,
    a_recv,
    b_send,
    b_recv,
    c_send,
    c_recv,
):
    me_g, me_m = lax.axis_index("group"), lax.axis_index("member")
    taken = wanted.shape[1]
    blocks, (width, tile) = back.shape[0] - 1, back.shape[1:]
    offered = rows.shape[1] // tile
    piece = landed.shape[1]
    base = code_base(tiles.shape[0])
    steps = (accs.shape[0] - 1) // STEP

    def backward(step, acc):
        terms = quad_terms(step, code, back, tiles, base)
        for u in range(STEP):
            q = step * STEP + u
            acc = terms[u] + jnp.where(quad[0, q] % 2 == 1, 0.0, acc)
            accs[q] = acc
        return acc

    entered = greet(groups, members)
    accs[accs.shape[0] - 1] = jnp.zeros((width, tile), F32)
    cuts = [steps * c // 10 for c in CUTS] + [steps]
    acc = lax.fori_loop(cuts[0], cuts[1], backward, jnp.zeros((width, tile), F32))
    entered()
    copies, first, second, third = [], [], [], []
    for o in range(1, members):
        peer = partner(me_m, o, members)
        at = pl.ds(pl.multiple_of(peer * piece, piece), piece)
        first.append(push(weights.at[at], landed.at[me_m], a_send, a_recv, o, (me_g, peer)))
    for o in range(1, members):
        peer = partner(me_m, o, members)
        copies.append(
            push(
                halo_grad.at[pl.ds(peer * taken, taken)],
                returned.at[me_m],
                h_send,
                h_recv,
                o,
                (me_g, peer),
            )
        )
    mine = pl.ds(pl.multiple_of(me_m * piece, piece), piece)
    landed[me_m] = weights[mine, :]
    returned[me_m] = halo_grad[pl.ds(me_m * taken, taken)]
    acc = lax.fori_loop(cuts[1], cuts[2], backward, acc)
    for copy in first:
        copy.wait_recv()
    total = landed[0].astype(F32)
    for p in range(1, members):
        total = total + landed[p].astype(F32)
    partial[...] = total.astype(partial.dtype)
    across[me_g] = total.astype(partial.dtype)
    for o in range(1, groups):
        to = lax.rem(me_g + o, groups)
        second.append(push(partial, across.at[me_g], b_send, b_recv, o, (to, me_m)))
    acc = lax.fori_loop(cuts[2], cuts[3], backward, acc)
    for copy in second:
        copy.wait_recv()
    total = across[0].astype(F32)
    for g in range(1, groups):
        total = total + across[g].astype(F32)
    share[...] = total.astype(share.dtype)
    whole[mine, :] = total.astype(share.dtype)
    for o in range(1, members):
        peer = partner(me_m, o, members)
        third.append(push(share, whole.at[mine], c_send, c_recv, o, (me_g, peer)))
    acc = lax.fori_loop(cuts[3], cuts[4], backward, acc)

    for copy in copies:
        copy.wait_recv()
    halves = []
    for j in range(offered):
        total = jnp.zeros((tile, width), F32)
        for p in range(members):
            for k in range(taken):
                w = jnp.broadcast_to(wanted[p, k][:1, :], (tile, width))
                total = total + jnp.where(w == j, returned[p, k].astype(F32), 0.0)
        high = total.astype(BF16)
        low = (total - high.astype(F32)).astype(BF16)
        halves.append(jnp.concatenate([high, low], axis=1))
    extra = jnp.concatenate(halves, axis=0)
    group = 4
    depth = group * tile

    def add(c):
        at = pl.ds(pl.multiple_of(c * depth, depth), depth)
        ids = lax.broadcasted_iota(jnp.int32, (depth, rows.shape[1]), 0) + c * depth
        hot = jnp.where(ids == rows[...], 1.0, 0.0).astype(BF16)
        more = jnp.dot(hot, extra, preferred_element_type=F32)
        own = lax.dot_general(
            dpre[at, :], w_self[...], (((1,), (1,)), ((), ())), preferred_element_type=F32
        )
        near = [accs[marks[0, c * group + i]].T for i in range(group)]
        own = own + jnp.concatenate(near, axis=0)
        grad_features[at, :] = (own + (more[:, :width] + more[:, width:])).astype(BF16)

    pl.loop(0, blocks // group)(add)
    for copy in third:
        copy.wait_recv()
    grad_self[...] = whole[:width, :].astype(F32) * factor
    grad_neigh[...] = whole[width:, :].astype(F32) * factor
    for copy in first + second + third + copies:
        copy.wait_send()


def combine(plans, tiles, back, dpre, halo_grad, weights, wanted, boundary_rows, w_self, sizes):
    groups, members = sizes
    nodes, width = dpre.shape
    tile = halo_grad.shape[1]
    blocks = nodes // tile
    taken = wanted.shape[1]
    piece = weights.shape[0] // members
    factor = 1.0 / math.sqrt(nodes * members * groups)
    smem = pl.BlockSpec(memory_space=pltpu.SMEM)
    vmem = pl.BlockSpec(memory_space=pltpu.VMEM)
    dma = pltpu.SemaphoreType.DMA
    return pl.pallas_call(
        functools.partial(combine_kernel, groups, members, factor),
        out_shape=(
            vmem_out((nodes, width), BF16),
            vmem_out((width, width), F32),
            vmem_out((width, width), F32),
        ),
        in_specs=[smem] * 3 + [vmem] * 8,
        out_specs=[vmem] * 3,
        scratch_shapes=[
            pltpu.VMEM((own_quads(tiles.shape[0], blocks) + 1, width, tile), F32),
            pltpu.VMEM((members, taken, tile, width), BF16),
            pltpu.VMEM((members, piece, width), weights.dtype),
            pltpu.VMEM((piece, width), weights.dtype),
            pltpu.VMEM((groups, piece, width), weights.dtype),
            pltpu.VMEM((piece, width), weights.dtype),
            pltpu.VMEM(weights.shape, weights.dtype),
            dma((members,)),
            dma((members,)),
            dma((members,)),
            dma((members,)),
            dma((groups,)),
            dma((groups,)),
            dma((members,)),
            dma((members,)),
        ],
        compiler_params=pltpu.CompilerParams(
            collective_id=1, has_side_effects=True, vmem_limit_bytes=24 << 20
        ),
    )(
        *hold(pltpu.SMEM, *plans),
        *hold(pltpu.VMEM, tiles, back, dpre, halo_grad, weights, wanted),
        boundary_rows,
        w_self,
    )


def write_kernel(a, b, c, out_a, out_b, out_c, sems):
    pairs = (a, out_a), (b, out_b), (c, out_c)
    copies = [pltpu.make_async_copy(x, y, sems.at[i]) for i, (x, y) in enumerate(pairs)]
    for copy in copies:
        copy.start()
    for copy in copies:
        copy.wait()


def write(*arrays):
    return pl.pallas_call(
        write_kernel,
        out_shape=[jax.ShapeDtypeStruct(a.shape, a.dtype) for a in arrays],
        in_specs=[pl.BlockSpec(memory_space=pltpu.VMEM)] * 3,
        out_specs=[pl.BlockSpec(memory_space=pltpu.HBM)] * 3,
        scratch_shapes=[pltpu.SemaphoreType.DMA((3,))],
        compiler_params=pltpu.CompilerParams(vmem_limit_bytes=4 << 20),
    )(*hold(pltpu.VMEM, *arrays))


def on_device(
    features,
    history,
    tiles,
    tile_src,
    degree,
    boundary_rows,
    picks,
    stale_rows,
    w_self,
    w_neigh,
    cotangent,
):
    sizes = lax.axis_size("group"), lax.axis_size("member")
    tiles, srcs, cot, part, wanted, code, quad, rest_code, rest_quad, marks, spots = gather(
        features,
        history,
        tiles,
        cotangent,
        boundary_rows,
        picks.T,
        stale_rows,
        tile_src.T,
        sizes,
    )
    n_halo = sizes[1] * picks.shape[1]
    wire = F32 if (2 * w_self.shape[0] // sizes[1]) % 16 else BF16
    layer_out, back, dpre, halo_grad, weights = middle(
        (code, quad, rest_code, rest_quad, marks, spots),
        tiles,
        srcs,
        cot,
        part,
        degree,
        w_self,
        w_neigh,
        n_halo,
        wire,
    )
    grad_features, grad_self, grad_neigh = combine(
        (code, quad, marks),
        tiles,
        back,
        dpre,
        halo_grad,
        weights,
        wanted,
        boundary_rows,
        w_self,
        sizes,
    )
    return layer_out, *write(grad_features, grad_self, grad_neigh)


def solution(mesh):
    nodes = P(("group", "member"), None)
    placed = (
        nodes,
        nodes,
        P(("group", "member"), None, None),
        nodes,
        P(("group", "member")),
        nodes,
        nodes,
        nodes,
        P(),
        P(),
        nodes,
    )
    return jax.shard_map(
        on_device,
        mesh=mesh,
        in_specs=placed,
        out_specs=(nodes, nodes, P(), P()),
        check_vma=False,
    )
```

```python
import functools
import math

import jax
import jax.numpy as jnp
from jax import lax
from jax.experimental import pallas as pl
from jax.experimental.pallas import tpu as pltpu
from jax.sharding import PartitionSpec as P

QUAD = 4
STEP = 8
EARLY = 8
CUTS = 0, 2, 6, 9
F32 = jnp.float32
BF16 = jnp.bfloat16
MESH = pl.DeviceIdType.MESH


def up(value, unit):
    return -(-value // unit) * unit


def iota(shape, axis):
    return lax.broadcasted_iota(jnp.int32, shape, axis).astype(F32)


def column(value):
    return jnp.broadcast_to(value, (8, value.shape[1])).T[:, :1]


def arrange(hit, values, keys, least, quads, pad, fence):
    wide, total = hit.shape
    low = hit.astype(BF16)
    earlier = jnp.where(iota((128, 128), 0) < iota((128, 128), 1), 1.0, 0.0).astype(BF16)
    count = jnp.zeros((wide, 1), F32)
    within = []
    for c in range(0, total, 128):
        part = low[:, c : c + 128]
        within.append(jnp.dot(part, earlier, preferred_element_type=F32) + count)
        count = count + jnp.sum(hit[:, c : c + 128], axis=1, keepdims=True)
    within = jnp.concatenate(within, axis=1)
    need = jnp.floor((count + (QUAD - 1)) / QUAD)
    need = jnp.where(iota((wide, 1), 0) < keys, jnp.maximum(need, least), 0.0)
    spread = jnp.broadcast_to(need, (wide, wide)).T
    before = iota((wide, wide), 1) < iota((wide, wide), 0)
    offset = jnp.sum(jnp.where(before, spread, 0.0), axis=1, keepdims=True)
    at_fence = iota((wide, 1), 0)
    first = jnp.sum(jnp.where(at_fence == fence, offset, 0.0), axis=0, keepdims=True)
    shift = STEP * jnp.floor((first + (STEP - 1)) / STEP) - first
    offset = offset + jnp.where(at_fence >= fence, shift, 0.0)
    end = jnp.sum(spread[:1, :], axis=1, keepdims=True) + shift
    pos = jnp.sum(hit * (QUAD * offset + within + 1.0), axis=0, keepdims=True) - 1.0
    high = jnp.floor(pos / 128.0)
    place = jnp.where(column(pos - 128.0 * high) == iota((total, 128), 1), 1.0, 0.0).astype(BF16)
    line = jnp.where(iota((8, total), 0) == high, 1.0, 0.0)
    terms = [line] + [line * row for row, _ in values]
    found = jnp.dot(
        jnp.concatenate(terms, axis=0).astype(BF16), place, preferred_element_type=F32
    )
    code = jnp.zeros((8, 128), F32)
    for i, (_, scale) in enumerate(values):
        code = code + scale * found[8 * (i + 1) : 8 * (i + 2), :]
    code = jnp.where(found[:8, :] > 0.0, code, pad)
    q = iota((wide, quads), 1)
    inside = (offset <= q) & (q < offset + need)
    info = 2.0 * iota((wide, quads), 0) + jnp.where(offset == q, 1.0, 0.0)
    quad = jnp.sum(jnp.where(inside, info + 1.0, 0.0), axis=0, keepdims=True)
    quad = jnp.where(quad > 0.0, quad - 1.0, 2.0 * keys + 1.0)
    return code.astype(jnp.int32), quad.astype(jnp.int32), offset, need, end


def back_quads(total, wanted):
    return up((total + wanted * (QUAD - 1)) // QUAD, 128)


def rest_quads_of(blocks, per):
    return up(blocks * (-(-per // QUAD)), 128)


def early_blocks(blocks):
    return blocks * EARLY // 32


def own_quads(total, blocks):
    return up((total + blocks * (QUAD - 1)) // QUAD, STEP)


def code_base(total):
    return 1 << (total - 1).bit_length()


def split(value, base):
    return lax.shift_right_logical(value, base.bit_length() - 1), value & (base - 1)


def entry(code, step, i):
    line = 128 // (STEP * QUAD)
    first = lax.shift_right_logical(step, line.bit_length() - 1)
    return code[first, (step & (line - 1)) * (STEP * QUAD) + i]


def greet(groups, members):
    me_g, me_m = lax.axis_index("group"), lax.axis_index("member")
    barrier = pltpu.get_barrier_semaphore()
    peers = [(me_g, partner(me_m, o, members)) for o in range(1, members)]
    peers += [(lax.rem(me_g + o, groups), me_m) for o in range(1, groups)]
    for peer in peers:
        pl.semaphore_signal(barrier, inc=1, device_id=peer, device_id_type=MESH)
    return lambda: pl.semaphore_wait(barrier, len(peers))


def partner(me, o, members):
    if members & (members - 1):
        return lax.rem(me + o, members)
    bit = 1
    while bit <= o:
        if o & bit:
            me = me + bit - 2 * bit * lax.rem(lax.div(me, bit), 2)
        bit *= 2
    return me


def sender(me, o, members):
    if members & (members - 1):
        return lax.rem(me + members - o, members)
    return partner(me, o, members)


def push(src, dst, send, recv, o, device):
    copy = pltpu.make_async_remote_copy(
        src_ref=src,
        dst_ref=dst,
        send_sem=send.at[o],
        recv_sem=recv.at[o],
        device_id=device,
        device_id_type=MESH,
    )
    copy.start()
    return copy


def pick_rows(row, table, chunk):
    count = row.shape[1]
    blocks, tile, width = table.shape
    half = blocks // 2
    ids_column = jnp.broadcast_to(row, (8, count)).T[:, :1]
    second = ids_column >= half * tile
    ids_column = jnp.where(second, ids_column - half * tile, ids_column)
    total = jnp.zeros((count, 2 * width), F32)
    depth = chunk * tile
    for c in range(0, half, chunk):
        ids = lax.broadcasted_iota(jnp.int32, (count, depth), 1) + c * tile
        hot = jnp.where(ids == ids_column, 1.0, 0.0).astype(BF16)
        both = [table[a : a + chunk].reshape(depth, width) for a in (c, half + c)]
        total = total + jnp.dot(
            hot, jnp.concatenate(both, axis=1), preferred_element_type=F32
        )
    return jnp.where(second, total[:, width:], total[:, :width])


def gather_kernel(
    groups,
    members,
    blocks,
    feats_in,
    hist_in,
    tiles_in,
    cot_in,
    rows_in,
    picks_in,
    stale_rows_in,
    src_in,
    tiles,
    srcs,
    cot,
    part,
    wanted,
    code_out,
    quad_out,
    rest_code_out,
    rest_quad_out,
    marks_out,
    spots_out,
    code,
    quad,
    rest_code,
    rest_quad,
    marks,
    spots_vec,
    rows,
    picks,
    stale_rows,
    src,
    src_vec,
    asked,
    own,
    hist,
    leaving,
    l_sems,
    t_sems,
    p_send,
    p_recv,
    d_send,
    d_recv,
    r_send,
    r_recv,
    s_send,
    s_recv,
):
    me_g, me_m = lax.axis_index("group"), lax.axis_index("member")
    taken = picks.shape[0]
    tile, width = srcs.shape[1], srcs.shape[2]
    offered = rows.shape[1] // tile
    each = stale_rows.shape[1] // tile
    per = src.shape[0]
    total = blocks * per
    pair = 1 if members & (members - 1) else 2

    load_feats = pltpu.make_async_copy(feats_in, own.at[pl.ds(0, blocks)], l_sems.at[0])
    keep_feats = pltpu.make_async_copy(feats_in, srcs.at[pl.ds(0, blocks)], l_sems.at[8])
    load_hist = pltpu.make_async_copy(hist_in, hist, l_sems.at[1])
    load_cot = pltpu.make_async_copy(cot_in, cot, l_sems.at[2])

    def chunk(b):
        at = pl.ds(b * per, per)
        return pltpu.make_async_copy(tiles_in.at[at], tiles.at[at], t_sems.at[b])

    small = [
        pltpu.make_async_copy(a, b, l_sems.at[3 + i])
        for i, (a, b) in enumerate(
            (
                (rows_in, rows),
                (picks_in, picks),
                (stale_rows_in, stale_rows),
                (src_in, src),
                (src_in, src_vec),
            )
        )
    ]
    load_feats.start()
    for copy in small:
        copy.start()
    load_hist.start()
    entered = greet(groups, members)
    for copy in small:
        copy.wait()
    for p in range(members):
        for k in range(taken):
            asked[p, k] = jnp.broadcast_to(picks[k : k + 1, p : p + 1], asked.shape[2:])
    wanted[me_m] = asked[me_m]
    own[blocks] = jnp.zeros((tile, width), BF16)
    srcs[blocks] = jnp.zeros((tile, width), BF16)
    load_feats.wait()

    @pl.loop(0, blocks)
    def _(b):
        chunk(b).start()

    load_cot.start()
    keep_feats.start()
    bounds = blocks + 1
    stales = bounds + members * offered
    mine = pl.ds(bounds + me_m * offered, offered)
    srcs[mine] = pick_rows(rows[...], own.at[pl.ds(0, blocks)], 4).astype(BF16).reshape(
        offered, tile, width
    )
    entered()
    direct, copies = [], []
    for o in range(1, members):
        if o % pair == 0:
            peer = partner(me_m, o, members)
            direct.append((o, push(srcs.at[mine], srcs.at[mine], d_send, d_recv, o, (me_g, peer))))
    if pair == 2:
        mate = partner(me_m, 1, members)
        copies.append(push(srcs.at[mine], srcs.at[mine], d_send, d_recv, 1, (me_g, mate)))
    load_hist.wait()
    for o in range(groups - 1, -1, -1):
        to = lax.rem(me_g + o, groups)
        found = pick_rows(stale_rows[pl.ds(to, 1), :], hist, 4)
        found = found.astype(BF16).reshape(each, tile, width)
        at = pl.ds(stales + me_g * each, each)
        if o == 0:
            srcs[at] = found
        else:
            leaving[o] = found
            copies.append(push(leaving.at[o], srcs.at[at], s_send, s_recv, o, (to, me_m)))
    for o in range(1, members):
        peer = partner(me_m, o, members)
        copies.append(push(asked.at[peer], wanted.at[me_m], p_send, p_recv, o, (me_g, peer)))

    def forward(b):
        chunk(b).wait()
        lhs = jnp.concatenate([tiles[b * per + t] for t in range(per)], axis=1)
        rhs = jnp.concatenate([own[jnp.minimum(src[t, b], blocks)] for t in range(per)], axis=0)
        part[b] = jnp.dot(lhs, rhs, preferred_element_type=F32)

    early = early_blocks(blocks)
    pl.loop(0, early, unroll=4)(forward)
    one = (per, total)
    owner = jnp.floor((iota(one, 1) + 0.5) / per)
    rank = iota(one, 1) - per * owner
    place = jnp.where(iota((blocks, total), 0) == owner[:1, :], 1.0, 0.0).astype(BF16)
    spread = jnp.dot(src_vec[...].astype(F32).astype(BF16), place, preferred_element_type=F32)
    row = jnp.sum(jnp.where(iota(one, 0) == rank, spread, 0.0), axis=0, keepdims=True)
    owner = owner[:1, :]
    base = code_base(total)
    inner = blocks + members * taken
    wide = up(inner + 1, 128)
    hit = jnp.where((iota((wide, total), 0) == row) & (row < inner), 1.0, 0.0)
    rank = rank[:1, :]
    numbers = [(owner, float(per)), (rank, 1.0)]
    code[...], quad[...], offset, need, end = arrange(
        hit,
        [(owner, float(base))] + numbers,
        inner,
        0.0,
        quad.shape[1],
        float(base * blocks),
        blocks,
    )

    def place_of(s):
        halo = s - blocks
        spot = jnp.where(halo < 0.0, s, s - inner + stales)
        for p in range(members):
            for k in range(taken):
                pick = picks[k : k + 1, p : p + 1].astype(F32)
                spot = jnp.where(halo == p * taken + k, bounds + p * offered + pick, spot)
        return spot

    spots_vec[...] = place_of(src_vec[...].astype(F32)).astype(jnp.int32)
    spot = place_of(row)
    remains = (row >= blocks) & (owner < early)
    hit = jnp.where((iota((128, total), 0) == owner) & remains, 1.0, 0.0)
    rest_code[...], rest_quad[...], _, _, rest_end = arrange(
        hit,
        [(spot, float(base))] + numbers,
        early,
        1.0,
        rest_quad.shape[1],
        float(base * blocks),
        blocks,
    )
    last = jnp.where(need > 0.0, offset + need - 1.0, float(own_quads(total, blocks)))
    last = jnp.broadcast_to(last, (wide, wide)).T[:8, :]
    first = jnp.sum(jnp.where(iota((wide, 1), 0) == blocks, offset, 0.0), axis=0, keepdims=True)
    which = iota((8, wide), 0)
    found = jnp.where(which == 1, jnp.floor(first / STEP), last)
    found = jnp.where(which == 2, jnp.floor((end + (STEP - 1)) / STEP), found)
    found = jnp.where(which == 3, jnp.floor((rest_end + (STEP - 1)) / STEP), found)
    marks[...] = found.astype(jnp.int32)

    outs = [
        pltpu.make_async_copy(a, b, l_sems.at[9 + i])
        for i, (a, b) in enumerate(
            (
                (code, code_out),
                (quad, quad_out),
                (rest_code, rest_code_out),
                (rest_quad, rest_quad_out),
                (marks, marks_out),
                (spots_vec, spots_out),
            )
        )
    ]
    for copy in outs:
        copy.start()

    for o, copy in direct:
        copy.wait_recv()
        if pair == 2:
            at = pl.ds(bounds + sender(me_m, o, members) * offered, offered)
            copies.append(push(srcs.at[at], srcs.at[at], r_send, r_recv, o, (me_g, mate)))

    @pl.loop(early, blocks)
    def _(b):
        chunk(b).wait()

    for copy in outs:
        copy.wait()
    load_cot.wait()
    keep_feats.wait()
    for _, copy in direct:
        copy.wait_send()
    for copy in copies:
        copy.wait()


def vmem_out(shape, dtype):
    return pltpu.VMEM(shape, dtype)


def hold(space, *arrays):
    return [pltpu.with_memory_space_constraint(a, space) for a in arrays]


def gather(features, history, tiles, cotangent, boundary_rows, picks, stale_rows, src, sizes):
    groups, members = sizes
    per, blocks = src.shape
    taken = picks.shape[0]
    tile, width = tiles.shape[1], features.shape[1]
    offered = boundary_rows.shape[1] // tile
    each = stale_rows.shape[1] // tile
    total = blocks * per
    inner = blocks + members * taken
    lists = (
        (8, 128),
        (1, back_quads(total, inner)),
        (8, 128),
        (1, rest_quads_of(blocks, per)),
        (8, up(inner + 1, 128)),
        src.shape,
    )
    held = blocks + 1 + members * offered + groups * each
    vmem = pl.BlockSpec(memory_space=pltpu.VMEM)
    dma = pltpu.SemaphoreType.DMA
    return pl.pallas_call(
        functools.partial(gather_kernel, groups, members, blocks),
        out_shape=(
            vmem_out(tiles.shape, BF16),
            vmem_out((held, tile, width), BF16),
            vmem_out((blocks * tile, width), BF16),
            vmem_out((early_blocks(blocks), tile, width), F32),
            vmem_out((members, taken, 8, 128), jnp.int32),
            *[pltpu.SMEM(shape, jnp.int32) for shape in lists],
        ),
        in_specs=[pl.BlockSpec(memory_space=pltpu.HBM)] * 8,
        out_specs=[vmem] * 5 + [pl.BlockSpec(memory_space=pltpu.SMEM)] * 6,
        scratch_shapes=[
            *[pltpu.VMEM(shape, jnp.int32) for shape in lists],
            pltpu.VMEM(boundary_rows.shape, jnp.int32),
            pltpu.VMEM(picks.shape, jnp.int32),
            pltpu.VMEM(stale_rows.shape, jnp.int32),
            pltpu.SMEM(src.shape, jnp.int32),
            pltpu.VMEM(src.shape, jnp.int32),
            pltpu.VMEM((members, taken, 8, 128), jnp.int32),
            pltpu.VMEM((blocks + 1, tile, width), BF16),
            pltpu.VMEM((blocks, tile, width), BF16),
            pltpu.VMEM((groups, each, tile, width), BF16),
            dma((15,)),
            dma((blocks,)),
            dma((members,)),
            dma((members,)),
            dma((members,)),
            dma((members,)),
            dma((members,)),
            dma((members,)),
            dma((groups,)),
            dma((groups,)),
        ],
        compiler_params=pltpu.CompilerParams(
            collective_id=0, has_side_effects=True, vmem_limit_bytes=16 << 20
        ),
    )(
        *hold(
            pltpu.HBM,
            features.reshape(blocks, tile, width),
            history.reshape(blocks, tile, width),
            tiles,
            cotangent,
            boundary_rows,
            picks,
            stale_rows,
            src,
        )
    )


def middle_kernel(
    code,
    quad,
    rest_code,
    rest_quad,
    marks,
    spots,
    tiles,
    srcs,
    cot,
    part,
    deg,
    w_self,
    w_neigh,
    out,
    back,
    dpre_out,
    halo_grad,
    weights,
    total,
    out_buf,
    grad,
    gt,
    inverse,
    sems,
):
    early, tile, width = part.shape
    blocks = deg.shape[0]
    per = spots.shape[0]
    base = code_base(tiles.shape[0])
    n_halo = halo_grad.shape[0]

    back[blocks] = jnp.zeros((width, tile), BF16)
    grad[blocks : blocks + n_halo] = jnp.zeros((n_halo, width, tile), F32)
    gt[...] = jnp.zeros_like(gt)
    inverse[...] = 1.0 / deg[...].astype(F32)

    def rest(step, acc):
        terms = []
        for u in range(STEP):
            lhs, rhs = [], []
            for i in range(QUAD):
                e, t = split(entry(rest_code, step, u * QUAD + i), base)
                lhs.append(tiles[t])
                rhs.append(srcs[e])
            terms.append(
                jnp.dot(
                    jnp.concatenate(lhs, axis=1),
                    jnp.concatenate(rhs, axis=0),
                    preferred_element_type=F32,
                )
            )
        for u in range(STEP):
            info = rest_quad[0, step * STEP + u]
            b = info // 2
            start = part[jnp.minimum(b, early - 1)]
            acc = terms[u] + jnp.where(info % 2 == 1, start, acc)
            total[b] = acc
        return acc

    lax.fori_loop(0, marks[3, 0], rest, jnp.zeros((tile, width), F32))

    def forward(b):
        lhs = jnp.concatenate([tiles[b * per + t] for t in range(per)], axis=1)
        rhs = jnp.concatenate([srcs[spots[t, b]] for t in range(per)], axis=0)
        total[b] = jnp.dot(lhs, rhs, preferred_element_type=F32)

    pl.loop(early, blocks, unroll=12)(forward)

    group = 16
    rows = group * tile
    w_cat = jnp.concatenate([w_self[...], w_neigh[...]], axis=0)

    def store(c):
        at = pl.ds(pl.multiple_of(c * rows, rows), rows)
        return pltpu.make_async_copy(out_buf.at[at], out.at[at], sems.at[c])

    def middle(c):
        at = pl.ds(pl.multiple_of(c * rows, rows), rows)
        agg = []
        for i in range(group):
            b = c * group + i
            d = jnp.broadcast_to(inverse[pl.ds(b, 1), :], (tile, tile)).T
            agg.append((total[b] * d).astype(BF16))
        own = srcs[pl.ds(c * group, group)].reshape(rows, width)
        fa = jnp.concatenate([own, jnp.concatenate(agg, axis=0)], axis=1)
        pre = jnp.dot(fa, w_cat, preferred_element_type=F32)
        scale = lax.rsqrt(jnp.mean(pre * pre, axis=-1, keepdims=True) + 1e-05)
        out_buf[at, :] = (pre * scale).astype(BF16)
        store(c).start()
        g = cot[at, :].astype(F32)
        m = jnp.mean(g * pre, axis=-1, keepdims=True)
        dpre = (scale * g - pre * (scale**3 * m)).astype(BF16)
        dpre_out[at, :] = dpre
        dpre_t = dpre.T
        gt[...] += jnp.dot(dpre_t, fa, preferred_element_type=F32)
        bt = jnp.dot(w_neigh[...], dpre_t, preferred_element_type=F32)
        for i in range(group):
            d = inverse[pl.ds(c * group + i, 1), :]
            back[c * group + i] = (bt[:, i * tile : (i + 1) * tile] * d).astype(BF16)

    pl.loop(0, blocks // group, unroll=2)(middle)

    weights[:width, :] = gt[:, :width].T.astype(weights.dtype)
    weights[width:, :] = gt[:, width:].T.astype(weights.dtype)

    def backward(step, acc):
        terms = quad_terms(step, code, back, tiles, base)
        for u in range(STEP):
            info = quad[0, step * STEP + u]
            acc = terms[u] + jnp.where(info % 2 == 1, 0.0, acc)
            grad[info // 2] = acc
        return acc

    lax.fori_loop(marks[1, 0], marks[2, 0], backward, jnp.zeros((width, tile), F32))
    for h in range(n_halo):
        halo_grad[h] = grad[blocks + h].T.astype(BF16)

    @pl.loop(0, blocks // group)
    def _(c):
        store(c).wait()


def quad_terms(step, code, back, tiles, base):
    terms = []
    for u in range(STEP):
        lhs, rhs = [], []
        for i in range(QUAD):
            b, t = split(entry(code, step, u * QUAD + i), base)
            lhs.append(back[b])
            rhs.append(tiles[t])
        terms.append(
            jnp.dot(
                jnp.concatenate(lhs, axis=1),
                jnp.concatenate(rhs, axis=0),
                preferred_element_type=F32,
            )
        )
    return terms


def middle(plans, tiles, srcs, cot, part, degree, w_self, w_neigh, n_halo, wire):
    tile, width = part.shape[1:]
    nodes = degree.shape[0]
    blocks = nodes // tile
    smem = pl.BlockSpec(memory_space=pltpu.SMEM)
    vmem = pl.BlockSpec(memory_space=pltpu.VMEM)
    return pl.pallas_call(
        middle_kernel,
        out_shape=(
            jax.ShapeDtypeStruct((nodes, width), BF16),
            vmem_out((blocks + 1, width, tile), BF16),
            vmem_out((nodes, width), BF16),
            vmem_out((n_halo, tile, width), BF16),
            vmem_out((2 * width, width), wire),
        ),
        in_specs=[smem] * 6 + [vmem] * 7,
        out_specs=[pl.BlockSpec(memory_space=pl.ANY)] + [vmem] * 4,
        scratch_shapes=[
            pltpu.VMEM((blocks + 1, tile, width), F32),
            pltpu.VMEM((nodes, width), BF16),
            pltpu.VMEM((blocks + n_halo + 1, width, tile), F32),
            pltpu.VMEM((width, 2 * width), F32),
            pltpu.VMEM((blocks, tile), F32),
            pltpu.SemaphoreType.DMA((blocks,)),
        ],
        compiler_params=pltpu.CompilerParams(vmem_limit_bytes=20 << 20),
    )(
        *hold(pltpu.SMEM, *plans),
        *hold(pltpu.VMEM, tiles, srcs, cot, part),
        degree.reshape(blocks, tile),
        w_self,
        w_neigh,
    )


def combine_kernel(
    groups,
    members,
    factor,
    code,
    quad,
    marks,
    tiles,
    back,
    dpre,
    halo_grad,
    weights,
    wanted,
    rows,
    w_self,
    grad_features,
    grad_self,
    grad_neigh,
    accs,
    returned,
    landed,
    partial,
    across,
    share,
    whole,
    h_send,
    h_recv,
    a_send,
    a_recv,
    b_send,
    b_recv,
    c_send,
    c_recv,
):
    me_g, me_m = lax.axis_index("group"), lax.axis_index("member")
    taken = wanted.shape[1]
    blocks, (width, tile) = back.shape[0] - 1, back.shape[1:]
    offered = rows.shape[1] // tile
    piece = landed.shape[1]
    base = code_base(tiles.shape[0])
    steps = (accs.shape[0] - 1) // STEP

    def backward(step, acc):
        terms = quad_terms(step, code, back, tiles, base)
        for u in range(STEP):
            q = step * STEP + u
            acc = terms[u] + jnp.where(quad[0, q] % 2 == 1, 0.0, acc)
            accs[q] = acc
        return acc

    entered = greet(groups, members)
    accs[accs.shape[0] - 1] = jnp.zeros((width, tile), F32)
    cuts = [steps * c // 10 for c in CUTS] + [steps]
    acc = lax.fori_loop(cuts[0], cuts[1], backward, jnp.zeros((width, tile), F32))
    entered()
    copies, first, second, third = [], [], [], []
    for o in range(1, members):
        peer = partner(me_m, o, members)
        at = pl.ds(pl.multiple_of(peer * piece, piece), piece)
        first.append(push(weights.at[at], landed.at[me_m], a_send, a_recv, o, (me_g, peer)))
    for o in range(1, members):
        peer = partner(me_m, o, members)
        copies.append(
            push(
                halo_grad.at[pl.ds(peer * taken, taken)],
                returned.at[me_m],
                h_send,
                h_recv,
                o,
                (me_g, peer),
            )
        )
    mine = pl.ds(pl.multiple_of(me_m * piece, piece), piece)
    landed[me_m] = weights[mine, :]
    returned[me_m] = halo_grad[pl.ds(me_m * taken, taken)]
    acc = lax.fori_loop(cuts[1], cuts[2], backward, acc)
    for copy in first:
        copy.wait_recv()
    total = landed[0].astype(F32)
    for p in range(1, members):
        total = total + landed[p].astype(F32)
    partial[...] = total.astype(partial.dtype)
    across[me_g] = total.astype(partial.dtype)
    for o in range(1, groups):
        to = lax.rem(me_g + o, groups)
        second.append(push(partial, across.at[me_g], b_send, b_recv, o, (to, me_m)))
    acc = lax.fori_loop(cuts[2], cuts[3], backward, acc)
    for copy in second:
        copy.wait_recv()
    total = across[0].astype(F32)
    for g in range(1, groups):
        total = total + across[g].astype(F32)
    share[...] = total.astype(share.dtype)
    whole[mine, :] = total.astype(share.dtype)
    for o in range(1, members):
        peer = partner(me_m, o, members)
        third.append(push(share, whole.at[mine], c_send, c_recv, o, (me_g, peer)))
    acc = lax.fori_loop(cuts[3], cuts[4], backward, acc)

    for copy in copies:
        copy.wait_recv()
    halves = []
    for j in range(offered):
        total = jnp.zeros((tile, width), F32)
        for p in range(members):
            for k in range(taken):
                w = jnp.broadcast_to(wanted[p, k][:1, :], (tile, width))
                total = total + jnp.where(w == j, returned[p, k].astype(F32), 0.0)
        high = total.astype(BF16)
        low = (total - high.astype(F32)).astype(BF16)
        halves.append(jnp.concatenate([high, low], axis=1))
    extra = jnp.concatenate(halves, axis=0)
    group = 4
    depth = group * tile

    def add(c):
        at = pl.ds(pl.multiple_of(c * depth, depth), depth)
        ids = lax.broadcasted_iota(jnp.int32, (depth, rows.shape[1]), 0) + c * depth
        hot = jnp.where(ids == rows[...], 1.0, 0.0).astype(BF16)
        more = jnp.dot(hot, extra, preferred_element_type=F32)
        own = lax.dot_general(
            dpre[at, :], w_self[...], (((1,), (1,)), ((), ())), preferred_element_type=F32
        )
        near = [accs[marks[0, c * group + i]].T for i in range(group)]
        own = own + jnp.concatenate(near, axis=0)
        grad_features[at, :] = (own + (more[:, :width] + more[:, width:])).astype(BF16)

    pl.loop(0, blocks // group)(add)
    for copy in third:
        copy.wait_recv()
    grad_self[...] = whole[:width, :].astype(F32) * factor
    grad_neigh[...] = whole[width:, :].astype(F32) * factor
    for copy in first + second + third + copies:
        copy.wait_send()


def combine(plans, tiles, back, dpre, halo_grad, weights, wanted, boundary_rows, w_self, sizes):
    groups, members = sizes
    nodes, width = dpre.shape
    tile = halo_grad.shape[1]
    blocks = nodes // tile
    taken = wanted.shape[1]
    piece = weights.shape[0] // members
    factor = 1.0 / math.sqrt(nodes * members * groups)
    smem = pl.BlockSpec(memory_space=pltpu.SMEM)
    vmem = pl.BlockSpec(memory_space=pltpu.VMEM)
    dma = pltpu.SemaphoreType.DMA
    return pl.pallas_call(
        functools.partial(combine_kernel, groups, members, factor),
        out_shape=(
            vmem_out((nodes, width), BF16),
            vmem_out((width, width), F32),
            vmem_out((width, width), F32),
        ),
        in_specs=[smem] * 3 + [vmem] * 8,
        out_specs=[vmem] * 3,
        scratch_shapes=[
            pltpu.VMEM((own_quads(tiles.shape[0], blocks) + 1, width, tile), F32),
            pltpu.VMEM((members, taken, tile, width), BF16),
            pltpu.VMEM((members, piece, width), weights.dtype),
            pltpu.VMEM((piece, width), weights.dtype),
            pltpu.VMEM((groups, piece, width), weights.dtype),
            pltpu.VMEM((piece, width), weights.dtype),
            pltpu.VMEM(weights.shape, weights.dtype),
            dma((members,)),
            dma((members,)),
            dma((members,)),
            dma((members,)),
            dma((groups,)),
            dma((groups,)),
            dma((members,)),
            dma((members,)),
        ],
        compiler_params=pltpu.CompilerParams(
            collective_id=1, has_side_effects=True, vmem_limit_bytes=24 << 20
        ),
    )(
        *hold(pltpu.SMEM, *plans),
        *hold(pltpu.VMEM, tiles, back, dpre, halo_grad, weights, wanted),
        boundary_rows,
        w_self,
    )


def write_kernel(a, b, c, out_a, out_b, out_c, sems):
    pairs = (a, out_a), (b, out_b), (c, out_c)
    copies = [pltpu.make_async_copy(x, y, sems.at[i]) for i, (x, y) in enumerate(pairs)]
    for copy in copies:
        copy.start()
    for copy in copies:
        copy.wait()


def write(*arrays):
    return pl.pallas_call(
        write_kernel,
        out_shape=[jax.ShapeDtypeStruct(a.shape, a.dtype) for a in arrays],
        in_specs=[pl.BlockSpec(memory_space=pltpu.VMEM)] * 3,
        out_specs=[pl.BlockSpec(memory_space=pltpu.HBM)] * 3,
        scratch_shapes=[pltpu.SemaphoreType.DMA((3,))],
        compiler_params=pltpu.CompilerParams(vmem_limit_bytes=4 << 20),
    )(*hold(pltpu.VMEM, *arrays))


def on_device(
    features,
    history,
    tiles,
    tile_src,
    degree,
    boundary_rows,
    picks,
    stale_rows,
    w_self,
    w_neigh,
    cotangent,
):
    sizes = lax.axis_size("group"), lax.axis_size("member")
    tiles, srcs, cot, part, wanted, code, quad, rest_code, rest_quad, marks, spots = gather(
        features,
        history,
        tiles,
        cotangent,
        boundary_rows,
        picks.T,
        stale_rows,
        tile_src.T,
        sizes,
    )
    n_halo = sizes[1] * picks.shape[1]
    wire = F32 if (2 * w_self.shape[0] // sizes[1]) % 16 else BF16
    layer_out, back, dpre, halo_grad, weights = middle(
        (code, quad, rest_code, rest_quad, marks, spots),
        tiles,
        srcs,
        cot,
        part,
        degree,
        w_self,
        w_neigh,
        n_halo,
        wire,
    )
    grad_features, grad_self, grad_neigh = combine(
        (code, quad, marks),
        tiles,
        back,
        dpre,
        halo_grad,
        weights,
        wanted,
        boundary_rows,
        w_self,
        sizes,
    )
    return layer_out, *write(grad_features, grad_self, grad_neigh)


def solution(mesh):
    nodes = P(("group", "member"), None)
    placed = (
        nodes,
        nodes,
        P(("group", "member"), None, None),
        nodes,
        P(("group", "member")),
        nodes,
        nodes,
        nodes,
        P(),
        P(),
        nodes,
    )
    return jax.shard_map(
        on_device,
        mesh=mesh,
        in_specs=placed,
        out_specs=(nodes, nodes, P(), P()),
        check_vma=False,
    )
```

```python
import functools
import math

import jax
import jax.numpy as jnp
from jax import lax
from jax.experimental import pallas as pl
from jax.experimental.pallas import tpu as pltpu
from jax.sharding import PartitionSpec as P

QUAD = 4
STEP = 8
EARLY = 8
CUTS = 0, 2, 6, 9
F32 = jnp.float32
BF16 = jnp.bfloat16
MESH = pl.DeviceIdType.MESH


def up(value, unit):
    return -(-value // unit) * unit


def iota(shape, axis):
    return lax.broadcasted_iota(jnp.int32, shape, axis).astype(F32)


def column(value):
    return jnp.broadcast_to(value, (8, value.shape[1])).T[:, :1]


def arrange(hit, values, keys, least, quads, pad, fence):
    wide, total = hit.shape
    low = hit.astype(BF16)
    earlier = jnp.where(iota((128, 128), 0) < iota((128, 128), 1), 1.0, 0.0).astype(BF16)
    count = jnp.zeros((wide, 1), F32)
    within = []
    for c in range(0, total, 128):
        part = low[:, c : c + 128]
        within.append(jnp.dot(part, earlier, preferred_element_type=F32) + count)
        count = count + jnp.sum(hit[:, c : c + 128], axis=1, keepdims=True)
    within = jnp.concatenate(within, axis=1)
    need = jnp.floor((count + (QUAD - 1)) / QUAD)
    need = jnp.where(iota((wide, 1), 0) < keys, jnp.maximum(need, least), 0.0)
    spread = jnp.broadcast_to(need, (wide, wide)).T
    before = iota((wide, wide), 1) < iota((wide, wide), 0)
    offset = jnp.sum(jnp.where(before, spread, 0.0), axis=1, keepdims=True)
    at_fence = iota((wide, 1), 0)
    first = jnp.sum(jnp.where(at_fence == fence, offset, 0.0), axis=0, keepdims=True)
    shift = STEP * jnp.floor((first + (STEP - 1)) / STEP) - first
    offset = offset + jnp.where(at_fence >= fence, shift, 0.0)
    end = jnp.sum(spread[:1, :], axis=1, keepdims=True) + shift
    pos = jnp.sum(hit * (QUAD * offset + within + 1.0), axis=0, keepdims=True) - 1.0
    high = jnp.floor(pos / 128.0)
    place = jnp.where(column(pos - 128.0 * high) == iota((total, 128), 1), 1.0, 0.0).astype(BF16)
    line = jnp.where(iota((8, total), 0) == high, 1.0, 0.0)
    terms = [line] + [line * row for row, _ in values]
    found = jnp.dot(
        jnp.concatenate(terms, axis=0).astype(BF16), place, preferred_element_type=F32
    )
    code = jnp.zeros((8, 128), F32)
    for i, (_, scale) in enumerate(values):
        code = code + scale * found[8 * (i + 1) : 8 * (i + 2), :]
    code = jnp.where(found[:8, :] > 0.0, code, pad)
    q = iota((wide, quads), 1)
    inside = (offset <= q) & (q < offset + need)
    info = 2.0 * iota((wide, quads), 0) + jnp.where(offset == q, 1.0, 0.0)
    quad = jnp.sum(jnp.where(inside, info + 1.0, 0.0), axis=0, keepdims=True)
    quad = jnp.where(quad > 0.0, quad - 1.0, 2.0 * keys + 1.0)
    return code.astype(jnp.int32), quad.astype(jnp.int32), offset, need, end


def back_quads(total, wanted):
    return up((total + wanted * (QUAD - 1)) // QUAD, 128)


def rest_quads_of(blocks, per):
    return up(blocks * (-(-per // QUAD)), 128)


def early_blocks(blocks):
    return blocks * EARLY // 32


def own_quads(total, blocks):
    return up((total + blocks * (QUAD - 1)) // QUAD, STEP)


def code_base(total):
    return 1 << (total - 1).bit_length()


def split(value, base):
    return lax.shift_right_logical(value, base.bit_length() - 1), value & (base - 1)


def entry(code, step, i):
    line = 128 // (STEP * QUAD)
    first = lax.shift_right_logical(step, line.bit_length() - 1)
    return code[first, (step & (line - 1)) * (STEP * QUAD) + i]


def greet(groups, members):
    me_g, me_m = lax.axis_index("group"), lax.axis_index("member")
    barrier = pltpu.get_barrier_semaphore()
    peers = [(me_g, partner(me_m, o, members)) for o in range(1, members)]
    peers += [(lax.rem(me_g + o, groups), me_m) for o in range(1, groups)]
    for peer in peers:
        pl.semaphore_signal(barrier, inc=1, device_id=peer, device_id_type=MESH)
    return lambda: pl.semaphore_wait(barrier, len(peers))


def partner(me, o, members):
    if members & (members - 1):
        return lax.rem(me + o, members)
    bit = 1
    while bit <= o:
        if o & bit:
            me = me + bit - 2 * bit * lax.rem(lax.div(me, bit), 2)
        bit *= 2
    return me


def sender(me, o, members):
    if members & (members - 1):
        return lax.rem(me + members - o, members)
    return partner(me, o, members)


def push(src, dst, send, recv, o, device):
    copy = pltpu.make_async_remote_copy(
        src_ref=src,
        dst_ref=dst,
        send_sem=send.at[o],
        recv_sem=recv.at[o],
        device_id=device,
        device_id_type=MESH,
    )
    copy.start()
    return copy


def pick_rows(row, table, chunk):
    count = row.shape[1]
    blocks, tile, width = table.shape
    half = blocks // 2
    ids_column = jnp.broadcast_to(row, (8, count)).T[:, :1]
    second = ids_column >= half * tile
    ids_column = jnp.where(second, ids_column - half * tile, ids_column)
    total = jnp.zeros((count, 2 * width), F32)
    depth = chunk * tile
    for c in range(0, half, chunk):
        ids = lax.broadcasted_iota(jnp.int32, (count, depth), 1) + c * tile
        hot = jnp.where(ids == ids_column, 1.0, 0.0).astype(BF16)
        both = [table[a : a + chunk].reshape(depth, width) for a in (c, half + c)]
        total = total + jnp.dot(
            hot, jnp.concatenate(both, axis=1), preferred_element_type=F32
        )
    return jnp.where(second, total[:, width:], total[:, :width])


def gather_kernel(
    groups,
    members,
    blocks,
    feats_in,
    hist_in,
    tiles_in,
    cot_in,
    rows_in,
    picks_in,
    stale_rows_in,
    src_in,
    tiles,
    srcs,
    cot,
    part,
    wanted,
    code_out,
    quad_out,
    rest_code_out,
    rest_quad_out,
    marks_out,
    spots_out,
    code,
    quad,
    rest_code,
    rest_quad,
    marks,
    spots_vec,
    rows,
    picks,
    stale_rows,
    src,
    src_vec,
    asked,
    own,
    hist,
    leaving,
    l_sems,
    t_sems,
    p_send,
    p_recv,
    d_send,
    d_recv,
    r_send,
    r_recv,
    s_send,
    s_recv,
):
    me_g, me_m = lax.axis_index("group"), lax.axis_index("member")
    taken = picks.shape[0]
    tile, width = srcs.shape[1], srcs.shape[2]
    offered = rows.shape[1] // tile
    each = stale_rows.shape[1] // tile
    per = src.shape[0]
    total = blocks * per
    pair = 1 if members & (members - 1) else 2

    load_feats = pltpu.make_async_copy(feats_in, own.at[pl.ds(0, blocks)], l_sems.at[0])
    keep_feats = pltpu.make_async_copy(feats_in, srcs.at[pl.ds(0, blocks)], l_sems.at[8])
    load_hist = pltpu.make_async_copy(hist_in, hist, l_sems.at[1])
    load_cot = pltpu.make_async_copy(cot_in, cot, l_sems.at[2])

    def chunk(b):
        at = pl.ds(b * per, per)
        return pltpu.make_async_copy(tiles_in.at[at], tiles.at[at], t_sems.at[b])

    small = [
        pltpu.make_async_copy(a, b, l_sems.at[3 + i])
        for i, (a, b) in enumerate(
            (
                (rows_in, rows),
                (picks_in, picks),
                (stale_rows_in, stale_rows),
                (src_in, src),
                (src_in, src_vec),
            )
        )
    ]
    load_feats.start()
    for copy in small:
        copy.start()
    load_hist.start()
    entered = greet(groups, members)
    for copy in small:
        copy.wait()
    for p in range(members):
        for k in range(taken):
            asked[p, k] = jnp.broadcast_to(picks[k : k + 1, p : p + 1], asked.shape[2:])
    wanted[me_m] = asked[me_m]
    own[blocks] = jnp.zeros((tile, width), BF16)
    srcs[blocks] = jnp.zeros((tile, width), BF16)
    load_feats.wait()

    @pl.loop(0, blocks)
    def _(b):
        chunk(b).start()

    load_cot.start()
    keep_feats.start()
    bounds = blocks + 1
    stales = bounds + members * offered
    mine = pl.ds(bounds + me_m * offered, offered)
    srcs[mine] = pick_rows(rows[...], own.at[pl.ds(0, blocks)], 4).astype(BF16).reshape(
        offered, tile, width
    )
    entered()
    direct, copies = [], []
    for o in range(1, members):
        if o % pair == 0:
            peer = partner(me_m, o, members)
            direct.append((o, push(srcs.at[mine], srcs.at[mine], d_send, d_recv, o, (me_g, peer))))
    if pair == 2:
        mate = partner(me_m, 1, members)
        copies.append(push(srcs.at[mine], srcs.at[mine], d_send, d_recv, 1, (me_g, mate)))
    load_hist.wait()
    for o in range(groups - 1, -1, -1):
        to = lax.rem(me_g + o, groups)
        found = pick_rows(stale_rows[pl.ds(to, 1), :], hist, 4)
        found = found.astype(BF16).reshape(each, tile, width)
        at = pl.ds(stales + me_g * each, each)
        if o == 0:
            srcs[at] = found
        else:
            leaving[o] = found
            copies.append(push(leaving.at[o], srcs.at[at], s_send, s_recv, o, (to, me_m)))
    for o in range(1, members):
        peer = partner(me_m, o, members)
        copies.append(push(asked.at[peer], wanted.at[me_m], p_send, p_recv, o, (me_g, peer)))

    def forward(b):
        chunk(b).wait()
        lhs = jnp.concatenate([tiles[b * per + t] for t in range(per)], axis=1)
        rhs = jnp.concatenate([own[jnp.minimum(src[t, b], blocks)] for t in range(per)], axis=0)
        part[b] = jnp.dot(lhs, rhs, preferred_element_type=F32)

    early = early_blocks(blocks)
    pl.loop(0, early, unroll=4)(forward)
    one = (per, total)
    owner = jnp.floor((iota(one, 1) + 0.5) / per)
    rank = iota(one, 1) - per * owner
    place = jnp.where(iota((blocks, total), 0) == owner[:1, :], 1.0, 0.0).astype(BF16)
    spread = jnp.dot(src_vec[...].astype(F32).astype(BF16), place, preferred_element_type=F32)
    row = jnp.sum(jnp.where(iota(one, 0) == rank, spread, 0.0), axis=0, keepdims=True)
    owner = owner[:1, :]
    base = code_base(total)
    inner = blocks + members * taken
    wide = up(inner + 1, 128)
    hit = jnp.where((iota((wide, total), 0) == row) & (row < inner), 1.0, 0.0)
    rank = rank[:1, :]
    numbers = [(owner, float(per)), (rank, 1.0)]
    code[...], quad[...], offset, need, end = arrange(
        hit,
        [(owner, float(base))] + numbers,
        inner,
        0.0,
        quad.shape[1],
        float(base * blocks),
        blocks,
    )

    def place_of(s):
        halo = s - blocks
        spot = jnp.where(halo < 0.0, s, s - inner + stales)
        for p in range(members):
            for k in range(taken):
                pick = picks[k : k + 1, p : p + 1].astype(F32)
                spot = jnp.where(halo == p * taken + k, bounds + p * offered + pick, spot)
        return spot

    spots_vec[...] = place_of(src_vec[...].astype(F32)).astype(jnp.int32)
    spot = place_of(row)
    remains = (row >= blocks) & (owner < early)
    hit = jnp.where((iota((128, total), 0) == owner) & remains, 1.0, 0.0)
    rest_code[...], rest_quad[...], _, _, rest_end = arrange(
        hit,
        [(spot, float(base))] + numbers,
        early,
        1.0,
        rest_quad.shape[1],
        float(base * blocks),
        blocks,
    )
    last = jnp.where(need > 0.0, offset + need - 1.0, float(own_quads(total, blocks)))
    last = jnp.broadcast_to(last, (wide, wide)).T[:8, :]
    first = jnp.sum(jnp.where(iota((wide, 1), 0) == blocks, offset, 0.0), axis=0, keepdims=True)
    which = iota((8, wide), 0)
    found = jnp.where(which == 1, jnp.floor(first / STEP), last)
    found = jnp.where(which == 2, jnp.floor((end + (STEP - 1)) / STEP), found)
    found = jnp.where(which == 3, jnp.floor((rest_end + (STEP - 1)) / STEP), found)
    marks[...] = found.astype(jnp.int32)

    outs = [
        pltpu.make_async_copy(a, b, l_sems.at[9 + i])
        for i, (a, b) in enumerate(
            (
                (code, code_out),
                (quad, quad_out),
                (rest_code, rest_code_out),
                (rest_quad, rest_quad_out),
                (marks, marks_out),
                (spots_vec, spots_out),
            )
        )
    ]
    for copy in outs:
        copy.start()

    for o, copy in direct:
        copy.wait_recv()
        if pair == 2:
            at = pl.ds(bounds + sender(me_m, o, members) * offered, offered)
            copies.append(push(srcs.at[at], srcs.at[at], r_send, r_recv, o, (me_g, mate)))

    @pl.loop(early, blocks)
    def _(b):
        chunk(b).wait()

    for copy in outs:
        copy.wait()
    load_cot.wait()
    keep_feats.wait()
    for _, copy in direct:
        copy.wait_send()
    for copy in copies:
        copy.wait()


def vmem_out(shape, dtype):
    return pltpu.VMEM(shape, dtype)


def hold(space, *arrays):
    return [pltpu.with_memory_space_constraint(a, space) for a in arrays]


def gather(features, history, tiles, cotangent, boundary_rows, picks, stale_rows, src, sizes):
    groups, members = sizes
    per, blocks = src.shape
    taken = picks.shape[0]
    tile, width = tiles.shape[1], features.shape[1]
    offered = boundary_rows.shape[1] // tile
    each = stale_rows.shape[1] // tile
    total = blocks * per
    inner = blocks + members * taken
    lists = (
        (8, 128),
        (1, back_quads(total, inner)),
        (8, 128),
        (1, rest_quads_of(blocks, per)),
        (8, up(inner + 1, 128)),
        src.shape,
    )
    held = blocks + 1 + members * offered + groups * each
    vmem = pl.BlockSpec(memory_space=pltpu.VMEM)
    dma = pltpu.SemaphoreType.DMA
    return pl.pallas_call(
        functools.partial(gather_kernel, groups, members, blocks),
        out_shape=(
            vmem_out(tiles.shape, BF16),
            vmem_out((held, tile, width), BF16),
            vmem_out((blocks * tile, width), BF16),
            vmem_out((early_blocks(blocks), tile, width), F32),
            vmem_out((members, taken, 8, 128), jnp.int32),
            *[pltpu.SMEM(shape, jnp.int32) for shape in lists],
        ),
        in_specs=[pl.BlockSpec(memory_space=pltpu.HBM)] * 8,
        out_specs=[vmem] * 5 + [pl.BlockSpec(memory_space=pltpu.SMEM)] * 6,
        scratch_shapes=[
            *[pltpu.VMEM(shape, jnp.int32) for shape in lists],
            pltpu.VMEM(boundary_rows.shape, jnp.int32),
            pltpu.VMEM(picks.shape, jnp.int32),
            pltpu.VMEM(stale_rows.shape, jnp.int32),
            pltpu.SMEM(src.shape, jnp.int32),
            pltpu.VMEM(src.shape, jnp.int32),
            pltpu.VMEM((members, taken, 8, 128), jnp.int32),
            pltpu.VMEM((blocks + 1, tile, width), BF16),
            pltpu.VMEM((blocks, tile, width), BF16),
            pltpu.VMEM((groups, each, tile, width), BF16),
            dma((15,)),
            dma((blocks,)),
            dma((members,)),
            dma((members,)),
            dma((members,)),
            dma((members,)),
            dma((members,)),
            dma((members,)),
            dma((groups,)),
            dma((groups,)),
        ],
        compiler_params=pltpu.CompilerParams(
            collective_id=0, has_side_effects=True, vmem_limit_bytes=16 << 20
        ),
    )(
        *hold(
            pltpu.HBM,
            features.reshape(blocks, tile, width),
            history.reshape(blocks, tile, width),
            tiles,
            cotangent,
            boundary_rows,
            picks,
            stale_rows,
            src,
        )
    )


def middle_kernel(
    code,
    quad,
    rest_code,
    rest_quad,
    marks,
    spots,
    tiles,
    srcs,
    cot,
    part,
    deg,
    w_self,
    w_neigh,
    out,
    back,
    dpre_out,
    halo_grad,
    weights,
    total,
    out_buf,
    grad,
    gt,
    inverse,
    sems,
):
    early, tile, width = part.shape
    blocks = deg.shape[0]
    per = spots.shape[0]
    base = code_base(tiles.shape[0])
    n_halo = halo_grad.shape[0]

    back[blocks] = jnp.zeros((width, tile), BF16)
    grad[blocks : blocks + n_halo] = jnp.zeros((n_halo, width, tile), F32)
    gt[...] = jnp.zeros_like(gt)
    inverse[...] = 1.0 / deg[...].astype(F32)

    def rest(step, acc):
        terms = []
        for u in range(STEP):
            lhs, rhs = [], []
            for i in range(QUAD):
                e, t = split(entry(rest_code, step, u * QUAD + i), base)
                lhs.append(tiles[t])
                rhs.append(srcs[e])
            terms.append(
                jnp.dot(
                    jnp.concatenate(lhs, axis=1),
                    jnp.concatenate(rhs, axis=0),
                    preferred_element_type=F32,
                )
            )
        for u in range(STEP):
            info = rest_quad[0, step * STEP + u]
            b = info // 2
            start = part[jnp.minimum(b, early - 1)]
            acc = terms[u] + jnp.where(info % 2 == 1, start, acc)
            total[b] = acc
        return acc

    lax.fori_loop(0, marks[3, 0], rest, jnp.zeros((tile, width), F32))

    def forward(b):
        lhs = jnp.concatenate([tiles[b * per + t] for t in range(per)], axis=1)
        rhs = jnp.concatenate([srcs[spots[t, b]] for t in range(per)], axis=0)
        total[b] = jnp.dot(lhs, rhs, preferred_element_type=F32)

    pl.loop(early, blocks, unroll=12)(forward)

    group = 16
    rows = group * tile
    w_cat = jnp.concatenate([w_self[...], w_neigh[...]], axis=0)

    def store(c):
        at = pl.ds(pl.multiple_of(c * rows, rows), rows)
        return pltpu.make_async_copy(out_buf.at[at], out.at[at], sems.at[c])

    def middle(c):
        at = pl.ds(pl.multiple_of(c * rows, rows), rows)
        agg = []
        for i in range(group):
            b = c * group + i
            d = jnp.broadcast_to(inverse[pl.ds(b, 1), :], (tile, tile)).T
            agg.append((total[b] * d).astype(BF16))
        own = srcs[pl.ds(c * group, group)].reshape(rows, width)
        fa = jnp.concatenate([own, jnp.concatenate(agg, axis=0)], axis=1)
        pre = jnp.dot(fa, w_cat, preferred_element_type=F32)
        scale = lax.rsqrt(jnp.mean(pre * pre, axis=-1, keepdims=True) + 1e-05)
        out_buf[at, :] = (pre * scale).astype(BF16)
        store(c).start()
        g = cot[at, :].astype(F32)
        m = jnp.mean(g * pre, axis=-1, keepdims=True)
        dpre = (scale * g - pre * (scale**3 * m)).astype(BF16)
        dpre_out[at, :] = dpre
        dpre_t = dpre.T
        gt[...] += jnp.dot(dpre_t, fa, preferred_element_type=F32)
        bt = jnp.dot(w_neigh[...], dpre_t, preferred_element_type=F32)
        for i in range(group):
            d = inverse[pl.ds(c * group + i, 1), :]
            back[c * group + i] = (bt[:, i * tile : (i + 1) * tile] * d).astype(BF16)

    pl.loop(0, blocks // group, unroll=2)(middle)

    weights[:width, :] = gt[:, :width].T.astype(weights.dtype)
    weights[width:, :] = gt[:, width:].T.astype(weights.dtype)

    def backward(step, acc):
        terms = quad_terms(step, code, back, tiles, base)
        for u in range(STEP):
            info = quad[0, step * STEP + u]
            acc = terms[u] + jnp.where(info % 2 == 1, 0.0, acc)
            grad[info // 2] = acc
        return acc

    lax.fori_loop(marks[1, 0], marks[2, 0], backward, jnp.zeros((width, tile), F32))
    for h in range(n_halo):
        halo_grad[h] = grad[blocks + h].T.astype(BF16)

    @pl.loop(0, blocks // group)
    def _(c):
        store(c).wait()


def quad_terms(step, code, back, tiles, base):
    terms = []
    for u in range(STEP):
        lhs, rhs = [], []
        for i in range(QUAD):
            b, t = split(entry(code, step, u * QUAD + i), base)
            lhs.append(back[b])
            rhs.append(tiles[t])
        terms.append(
            jnp.dot(
                jnp.concatenate(lhs, axis=1),
                jnp.concatenate(rhs, axis=0),
                preferred_element_type=F32,
            )
        )
    return terms


def middle(plans, tiles, srcs, cot, part, degree, w_self, w_neigh, n_halo, wire):
    tile, width = part.shape[1:]
    nodes = degree.shape[0]
    blocks = nodes // tile
    smem = pl.BlockSpec(memory_space=pltpu.SMEM)
    vmem = pl.BlockSpec(memory_space=pltpu.VMEM)
    return pl.pallas_call(
        middle_kernel,
        out_shape=(
            jax.ShapeDtypeStruct((nodes, width), BF16),
            vmem_out((blocks + 1, width, tile), BF16),
            vmem_out((nodes, width), BF16),
            vmem_out((n_halo, tile, width), BF16),
            vmem_out((2 * width, width), wire),
        ),
        in_specs=[smem] * 6 + [vmem] * 7,
        out_specs=[pl.BlockSpec(memory_space=pl.ANY)] + [vmem] * 4,
        scratch_shapes=[
            pltpu.VMEM((blocks + 1, tile, width), F32),
            pltpu.VMEM((nodes, width), BF16),
            pltpu.VMEM((blocks + n_halo + 1, width, tile), F32),
            pltpu.VMEM((width, 2 * width), F32),
            pltpu.VMEM((blocks, tile), F32),
            pltpu.SemaphoreType.DMA((blocks,)),
        ],
        compiler_params=pltpu.CompilerParams(vmem_limit_bytes=20 << 20),
    )(
        *hold(pltpu.SMEM, *plans),
        *hold(pltpu.VMEM, tiles, srcs, cot, part),
        degree.reshape(blocks, tile),
        w_self,
        w_neigh,
    )


def combine_kernel(
    groups,
    members,
    factor,
    code,
    quad,
    marks,
    tiles,
    back,
    dpre,
    halo_grad,
    weights,
    wanted,
    rows,
    w_self,
    grad_features,
    grad_self,
    grad_neigh,
    accs,
    returned,
    landed,
    partial,
    across,
    share,
    whole,
    h_send,
    h_recv,
    a_send,
    a_recv,
    b_send,
    b_recv,
    c_send,
    c_recv,
):
    me_g, me_m = lax.axis_index("group"), lax.axis_index("member")
    taken = wanted.shape[1]
    blocks, (width, tile) = back.shape[0] - 1, back.shape[1:]
    offered = rows.shape[1] // tile
    piece = landed.shape[1]
    base = code_base(tiles.shape[0])
    steps = (accs.shape[0] - 1) // STEP

    def backward(step, acc):
        terms = quad_terms(step, code, back, tiles, base)
        for u in range(STEP):
            q = step * STEP + u
            acc = terms[u] + jnp.where(quad[0, q] % 2 == 1, 0.0, acc)
            accs[q] = acc
        return acc

    entered = greet(groups, members)
    accs[accs.shape[0] - 1] = jnp.zeros((width, tile), F32)
    cuts = [steps * c // 10 for c in CUTS] + [steps]
    acc = lax.fori_loop(cuts[0], cuts[1], backward, jnp.zeros((width, tile), F32))
    entered()
    copies, first, second, third = [], [], [], []
    for o in range(1, members):
        peer = partner(me_m, o, members)
        at = pl.ds(pl.multiple_of(peer * piece, piece), piece)
        first.append(push(weights.at[at], landed.at[me_m], a_send, a_recv, o, (me_g, peer)))
    mine = pl.ds(pl.multiple_of(me_m * piece, piece), piece)
    landed[me_m] = weights[mine, :]
    returned[me_m] = halo_grad[pl.ds(me_m * taken, taken)]
    acc = lax.fori_loop(cuts[1], cuts[1] + 2, backward, acc)
    for o in range(1, members):
        peer = partner(me_m, o, members)
        copies.append(
            push(
                halo_grad.at[pl.ds(peer * taken, taken)],
                returned.at[me_m],
                h_send,
                h_recv,
                o,
                (me_g, peer),
            )
        )
    acc = lax.fori_loop(cuts[1] + 2, cuts[2], backward, acc)
    for copy in first:
        copy.wait_recv()
    total = landed[0].astype(F32)
    for p in range(1, members):
        total = total + landed[p].astype(F32)
    partial[...] = total.astype(partial.dtype)
    across[me_g] = total.astype(partial.dtype)
    for o in range(1, groups):
        to = lax.rem(me_g + o, groups)
        second.append(push(partial, across.at[me_g], b_send, b_recv, o, (to, me_m)))
    acc = lax.fori_loop(cuts[2], cuts[3], backward, acc)
    for copy in second:
        copy.wait_recv()
    total = across[0].astype(F32)
    for g in range(1, groups):
        total = total + across[g].astype(F32)
    share[...] = total.astype(share.dtype)
    whole[mine, :] = total.astype(share.dtype)
    for o in range(1, members):
        peer = partner(me_m, o, members)
        third.append(push(share, whole.at[mine], c_send, c_recv, o, (me_g, peer)))
    acc = lax.fori_loop(cuts[3], cuts[4], backward, acc)

    for copy in copies:
        copy.wait_recv()
    halves = []
    for j in range(offered):
        total = jnp.zeros((tile, width), F32)
        for p in range(members):
            for k in range(taken):
                w = jnp.broadcast_to(wanted[p, k][:1, :], (tile, width))
                total = total + jnp.where(w == j, returned[p, k].astype(F32), 0.0)
        high = total.astype(BF16)
        low = (total - high.astype(F32)).astype(BF16)
        halves.append(jnp.concatenate([high, low], axis=1))
    extra = jnp.concatenate(halves, axis=0)
    group = 4
    depth = group * tile

    def add(c):
        at = pl.ds(pl.multiple_of(c * depth, depth), depth)
        ids = lax.broadcasted_iota(jnp.int32, (depth, rows.shape[1]), 0) + c * depth
        hot = jnp.where(ids == rows[...], 1.0, 0.0).astype(BF16)
        more = jnp.dot(hot, extra, preferred_element_type=F32)
        own = lax.dot_general(
            dpre[at, :], w_self[...], (((1,), (1,)), ((), ())), preferred_element_type=F32
        )
        near = [accs[marks[0, c * group + i]].T for i in range(group)]
        own = own + jnp.concatenate(near, axis=0)
        grad_features[at, :] = (own + (more[:, :width] + more[:, width:])).astype(BF16)

    pl.loop(0, blocks // group)(add)
    for copy in third:
        copy.wait_recv()
    grad_self[...] = whole[:width, :].astype(F32) * factor
    grad_neigh[...] = whole[width:, :].astype(F32) * factor
    for copy in first + second + third + copies:
        copy.wait_send()


def combine(plans, tiles, back, dpre, halo_grad, weights, wanted, boundary_rows, w_self, sizes):
    groups, members = sizes
    nodes, width = dpre.shape
    tile = halo_grad.shape[1]
    blocks = nodes // tile
    taken = wanted.shape[1]
    piece = weights.shape[0] // members
    factor = 1.0 / math.sqrt(nodes * members * groups)
    smem = pl.BlockSpec(memory_space=pltpu.SMEM)
    vmem = pl.BlockSpec(memory_space=pltpu.VMEM)
    dma = pltpu.SemaphoreType.DMA
    return pl.pallas_call(
        functools.partial(combine_kernel, groups, members, factor),
        out_shape=(
            vmem_out((nodes, width), BF16),
            vmem_out((width, width), F32),
            vmem_out((width, width), F32),
        ),
        in_specs=[smem] * 3 + [vmem] * 8,
        out_specs=[vmem] * 3,
        scratch_shapes=[
            pltpu.VMEM((own_quads(tiles.shape[0], blocks) + 1, width, tile), F32),
            pltpu.VMEM((members, taken, tile, width), BF16),
            pltpu.VMEM((members, piece, width), weights.dtype),
            pltpu.VMEM((piece, width), weights.dtype),
            pltpu.VMEM((groups, piece, width), weights.dtype),
            pltpu.VMEM((piece, width), weights.dtype),
            pltpu.VMEM(weights.shape, weights.dtype),
            dma((members,)),
            dma((members,)),
            dma((members,)),
            dma((members,)),
            dma((groups,)),
            dma((groups,)),
            dma((members,)),
            dma((members,)),
        ],
        compiler_params=pltpu.CompilerParams(
            collective_id=1, has_side_effects=True, vmem_limit_bytes=24 << 20
        ),
    )(
        *hold(pltpu.SMEM, *plans),
        *hold(pltpu.VMEM, tiles, back, dpre, halo_grad, weights, wanted),
        boundary_rows,
        w_self,
    )


def write_kernel(a, b, c, out_a, out_b, out_c, sems):
    pairs = (a, out_a), (b, out_b), (c, out_c)
    copies = [pltpu.make_async_copy(x, y, sems.at[i]) for i, (x, y) in enumerate(pairs)]
    for copy in copies:
        copy.start()
    for copy in copies:
        copy.wait()


def write(*arrays):
    return pl.pallas_call(
        write_kernel,
        out_shape=[jax.ShapeDtypeStruct(a.shape, a.dtype) for a in arrays],
        in_specs=[pl.BlockSpec(memory_space=pltpu.VMEM)] * 3,
        out_specs=[pl.BlockSpec(memory_space=pltpu.HBM)] * 3,
        scratch_shapes=[pltpu.SemaphoreType.DMA((3,))],
        compiler_params=pltpu.CompilerParams(vmem_limit_bytes=4 << 20),
    )(*hold(pltpu.VMEM, *arrays))


def on_device(
    features,
    history,
    tiles,
    tile_src,
    degree,
    boundary_rows,
    picks,
    stale_rows,
    w_self,
    w_neigh,
    cotangent,
):
    sizes = lax.axis_size("group"), lax.axis_size("member")
    tiles, srcs, cot, part, wanted, code, quad, rest_code, rest_quad, marks, spots = gather(
        features,
        history,
        tiles,
        cotangent,
        boundary_rows,
        picks.T,
        stale_rows,
        tile_src.T,
        sizes,
    )
    n_halo = sizes[1] * picks.shape[1]
    wire = F32 if (2 * w_self.shape[0] // sizes[1]) % 16 else BF16
    layer_out, back, dpre, halo_grad, weights = middle(
        (code, quad, rest_code, rest_quad, marks, spots),
        tiles,
        srcs,
        cot,
        part,
        degree,
        w_self,
        w_neigh,
        n_halo,
        wire,
    )
    grad_features, grad_self, grad_neigh = combine(
        (code, quad, marks),
        tiles,
        back,
        dpre,
        halo_grad,
        weights,
        wanted,
        boundary_rows,
        w_self,
        sizes,
    )
    return layer_out, *write(grad_features, grad_self, grad_neigh)


def solution(mesh):
    nodes = P(("group", "member"), None)
    placed = (
        nodes,
        nodes,
        P(("group", "member"), None, None),
        nodes,
        P(("group", "member")),
        nodes,
        nodes,
        nodes,
        P(),
        P(),
        nodes,
    )
    return jax.shard_map(
        on_device,
        mesh=mesh,
        in_specs=placed,
        out_specs=(nodes, nodes, P(), P()),
        check_vma=False,
    )
```
